128 devices in a mesh: tok: 8 (over y, x_lo), tp: 16 (over z, x_hi, core).
Axes of the slice: x: 4 (x_hi: 2, x_lo: 2; x = x_hi * 2 + x_lo), y: 4, z: 4, core: 2. Of those that a mesh axis runs over, the one named last changes fastest.
Arguments:
- source: bfloat16 [2048, 8192], P('tp', 'tok'), may hold values from -6 to 6
- row_token: int32 [2048], replicated, may hold values from 0 to 2047, each once
- seg_ids: int32 [8, 256], P('tok'), may hold values from 0 to 3, never falling along the last dimension, each value on 1 to 128 neighbouring positions
- stitch_weight: bfloat16 [8192, 8192], P('tok', 'tp'), may hold values from -0.0625 to 0.0625
- norm_gain: float32 [8192], replicated, may hold values from 0.5 to 1.5
- q_weight: bfloat16 [8192, 8192], P(None, 'tp'), may hold values from -2 to 2
- kv_weight: bfloat16 [8192, 2048], P(None, 'tp'), may hold values from -2 to 2
- o_weight: bfloat16 [8192, 8192], P('tp'), may hold values from -0.0625 to 0.0625
- out_grad: bfloat16 [2048, 8192], P('tok', 'tp'), may hold values from -6 to 6
Outputs:
- layer_out: bfloat16 [2048, 8192], P('tok', 'tp')
- stitch_grad: float32 [8192, 8192], P('tok', 'tp')
The draws below stay inside these ranges and needn't reach their ends.
Inputs may be any that keep to these rules, and one draw needn't show every extreme that they name: `row_token`: each token index appears exactly once. `seg_ids`: within a pack the ids never fall; a document holds 1 to 128 tokens.
All inputs are finite; a program needn't handle non-finite values.
Results may differ from the reference program's by a relative error of at most 0.024.
Values may be sent and summed in bfloat16 or wider, within the bound.
A program may use at most 128 MiB of HBM per device.

```python
import math
import jax
import jax.numpy as jnp
import numpy as np
from jax import lax

DS = 8192
D = 8192
HEADS = 64
KV = 8
HD = 128
TOK_DEV = 256
DOCS = 4
PACKS = 8
TOKENS = 2048


def draw_q_weight(key, part):
    result = jax.random.normal(jax.random.fold_in(key, 1), (D, HEADS * HD), jnp.float32) * D ** (-0.5)
    return jnp.clip(result, -2.0, 2.0).astype(jnp.bfloat16)


def draw_kv_weight(key, part):
    key_cols = jax.random.normal(jax.random.fold_in(key, 2), (D, KV, HD), jnp.float32) * D ** (-0.5)
    value_cols = jax.random.normal(jax.random.fold_in(key, 4), (D, KV, HD), jnp.float32) * D ** (-0.5)
    result = jnp.stack([key_cols, value_cols], axis=2).reshape(D, 2 * KV * HD)
    return jnp.clip(result, -2.0, 2.0).astype(jnp.bfloat16)


def steps_of(stream_key, dims, split, low, high):
    loudness, own = 1.0, jax.random.fold_in(stream_key, 6)
    for position, shards_of in split:
        heights = jnp.exp(jax.random.uniform(jax.random.fold_in(own, position), (shards_of,), jnp.float32, low / len(split), high / len(split)))
        loudness = loudness * jnp.repeat(heights, dims[position] // shards_of).reshape([-1 if axis == position else 1 for axis in range(len(dims))])
    return loudness


def length_profile(amount, total, limit, slope):
    loads = [(1 << 20) // math.isqrt(grade ** slope) + 1 for grade in range(2, amount + 1)]
    spare, counts = total - limit - (amount - 1), [1] * (amount - 1)
    while spare > 0:
        candidates = [i for i in range(amount - 1) if counts[i] < limit]
        pool, budget = sum([loads[i] for i in candidates]), spare
        for i in candidates:
            addition = min(limit - counts[i], max(1, budget * loads[i] // pool), spare)
            counts[i] = counts[i] + addition
            spare = spare - addition
    return np.array([limit] + counts)


def ragged(stream_key, amount, total, reach, lean):
    if amount == 2:
        one = jax.random.randint(stream_key, (), max(1, total - reach), min(reach, total - 1) + 1)
        return jnp.stack([one, total - one])
    sizes = jnp.asarray(length_profile(amount, total, reach, lean), jnp.int32)
    twos = (amount - 1) // 2
    source_of, taker = sizes[1:1 + 2 * twos:2], sizes[2:2 + 2 * twos:2]
    room = jnp.minimum(source_of - 1, reach - taker)
    passed = jax.random.randint(jax.random.fold_in(stream_key, 1), (twos,), 0, 1 << 20) % (room + 1)
    sizes = sizes.at[1:1 + 2 * twos:2].set(source_of - passed).at[2:2 + 2 * twos:2].set(taker + passed)
    return sizes[jax.random.permutation(jax.random.fold_in(stream_key, 2), amount)]


def bell_draw(own_key, shape, spread, most, shards=(), kind=jnp.bfloat16):
    values = jax.random.normal(own_key, shape, jnp.float32) * spread
    if len(shards) > 0:
        values = steps_of(own_key, shape, shards, -0.22, 0.18) * values
    return jnp.clip(values, min=-most, max=most).astype(kind)


def setup_inputs(seed: int = 0) -> dict:
    key_of = jax.random.split(jax.random.key(seed), 10)
    return {
        "source": bell_draw(key_of[0], (TOKENS, DS), 1.0, 6.0, ((0, 16), (1, 8))),
        "row_token": jax.random.permutation(key_of[1], TOKENS).astype(jnp.int32),
        "seg_ids": jax.vmap(lambda own: jnp.searchsorted(jnp.cumsum(ragged(own, DOCS, TOK_DEV, TOK_DEV // 2, 1)), jnp.arange(TOK_DEV), side="right"))(jax.random.split(key_of[2], PACKS)).reshape((PACKS, TOK_DEV)).astype(jnp.int32),
        "stitch_weight": bell_draw(key_of[3], (DS, D), DS ** -0.5, 0.0625, ((0, 8), (1, 16))),
        "norm_gain": jnp.clip(1.0 + 0.1 * jax.random.normal(key_of[4], (D,), jnp.float32), 0.5, 1.5),
        "q_weight": draw_q_weight(jax.random.fold_in(key_of[9], 71), 0),
        "kv_weight": draw_kv_weight(jax.random.fold_in(key_of[9], 71), 0),
        "o_weight": bell_draw(key_of[7], (HEADS * HD, D), (HEADS * HD) ** -0.5, 0.0625, ((0, 16),)),
        "out_grad": bell_draw(key_of[8], (TOKENS, D), 1.0, 6.0, ((0, 8), (1, 16))),
    }


epsilon = 1e-05

def to_wide(narrow):
    return lax.optimization_barrier(narrow).astype(jnp.float32)

def frequencies():
    exponent = jnp.arange(0, HD, 2).astype(jnp.float32) / HD
    plain_rate = 500000.0 ** (-exponent)
    wavelength = 2.0 * math.pi / plain_rate
    smoothing = (8192.0 / wavelength - 1.0) / 3.0
    blended = (1.0 - smoothing) * plain_rate / 8.0 + smoothing * plain_rate
    return jnp.where(wavelength < 2048.0, plain_rate, jnp.where(wavelength > 8192.0, plain_rate / 8.0, blended))

def rotate(vector_in, cosine_table, sine_table):
    half_size = vector_in.shape[-1] // 2
    first_half = vector_in[..., :half_size]
    second = vector_in[..., half_size:]
    return jnp.concatenate([first_half * cosine_table - second * sine_table, second * cosine_table + first_half * sine_table], axis=-1)

def unrotate(vector_in, cosine_table, sine_table):
    half_size = vector_in.shape[-1] // 2
    first_half = vector_in[..., :half_size]
    second = vector_in[..., half_size:]
    return jnp.concatenate([first_half * cosine_table + second * sine_table, second * cosine_table - first_half * sine_table], axis=-1)

def positions(seg_rows):
    earlier = lax.optimization_barrier(jnp.sum((seg_rows[:, None, :] < seg_rows[:, :, None]).astype(jnp.int32), axis=2))
    return jnp.arange(seg_rows.shape[1], dtype=jnp.int32)[None, :] - earlier

def allowed_mask(seg_rows):
    same_doc = seg_rows[:, :, None] == seg_rows[:, None, :]
    index_row = jnp.arange(seg_rows.shape[1], dtype=jnp.int32)
    return (same_doc & (index_row[None, None, :] <= index_row[None, :, None])).astype(jnp.int32)

def reference(source, row_token, seg_ids, stitch_weight, norm_gain, q_weight, kv_weight, o_weight, out_grad):
    group_size = HEADS // KV
    score_scale = 1.0 / math.sqrt(HD)
    source_tok = jnp.zeros_like(source).at[row_token].set(source)
    hidden_in = jnp.dot(source_tok, stitch_weight, preferred_element_type=jnp.float32).astype(jnp.bfloat16)
    hidden_f = to_wide(hidden_in)
    inv_rms = lax.rsqrt(lax.optimization_barrier(jnp.mean(hidden_f * hidden_f, axis=1, keepdims=True)) + epsilon)
    normed = (hidden_f * inv_rms * norm_gain).astype(jnp.bfloat16)
    angles = positions(seg_ids).reshape(TOKENS).astype(jnp.float32)[:, None] * frequencies()[None, :]
    cosines = jnp.cos(angles)[:, None, :]
    sine_table = jnp.sin(angles)[:, None, :]
    queries = rotate(jnp.dot(normed, q_weight, preferred_element_type=jnp.float32).reshape(TOKENS, HEADS, HD), cosines, sine_table).astype(jnp.bfloat16)
    pair_proj = jnp.dot(normed, kv_weight, preferred_element_type=jnp.float32).reshape(TOKENS, KV, 2, HD)
    keys_bf = rotate(pair_proj[:, :, 0], cosines, sine_table).astype(jnp.bfloat16)
    values = pair_proj[:, :, 1].astype(jnp.bfloat16)
    query_f = to_wide(queries).reshape(PACKS, TOK_DEV, KV, group_size, HD)
    key_f = to_wide(keys_bf).reshape(PACKS, TOK_DEV, KV, HD)
    value_f = to_wide(values).reshape(PACKS, TOK_DEV, KV, HD)
    scores = jnp.einsum('ptgrd,psgd->pgrts', query_f, key_f) * score_scale
    allowed = allowed_mask(seg_ids)[:, None, None]
    scores = jnp.where(allowed != 0, scores, -1e+30)
    row_max = lax.optimization_barrier(jnp.max(scores, axis=-1, keepdims=True))
    exponents = jnp.exp(scores - row_max)
    attention = exponents / lax.optimization_barrier(jnp.sum(exponents, axis=-1, keepdims=True))
    attention_half_precision = attention.astype(jnp.bfloat16)
    attention_w = to_wide(attention_half_precision)
    context = jnp.einsum('pgrts,psgd->ptgrd', attention_w, value_f).astype(jnp.bfloat16).reshape(TOKENS, HEADS * HD)
    attended = jnp.dot(context, o_weight, preferred_element_type=jnp.float32)
    layer_out = (hidden_f + attended).astype(jnp.bfloat16)
    grad_context = jnp.dot(out_grad, o_weight.T, preferred_element_type=jnp.float32).astype(jnp.bfloat16)
    context_gradient = to_wide(grad_context).reshape(PACKS, TOK_DEV, KV, group_size, HD)
    grad_probs = jnp.einsum('ptgrd,psgd->pgrts', context_gradient, value_f)
    centered = grad_probs - lax.optimization_barrier(jnp.sum(grad_probs * attention, axis=-1, keepdims=True))
    score_gradient = to_wide((attention * centered * score_scale).astype(jnp.bfloat16))
    grad_queries = unrotate(jnp.einsum('pgrts,psgd->ptgrd', score_gradient, key_f).reshape(TOKENS, HEADS, HD), cosines, sine_table).astype(jnp.bfloat16)
    grad_keys = unrotate(jnp.einsum('pgrts,ptgrd->psgd', score_gradient, query_f).reshape(TOKENS, KV, HD), cosines, sine_table).astype(jnp.bfloat16)
    grad_values = jnp.einsum('pgrts,ptgrd->psgd', attention_w, context_gradient).reshape(TOKENS, KV, HD).astype(jnp.bfloat16)
    grad_pairs = jnp.stack([grad_keys, grad_values], axis=2).reshape(TOKENS, 2 * KV * HD)
    grad_normed = jnp.dot(grad_queries.reshape(TOKENS, HEADS * HD), q_weight.T, preferred_element_type=jnp.float32)
    grad_normed = grad_normed + jnp.dot(grad_pairs, kv_weight.T, preferred_element_type=jnp.float32)
    weighted = norm_gain * grad_normed
    cubed = inv_rms * inv_rms * inv_rms
    grad_hidden = (to_wide(out_grad) + inv_rms * weighted - hidden_f * cubed * lax.optimization_barrier(jnp.mean(weighted * hidden_f, axis=1, keepdims=True))).astype(jnp.bfloat16)

    def add_pack(running, pack_index):
        row_start = (pack_index * TOK_DEV).astype(jnp.int32)
        rows_here = lax.dynamic_slice_in_dim(source_tok, row_start, TOK_DEV, 0)
        grads_here = lax.dynamic_slice_in_dim(grad_hidden, row_start, TOK_DEV, 0)
        product = lax.dot_general(rows_here, grads_here, (((0,), (0,)), ((), ())), preferred_element_type=jnp.float32).astype(jnp.bfloat16)
        return (running + to_wide(product), None)
    stitch_grad, unused_out = lax.scan(add_pack, jnp.zeros((DS, D), jnp.float32), jnp.arange(PACKS, dtype=jnp.int32))
    return (layer_out, stitch_grad)
```

```python
import math

import jax
import jax.numpy as jnp
from jax import lax
from jax.sharding import PartitionSpec as P

HD = 128


epsilon = 1e-05


def swapped(value, axis, distance):
    mask = 2**distance
    pairs = [(source, source ^ mask) for source in range(lax.axis_size(axis))]
    return lax.ppermute(value, axis, pairs)


def frequencies():
    exponent = jnp.arange(0, HD, 2).astype(jnp.float32) / HD
    plain_rate = 500000.0 ** (-exponent)
    wavelength = 2.0 * math.pi / plain_rate
    smoothing = (8192.0 / wavelength - 1.0) / 3.0
    blended = (1.0 - smoothing) * plain_rate / 8.0 + smoothing * plain_rate
    return jnp.where(
        wavelength < 2048.0, plain_rate, jnp.where(wavelength > 8192.0, plain_rate / 8.0, blended)
    )


def rotate(vector_in, cosine_table, sine_table):
    half_size = vector_in.shape[-1] // 2
    first_half = vector_in[..., :half_size]
    second = vector_in[..., half_size:]
    return jnp.concatenate(
        [
            first_half * cosine_table - second * sine_table,
            second * cosine_table + first_half * sine_table,
        ],
        axis=-1,
    )


def unrotate(vector_in, cosine_table, sine_table):
    half_size = vector_in.shape[-1] // 2
    first_half = vector_in[..., :half_size]
    second = vector_in[..., half_size:]
    return jnp.concatenate(
        [
            first_half * cosine_table + second * sine_table,
            second * cosine_table - first_half * sine_table,
        ],
        axis=-1,
    )


def body(
    source, row_token, seg_ids, stitch_weight, norm_gain, q_weight, kv_weight, o_weight, out_grad
):
    tp_rank = lax.axis_index("tp")
    pack_len = seg_ids.shape[1]
    score_scale = 1.0 / math.sqrt(HD)
    gathered = lax.all_gather(source, "tp", axis=0, tiled=True)
    every_row_stack = gathered.shape[0]
    placing = (
        jnp.zeros((every_row_stack,), jnp.int32)
        .at[row_token]
        .set(jnp.arange(every_row_stack, dtype=jnp.int32))
    )
    token_rows = jnp.take(gathered, placing, axis=0)
    hidden_part = jnp.dot(token_rows, stitch_weight, preferred_element_type=jnp.float32)
    hidden_bf = lax.psum_scatter(
        hidden_part.astype(jnp.bfloat16), "tok", scatter_dimension=0, tiled=True
    )
    hidden_all = lax.all_gather(hidden_bf, "tp", axis=1, tiled=True)
    hidden_f = hidden_all.astype(jnp.float32)
    inv_rms = lax.rsqrt(jnp.mean(hidden_f * hidden_f, axis=1, keepdims=True) + epsilon)
    normed = (hidden_f * inv_rms * norm_gain).astype(jnp.bfloat16)
    seg_row = seg_ids[0]
    earlier = jnp.sum((seg_row[None, :] < seg_row[:, None]).astype(jnp.int32), axis=1)
    index_row = jnp.arange(pack_len, dtype=jnp.int32)
    angles = (index_row - earlier).astype(jnp.float32)[:, None] * frequencies()[None, :]
    cosines = jnp.cos(angles)[:, None, :]
    sine_table = jnp.sin(angles)[:, None, :]
    allowed = (
        (seg_row[:, None] == seg_row[None, :]) & (index_row[None, :] <= index_row[:, None])
    ).astype(jnp.int32)
    local_heads = q_weight.shape[1] // HD
    kv_local = 1
    repeat = local_heads // kv_local
    queries = rotate(
        jnp.dot(normed, q_weight, preferred_element_type=jnp.float32).reshape(
            pack_len, local_heads, HD
        ),
        cosines,
        sine_table,
    ).astype(jnp.bfloat16)
    projected = jnp.dot(normed, kv_weight, preferred_element_type=jnp.float32)
    is_key = tp_rank % 2 == 0
    own_part = jnp.where(
        is_key, rotate(projected, cosines[:, 0], sine_table[:, 0]), projected
    ).astype(jnp.bfloat16)
    partner = swapped(own_part, "tp", 0)
    per_head_keys = jnp.where(is_key, own_part, partner)[:, None, :]
    per_head_values = jnp.where(is_key, partner, own_part)[:, None, :]
    per_head_queries = queries.reshape(pack_len, kv_local, repeat, HD)
    scores = (
        jnp.einsum(
            "nkej,wkj->kenw", per_head_queries, per_head_keys, preferred_element_type=jnp.float32
        )
        * score_scale
    )
    scores = jnp.where(allowed != 0, scores, -1e30)
    row_max = jnp.max(scores, axis=-1, keepdims=True)
    exponents = jnp.exp(scores - row_max)
    attention = exponents / jnp.sum(exponents, axis=-1, keepdims=True)
    attention_half_precision = attention.astype(jnp.bfloat16)
    context = jnp.einsum(
        "cnfo,och->fcnh",
        attention_half_precision,
        per_head_values,
        preferred_element_type=jnp.float32,
    ).astype(jnp.bfloat16)
    context = context.reshape(pack_len, local_heads * HD)
    attended = lax.psum_scatter(
        jnp.dot(context, o_weight, preferred_element_type=jnp.float32).astype(jnp.bfloat16),
        "tp",
        scatter_dimension=1,
        tiled=True,
    ).astype(jnp.float32)
    layer_out = (hidden_bf.astype(jnp.float32) + attended).astype(jnp.bfloat16)
    gradient_every_row = lax.all_gather(out_grad, "tp", axis=1, tiled=True)
    grad_context = jnp.dot(
        gradient_every_row, o_weight.T, preferred_element_type=jnp.float32
    ).astype(jnp.bfloat16)
    context_gradient = grad_context.reshape(pack_len, kv_local, repeat, HD)
    grad_probs = jnp.einsum(
        "nkej,wkj->kenw", context_gradient, per_head_values, preferred_element_type=jnp.float32
    )
    centered = grad_probs - jnp.sum(grad_probs * attention, axis=-1, keepdims=True)
    score_gradient = (attention * centered * score_scale).astype(jnp.bfloat16)
    query_grad = jnp.einsum(
        "cnfo,och->fcnh", score_gradient, per_head_keys, preferred_element_type=jnp.float32
    )
    grad_queries = unrotate(
        query_grad.reshape(pack_len, local_heads, HD), cosines, sine_table
    ).astype(jnp.bfloat16)
    key_part = jnp.einsum(
        "bwlf,lbwj->fbj", score_gradient, per_head_queries, preferred_element_type=jnp.float32
    )
    value_part = jnp.einsum(
        "bwlf,lbwj->fbj",
        attention_half_precision,
        context_gradient,
        preferred_element_type=jnp.float32,
    )
    outgoing = jnp.where(is_key, value_part, key_part)[:, 0]
    incoming = swapped(outgoing.astype(jnp.bfloat16), "tp", 0).astype(outgoing.dtype)
    own_sum = jnp.where(is_key, key_part, value_part)[:, 0] + incoming
    grad_pairs = jnp.where(
        is_key, unrotate(own_sum, cosines[:, 0], sine_table[:, 0]), own_sum
    ).astype(jnp.bfloat16)
    grad_normed = jnp.dot(
        grad_queries.reshape(pack_len, local_heads * HD),
        q_weight.T,
        preferred_element_type=jnp.float32,
    )
    grad_normed = grad_normed + jnp.dot(grad_pairs, kv_weight.T, preferred_element_type=jnp.float32)
    weighted = norm_gain * grad_normed
    cubed = inv_rms * inv_rms * inv_rms
    norm_term = inv_rms * weighted - hidden_f * cubed * jnp.mean(
        weighted * hidden_f, axis=1, keepdims=True
    )
    grad_sum = lax.psum_scatter(
        norm_term.astype(jnp.bfloat16), "tp", scatter_dimension=1, tiled=True
    ).astype(jnp.float32)
    grad_hidden = (out_grad.astype(jnp.float32) + grad_sum).astype(jnp.bfloat16)
    every_grad = lax.all_gather(grad_hidden, "tok", axis=0, tiled=True)
    stitch_grad = lax.dot_general(
        token_rows, every_grad, (((0,), (0,)), ((), ())), preferred_element_type=jnp.float32
    )
    return (layer_out, stitch_grad)


def solution(mesh):
    placed = (
        P("tp", "tok"),
        P(),
        P("tok", None),
        P("tok", "tp"),
        P(),
        P(None, "tp"),
        P(None, "tp"),
        P("tp", None),
        P("tok", "tp"),
    )
    return jax.shard_map(
        body,
        mesh=mesh,
        in_specs=placed,
        out_specs=(P("tok", "tp"), P("tok", "tp")),
        check_vma=False,
    )
```

```python
import math

import jax
import jax.numpy as jnp
from jax import lax
from jax.experimental import pallas as pl
from jax.experimental.pallas import tpu as pltpu
from jax.sharding import PartitionSpec as P

HD = 128


epsilon = 1e-05


def swapped(value, axis, distance):
    mask = 2**distance
    pairs = [(source, source ^ mask) for source in range(lax.axis_size(axis))]
    return lax.ppermute(value, axis, pairs)


def frequencies():
    exponent = jnp.arange(0, HD, 2).astype(jnp.float32) / HD
    plain_rate = 500000.0 ** (-exponent)
    wavelength = 2.0 * math.pi / plain_rate
    smoothing = (8192.0 / wavelength - 1.0) / 3.0
    blended = (1.0 - smoothing) * plain_rate / 8.0 + smoothing * plain_rate
    return jnp.where(
        wavelength < 2048.0, plain_rate, jnp.where(wavelength > 8192.0, plain_rate / 8.0, blended)
    )


def rotate(vector_in, cosine_table, sine_table):
    half_size = vector_in.shape[-1] // 2
    first_half = vector_in[..., :half_size]
    second = vector_in[..., half_size:]
    return jnp.concatenate(
        [
            first_half * cosine_table - second * sine_table,
            second * cosine_table + first_half * sine_table,
        ],
        axis=-1,
    )


def unrotate(vector_in, cosine_table, sine_table):
    half_size = vector_in.shape[-1] // 2
    first_half = vector_in[..., :half_size]
    second = vector_in[..., half_size:]
    return jnp.concatenate(
        [
            first_half * cosine_table + second * sine_table,
            second * cosine_table - first_half * sine_table,
        ],
        axis=-1,
    )


class Group:
    def __init__(self, axis):
        tok, tp = lax.axis_index("tok"), lax.axis_index("tp")
        self.axis, self.tok, self.tp = axis, tok, tp
        if axis == "tp":
            self.ring, self.pair, self.core = tp // 4, (tp // 2) % 2, tp % 2
        else:
            self.ring, self.pair, self.core = tok // 2, tok % 2, 0

    def index(self, step, across, sibling=0):
        ring = lax.rem(self.ring + step, 4)
        pair = 1 - self.pair if across else self.pair
        if self.axis == "tp":
            core = 1 - self.core if sibling else self.core
            return ring * 4 + pair * 2 + core
        return ring * 2 + pair

    def device(self, step, across, sibling=0):
        index = self.index(step, across, sibling)
        return (self.tok, index) if self.axis == "tp" else (index, self.tp)

    def peers(self):
        found = [self.device(step, 0) for step in (1, 2, 3)] + [self.device(0, 1)]
        return found + ([self.device(0, 0, 1)] if self.axis == "tp" else [])


class Wire:
    def __init__(self, send, recv):
        self.send, self.recv, self.slots, self.sent = send, recv, {}, []

    def slot(self, key):
        return self.recv.at[self.slots.setdefault(key, len(self.slots))]

    def put(self, src, dst, device, key):
        copy = pltpu.make_async_remote_copy(
            src_ref=src,
            dst_ref=dst,
            send_sem=self.send.at[len(self.sent)],
            recv_sem=self.slot(key),
            device_id=device,
            device_id_type=pl.DeviceIdType.MESH,
        )
        copy.start()
        self.sent.append(copy)

    def got(self, view, device, key):
        pltpu.make_async_remote_copy(
            src_ref=view,
            dst_ref=view,
            send_sem=self.send.at[0],
            recv_sem=self.slot(key),
            device_id=device,
            device_id_type=pl.DeviceIdType.MESH,
        ).wait_recv()

    def drain(self):
        for copy in self.sent:
            copy.wait_send()


def greet(*groups):
    barrier = pltpu.get_barrier_semaphore()
    peers = [peer for group in groups for peer in group.peers()]
    for peer in peers:
        pl.semaphore_signal(
            barrier, inc=1, device_id=peer, device_id_type=pl.DeviceIdType.MESH
        )
    pl.semaphore_wait(barrier, len(peers))


def gather_steps(group, wire, shard, whole, local, name):
    two_cores = group.axis == "tp"

    def pass_on(step, across, half):
        if two_cores:
            view = whole(group.index(step, across), half)
            wire.put(view, view, group.device(0, 0, 1), (name, "core", step, across, half))

    def arrived(step, across, half):
        view = whole(group.index(step, across), half)
        wire.got(view, group.device(0, 1), (name, step, across, half))

    own = group.index(0, 0)
    wire.put(shard(0), whole(own, 0), group.device(0, 1), (name, 0, 1, 0))
    for half in (1, 0):
        for step in (1, 3, 2):
            wire.put(
                shard(half), whole(own, half), group.device(step, 0), (name, 4 - step, 0, half)
            )
    wire.put(shard(1), whole(own, 1), group.device(0, 1), (name, 0, 1, 1))
    kept = [pltpu.make_async_copy(shard(half), whole(own, half), local.at[half]) for half in (0, 1)]
    for copy in kept:
        copy.start()
    if two_cores:
        for half in (0, 1):
            wire.put(
                shard(half), whole(own, half), group.device(0, 0, 1), (name, "core", 0, 0, half)
            )
    yield
    arrived(0, 1, 0)
    view = whole(group.index(0, 1), 0)
    for step in (1, 3, 2):
        wire.put(view, view, group.device(step, 0), (name, 4 - step, 1, 0))
    pass_on(0, 1, 0)
    for step in (1, 3, 2):
        arrived(step, 0, 1)
        view = whole(group.index(step, 0), 1)
        wire.put(view, view, group.device(0, 1), (name, step, 1, 1))
        pass_on(step, 0, 1)
    yield
    for step in (1, 3, 2):
        arrived(step, 0, 0)
        pass_on(step, 0, 0)
    arrived(0, 1, 1)
    pass_on(0, 1, 1)
    yield
    for step in (1, 3, 2):
        for half in (0, 1):
            arrived(step, 1, half)
            pass_on(step, 1, half)
    if two_cores:
        for step in (0, 1, 3, 2):
            for across in (0, 1):
                for half in (0, 1):
                    view = whole(group.index(step, across, 1), half)
                    wire.got(view, group.device(0, 0, 1), (name, "core", step, across, half))
    for copy in kept:
        copy.wait()


def wide(value):
    return value.astype(jnp.float32)


def scatter_steps(group, wire, part, finish, rows, buffers, name):
    mine, by_core, by_pair, by_ring, by_ring_last, by_pair_last = buffers
    half_rows = rows // 2
    first, second = slice(0, half_rows), slice(half_rows, rows)
    two_cores = group.axis == "tp"
    order = [(step, 1) for step in (0, 1, 3, 2)] + [(step, 0) for step in (1, 3, 2, 0)]
    if two_cores:
        for step, across in order:
            wire.put(
                part(group.index(step, across, 1)),
                by_core.at[step, across],
                group.device(0, 0, 1),
                (name, "core", step, across),
            )
    yield
    for step, across in order:
        value = part(group.index(step, across))[...]
        if two_cores:
            wire.got(by_core.at[step, across], group.device(0, 0, 1), (name, "core", step, across))
            value = (wide(value) + wide(by_core[step, across])).astype(jnp.bfloat16)
        mine[step, across] = value
        if across:
            wire.put(
                mine.at[step, 1, first], by_pair.at[step], group.device(0, 1), (name, "pair", step)
            )
        if step:
            wire.put(
                mine.at[step, across, second],
                by_ring.at[4 - step, across],
                group.device(step, 0),
                (name, "ring", 4 - step, across),
            )
    yield
    for step in (1, 3, 2, 0):
        wire.got(by_pair.at[step], group.device(0, 1), (name, "pair", step))
        total = wide(mine[step, 0, first]) + wide(by_pair[step])
        if step:
            mine[step, 0, first] = total.astype(jnp.bfloat16)
            wire.put(
                mine.at[step, 0, first],
                by_ring_last.at[4 - step],
                group.device(step, 0),
                (name, "last", 4 - step),
            )
        else:
            first_total = total
    for across in (1, 0):
        total = wide(mine[0, across, second])
        for step in (1, 3, 2):
            wire.got(by_ring.at[step, across], group.device(step, 0), (name, "ring", step, across))
            total = total + wide(by_ring[step, across])
        if across:
            mine[0, 1, second] = total.astype(jnp.bfloat16)
            wire.put(mine.at[0, 1, second], by_pair_last, group.device(0, 1), (name, "last"))
    yield
    wire.got(by_pair_last, group.device(0, 1), (name, "last"))
    finish(second, total + wide(by_pair_last[...]))
    for step in (1, 3, 2):
        wire.got(by_ring_last.at[step], group.device(step, 0), (name, "last", step))
        first_total = first_total + wide(by_ring_last[step])
    finish(first, first_total)


def scatter_buffers(rows, columns, two_cores):
    half, kind = rows // 2, jnp.bfloat16
    return [
        pltpu.VMEM((4, 2, rows, columns), kind),
        pltpu.VMEM((4, 2, rows, columns) if two_cores else (1, 1, 16, 128), kind),
        pltpu.VMEM((4, half, columns), kind),
        pltpu.VMEM((4, 2, half, columns), kind),
        pltpu.VMEM((4, half, columns), kind),
        pltpu.VMEM((half, columns), kind),
    ]


def interleave(*streams):
    streams = list(streams)
    while streams:
        for stream in list(streams):
            if next(stream, "end") == "end":
                streams.remove(stream)


def column_views(ref, rows, columns):
    half_rows = rows // 2

    def view(slot, half=None):
        lanes = pl.ds(pl.multiple_of(slot * columns, columns), columns)
        if half is None:
            return ref.at[:, lanes]
        return ref.at[pl.ds(half * half_rows, half_rows), lanes]

    return view


def row_views(ref, rows):
    half_rows = rows // 2

    def view(slot, half=None):
        if half is None:
            return ref.at[pl.ds(pl.multiple_of(slot * rows, rows), rows)]
        return ref.at[pl.ds(pl.multiple_of(slot * rows + half * half_rows, half_rows), half_rows)]

    return view


def halves(ref):
    half_rows = ref.shape[0] // 2
    return lambda half: ref.at[pl.ds(half * half_rows, half_rows)]


SEMS = [pltpu.SemaphoreType.DMA((80,)), pltpu.SemaphoreType.DMA((80,)), pltpu.SemaphoreType.DMA((2,))]
ANYWHERE = pl.BlockSpec(memory_space=pl.ANY)
ON_CHIP = pl.BlockSpec(memory_space=pltpu.VMEM)


def call(kernel, name, number, out_shape, in_specs, out_specs, scratch, moved, *operands):
    return pl.pallas_call(
        kernel,
        out_shape=out_shape,
        in_specs=in_specs,
        out_specs=out_specs,
        scratch_shapes=scratch,
        compiler_params=pltpu.CompilerParams(
            collective_id=number, has_side_effects=True, vmem_limit_bytes=40 << 20
        ),
        cost_estimate=pl.CostEstimate(flops=0, bytes_accessed=moved, transcendentals=0),
        name=name,
    )(*operands)


def gather_source(source):
    rows, columns = source.shape

    def kernel(x, whole, send, recv, local):
        group, wire = Group("tp"), Wire(send, recv)
        greet(group)
        interleave(gather_steps(group, wire, halves(x), row_views(whole, rows), local, "a"))
        wire.drain()

    return call(
        kernel, "gather_source", 1, jax.ShapeDtypeStruct((16 * rows, columns), source.dtype),
        [ANYWHERE], ANYWHERE, SEMS, 40 << 20, source,
    )


def gather_hidden(hidden):
    rows, columns = hidden.shape

    def kernel(x, whole, send, recv, local):
        group, wire = Group("tp"), Wire(send, recv)
        greet(group)
        interleave(
            gather_steps(group, wire, halves(x), column_views(whole, rows, columns), local, "a")
        )
        wire.drain()

    return call(
        kernel, "gather_hidden", 2, jax.ShapeDtypeStruct((rows, 16 * columns), hidden.dtype),
        [ANYWHERE], ANYWHERE, SEMS, 40 << 20, hidden,
    )


def gather_gradient_scatter_hidden(out_grad, part):
    rows, columns = out_grad.shape

    def kernel(x, part_ref, whole, total, send, recv, local, *buffers):
        across, along, wire = Group("tp"), Group("tok"), Wire(send, recv)
        greet(across, along)

        def finish(where, value):
            total[where] = value.astype(total.dtype)

        interleave(
            scatter_steps(along, wire, row_views(part_ref, rows), finish, rows, buffers, "s"),
            gather_steps(across, wire, halves(x), column_views(whole, rows, columns), local, "a"),
        )
        wire.drain()

    return call(
        kernel, "gather_gradient_scatter_hidden", 3,
        (
            jax.ShapeDtypeStruct((rows, 16 * columns), out_grad.dtype),
            jax.ShapeDtypeStruct((rows, columns), part.dtype),
        ),
        [ANYWHERE, ON_CHIP], (ANYWHERE, ON_CHIP),
        SEMS + scatter_buffers(rows, columns, False), 60 << 20, out_grad, part,
    )


def scatter_gradient(part, out_grad):
    rows, columns = out_grad.shape

    def kernel(part_ref, base, total, send, recv, local, *buffers):
        group, wire = Group("tp"), Wire(send, recv)
        greet(group)

        def finish(where, value):
            total[where] = (wide(base[where]) + value).astype(total.dtype)

        interleave(
            scatter_steps(
                group, wire, column_views(part_ref, rows, columns), finish, rows, buffers, "s"
            )
        )
        wire.drain()

    return call(
        kernel, "scatter_gradient", 4, jax.ShapeDtypeStruct((rows, columns), out_grad.dtype),
        [ON_CHIP, ON_CHIP], ON_CHIP, SEMS + scatter_buffers(rows, columns, True), 40 << 20,
        part, out_grad,
    )


def scatter_attended_gather_gradient(part, hidden, gradient):
    rows, columns = hidden.shape

    def kernel(part_ref, base, x, total, whole, send, recv, local, *buffers):
        across, along, wire = Group("tp"), Group("tok"), Wire(send, recv)
        greet(across, along)

        def finish(where, value):
            total[where] = (wide(base[where]) + value).astype(total.dtype)

        interleave(
            gather_steps(along, wire, halves(x), row_views(whole, rows), local, "a"),
            scatter_steps(
                across, wire, column_views(part_ref, rows, columns), finish, rows, buffers, "s"
            ),
        )
        wire.drain()

    return call(
        kernel, "scatter_attended_gather_gradient", 5,
        (
            jax.ShapeDtypeStruct((rows, columns), hidden.dtype),
            jax.ShapeDtypeStruct((8 * rows, columns), gradient.dtype),
        ),
        [ON_CHIP, ON_CHIP, ANYWHERE], (ON_CHIP, ANYWHERE),
        SEMS + scatter_buffers(rows, columns, True), 60 << 20, part, hidden, gradient,
    )


def body(
    source, row_token, seg_ids, stitch_weight, norm_gain, q_weight, kv_weight, o_weight, out_grad
):
    tp_rank = lax.axis_index("tp")
    pack_len = seg_ids.shape[1]
    score_scale = 1.0 / math.sqrt(HD)
    gathered = gather_source(source)
    every_row = gathered.shape[0]
    part = jnp.dot(gathered, stitch_weight, preferred_element_type=jnp.float32)
    placing = (
        jnp.arange(every_row, dtype=jnp.int32)[:, None] == row_token[None, :]
    ).astype(jnp.bfloat16)
    token_part = jnp.dot(
        placing, part.astype(jnp.bfloat16), preferred_element_type=jnp.float32
    ).astype(jnp.bfloat16)
    gradient_every_row, hidden_bf = gather_gradient_scatter_hidden(out_grad, token_part)
    hidden_all = gather_hidden(hidden_bf)
    hidden_f = hidden_all.astype(jnp.float32)
    inv_rms = lax.rsqrt(jnp.mean(hidden_f * hidden_f, axis=1, keepdims=True) + epsilon)
    normed = (hidden_f * inv_rms * norm_gain).astype(jnp.bfloat16)
    seg_row = seg_ids[0]
    earlier = jnp.sum((seg_row[None, :] < seg_row[:, None]).astype(jnp.int32), axis=1)
    index_row = jnp.arange(pack_len, dtype=jnp.int32)
    angles = (index_row - earlier).astype(jnp.float32)[:, None] * frequencies()[None, :]
    cosines = jnp.cos(angles)[:, None, :]
    sine_table = jnp.sin(angles)[:, None, :]
    allowed = (
        (seg_row[:, None] == seg_row[None, :]) & (index_row[None, :] <= index_row[:, None])
    ).astype(jnp.int32)
    local_heads = q_weight.shape[1] // HD
    kv_local = 1
    repeat = local_heads // kv_local
    queries = rotate(
        jnp.dot(normed, q_weight, preferred_element_type=jnp.float32).reshape(
            pack_len, local_heads, HD
        ),
        cosines,
        sine_table,
    ).astype(jnp.bfloat16)
    projected = jnp.dot(normed, kv_weight, preferred_element_type=jnp.float32)
    is_key = tp_rank % 2 == 0
    own_part = jnp.where(
        is_key, rotate(projected, cosines[:, 0], sine_table[:, 0]), projected
    ).astype(jnp.bfloat16)
    partner = swapped(own_part, "tp", 0)
    per_head_keys = jnp.where(is_key, own_part, partner)[:, None, :]
    per_head_values = jnp.where(is_key, partner, own_part)[:, None, :]
    per_head_queries = queries.reshape(pack_len, kv_local, repeat, HD)
    scores = (
        jnp.einsum(
            "nkej,wkj->kenw", per_head_queries, per_head_keys, preferred_element_type=jnp.float32
        )
        * score_scale
    )
    scores = jnp.where(allowed != 0, scores, -1e30)
    row_max = jnp.max(scores, axis=-1, keepdims=True)
    exponents = jnp.exp(scores - row_max)
    attention = exponents / jnp.sum(exponents, axis=-1, keepdims=True)
    attention_half_precision = attention.astype(jnp.bfloat16)
    context = jnp.einsum(
        "cnfo,och->fcnh",
        attention_half_precision,
        per_head_values,
        preferred_element_type=jnp.float32,
    ).astype(jnp.bfloat16)
    context = context.reshape(pack_len, local_heads * HD)
    attended_part = jnp.dot(context, o_weight, preferred_element_type=jnp.float32).astype(
        jnp.bfloat16
    )
    grad_context = jnp.dot(
        gradient_every_row, o_weight.T, preferred_element_type=jnp.float32
    ).astype(jnp.bfloat16)
    context_gradient = grad_context.reshape(pack_len, kv_local, repeat, HD)
    grad_probs = jnp.einsum(
        "nkej,wkj->kenw", context_gradient, per_head_values, preferred_element_type=jnp.float32
    )
    centered = grad_probs - jnp.sum(grad_probs * attention, axis=-1, keepdims=True)
    score_gradient = (attention * centered * score_scale).astype(jnp.bfloat16)
    query_grad = jnp.einsum(
        "cnfo,och->fcnh", score_gradient, per_head_keys, preferred_element_type=jnp.float32
    )
    grad_queries = unrotate(
        query_grad.reshape(pack_len, local_heads, HD), cosines, sine_table
    ).astype(jnp.bfloat16)
    key_part = jnp.einsum(
        "bwlf,lbwj->fbj", score_gradient, per_head_queries, preferred_element_type=jnp.float32
    )
    value_part = jnp.einsum(
        "bwlf,lbwj->fbj",
        attention_half_precision,
        context_gradient,
        preferred_element_type=jnp.float32,
    )
    outgoing = jnp.where(is_key, value_part, key_part)[:, 0]
    incoming = swapped(outgoing.astype(jnp.bfloat16), "tp", 0).astype(outgoing.dtype)
    own_sum = jnp.where(is_key, key_part, value_part)[:, 0] + incoming
    grad_pairs = jnp.where(
        is_key, unrotate(own_sum, cosines[:, 0], sine_table[:, 0]), own_sum
    ).astype(jnp.bfloat16)
    grad_normed = jnp.dot(
        grad_queries.reshape(pack_len, local_heads * HD),
        q_weight.T,
        preferred_element_type=jnp.float32,
    )
    grad_normed = grad_normed + jnp.dot(grad_pairs, kv_weight.T, preferred_element_type=jnp.float32)
    weighted = norm_gain * grad_normed
    cubed = inv_rms * inv_rms * inv_rms
    norm_term = inv_rms * weighted - hidden_f * cubed * jnp.mean(
        weighted * hidden_f, axis=1, keepdims=True
    )
    grad_hidden = scatter_gradient(norm_term.astype(jnp.bfloat16), out_grad)
    layer_out, every_grad = scatter_attended_gather_gradient(attended_part, hidden_bf, grad_hidden)
    source_grad = jnp.dot(
        placing.T, every_grad, preferred_element_type=jnp.float32
    ).astype(jnp.bfloat16)
    stitch_grad = lax.dot_general(
        gathered, source_grad, (((0,), (0,)), ((), ())), preferred_element_type=jnp.float32
    )
    return (layer_out, stitch_grad)


def solution(mesh):
    placed = (
        P("tp", "tok"),
        P(),
        P("tok", None),
        P("tok", "tp"),
        P(),
        P(None, "tp"),
        P(None, "tp"),
        P("tp", None),
        P("tok", "tp"),
    )
    return jax.shard_map(
        body,
        mesh=mesh,
        in_specs=placed,
        out_specs=(P("tok", "tp"), P("tok", "tp")),
        check_vma=False,
    )
```

```python
import math

import jax
import jax.numpy as jnp
from jax import lax
from jax.experimental import pallas as pl
from jax.experimental.pallas import tpu as pltpu
from jax.sharding import PartitionSpec as P

HD = 128


epsilon = 1e-05


def frequencies():
    exponent = jnp.arange(0, HD, 2).astype(jnp.float32) / HD
    plain_rate = 500000.0 ** (-exponent)
    wavelength = 2.0 * math.pi / plain_rate
    smoothing = (8192.0 / wavelength - 1.0) / 3.0
    blended = (1.0 - smoothing) * plain_rate / 8.0 + smoothing * plain_rate
    return jnp.where(
        wavelength < 2048.0, plain_rate, jnp.where(wavelength > 8192.0, plain_rate / 8.0, blended)
    )


class Group:
    def __init__(self, axis):
        tok, tp = lax.axis_index("tok"), lax.axis_index("tp")
        self.axis, self.tok, self.tp = axis, tok, tp
        if axis == "tp":
            self.ring, self.pair, self.core = tp // 4, (tp // 2) % 2, tp % 2
        else:
            self.ring, self.pair, self.core = tok // 2, tok % 2, 0

    def index(self, step, across, sibling=0):
        ring = lax.rem(self.ring + step, 4)
        pair = 1 - self.pair if across else self.pair
        if self.axis == "tp":
            core = 1 - self.core if sibling else self.core
            return ring * 4 + pair * 2 + core
        return ring * 2 + pair

    def device(self, step, across, sibling=0):
        index = self.index(step, across, sibling)
        return (self.tok, index) if self.axis == "tp" else (index, self.tp)

    def peers(self):
        found = [self.device(step, 0) for step in (1, 2, 3)] + [self.device(0, 1)]
        return found + ([self.device(0, 0, 1)] if self.axis == "tp" else [])


class Wire:
    def __init__(self, send, recv):
        self.send, self.recv, self.slots, self.sent = send, recv, {}, []

    def slot(self, key):
        return self.recv.at[self.slots.setdefault(key, len(self.slots))]

    def put(self, src, dst, device, key):
        copy = pltpu.make_async_remote_copy(
            src_ref=src,
            dst_ref=dst,
            send_sem=self.send.at[len(self.sent)],
            recv_sem=self.slot(key),
            device_id=device,
            device_id_type=pl.DeviceIdType.MESH,
        )
        copy.start()
        self.sent.append(copy)

    def got(self, view, device, key):
        pltpu.make_async_remote_copy(
            src_ref=view,
            dst_ref=view,
            send_sem=self.send.at[0],
            recv_sem=self.slot(key),
            device_id=device,
            device_id_type=pl.DeviceIdType.MESH,
        ).wait_recv()

    def drain(self):
        for copy in self.sent:
            copy.wait_send()


def greet(*groups):
    barrier = pltpu.get_barrier_semaphore()
    peers = [peer for group in groups for peer in group.peers()]
    for peer in peers:
        pl.semaphore_signal(
            barrier, inc=1, device_id=peer, device_id_type=pl.DeviceIdType.MESH
        )
    pl.semaphore_wait(barrier, len(peers))


def wide(value):
    return value.astype(jnp.float32)


def gather_steps(group, wire, shard, whole, cut, local, name, ready):
    two_cores = group.axis == "tp"

    def pass_on(step, across, half):
        if two_cores:
            view = whole(group.index(step, across), half)
            wire.put(view, view, group.device(0, 0, 1), (name, "core", step, across, half))

    def arrived(step, across, half):
        view = whole(group.index(step, across), half)
        wire.got(view, group.device(0, 1), (name, step, across, half))

    def complete(step, across):
        if two_cores:
            for half in (0, 1):
                view = whole(group.index(step, across, 1), half)
                wire.got(view, group.device(0, 0, 1), (name, "core", step, across, half))
        ready(step, across)

    own = group.index(0, 0)
    wire.put(shard(0), whole(own, 0), group.device(0, 1), (name, 0, 1, 0))
    for half in (1, 0):
        for step in (1, 3, 2):
            wire.put(
                shard(half), whole(own, half), group.device(step, 0), (name, 4 - step, 0, half)
            )
    wire.put(shard(1), whole(own, 1), group.device(0, 1), (name, 0, 1, 1))
    kept = [pltpu.make_async_copy(shard(half), whole(own, half), local.at[half]) for half in (0, 1)]
    for copy in kept:
        copy.start()
    if two_cores:
        for half in (0, 1):
            wire.put(
                shard(half), whole(own, half), group.device(0, 0, 1), (name, "core", 0, 0, half)
            )
    for copy in kept:
        copy.wait()
    complete(0, 0)
    yield
    arrived(0, 1, 0)
    view = whole(group.index(0, 1), 0)
    for step in (1, 3, 2):
        wire.put(view, view, group.device(step, 0), (name, 4 - step, 1, 0))
    pass_on(0, 1, 0)
    for step in (1, 3, 2):
        arrived(step, 0, 1)
        view = whole(group.index(step, 0), 1)
        wire.put(view, view, group.device(0, 1), (name, step, 1, 1))
        pass_on(step, 0, 1)
    yield
    for step in (1, 3, 2):
        arrived(step, 0, 0)
        pass_on(step, 0, 0)
    arrived(0, 1, 1)
    pass_on(0, 1, 1)
    yield
    for step in (1, 3, 2):
        complete(step, 0)
    complete(0, 1)
    yield
    for step in (1, 3, 2):
        for half in (0, 1):
            arrived(step, 1, half)
            pass_on(step, 1, half)
    yield
    for step in (1, 3, 2):
        complete(step, 1)


ORDER = [(step, 1) for step in (0, 1, 3, 2)] + [(step, 0) for step in (1, 3, 2, 0)]


def core_steps(group, wire, term, mine, leaving, by_core, name):
    for step, across in ORDER:
        leaving[step, across] = term(group.index(step, across, 1))
        wire.put(
            leaving.at[step, across],
            by_core.at[step, across],
            group.device(0, 0, 1),
            (name, "core", step, across),
        )
        mine[step, across] = term(group.index(step, across))
        yield
        wire.got(by_core.at[step, across], group.device(0, 0, 1), (name, "core", step, across))
        mine[step, across] = (wide(mine[step, across]) + wide(by_core[step, across])).astype(
            jnp.bfloat16
        )
        yield step, across


def scatter_first(group, wire, mine, by_pair, by_ring, cut, name, step, across):
    if across:
        wire.put(
            mine(step, 1, 0), by_pair.at[step], group.device(0, 1), (name, "pair", step)
        )
    if step:
        wire.put(
            mine(step, across, 1),
            by_ring.at[4 - step, across],
            group.device(step, 0),
            (name, "ring", 4 - step, across),
        )


def scatter_steps(group, wire, mine, finish, last, buffers, name):
    by_pair, by_ring, by_ring_last, by_pair_last = buffers
    going, going_last = last
    for step in (1, 3, 2, 0):
        wire.got(by_pair.at[step], group.device(0, 1), (name, "pair", step))
        total = wide(mine(step, 0, 0)[...]) + wide(by_pair[step])
        if step:
            going[step] = total.astype(jnp.bfloat16)
            wire.put(
                going.at[step], by_ring_last.at[4 - step], group.device(step, 0),
                (name, "last", 4 - step),
            )
        else:
            first_total = total
    for across in (1, 0):
        total = wide(mine(0, across, 1)[...])
        for step in (1, 3, 2):
            wire.got(by_ring.at[step, across], group.device(step, 0), (name, "ring", step, across))
            total = total + wide(by_ring[step, across])
        if across:
            going_last[...] = total.astype(jnp.bfloat16)
            wire.put(going_last, by_pair_last, group.device(0, 1), (name, "last"))
    yield
    wire.got(by_pair_last, group.device(0, 1), (name, "last"))
    finish(1, total + wide(by_pair_last[...]))
    for step in (1, 3, 2):
        wire.got(by_ring_last.at[step], group.device(step, 0), (name, "last", step))
        first_total = first_total + wide(by_ring_last[step])
    finish(0, first_total)


def scatter_buffers(rows, columns, cut):
    first, second, kind = cut, rows - cut, jnp.bfloat16
    return [
        pltpu.VMEM((4, first, columns), kind),
        pltpu.VMEM((4, 2, second, columns), kind),
        pltpu.VMEM((4, first, columns), kind),
        pltpu.VMEM((second, columns), kind),
        pltpu.VMEM((4, first, columns), kind),
        pltpu.VMEM((second, columns), kind),
    ]


def part_of(half, rows, cut):
    return pl.ds(cut, rows - cut) if half else pl.ds(0, cut)


def chunk_views(ref, rows, cut):
    return lambda step, across, half: ref.at[step, across, part_of(half, rows, cut)]


def column_views(ref, rows, columns, cut):
    def view(slot, half):
        return ref.at[
            part_of(half, rows, cut), pl.ds(pl.multiple_of(slot * columns, columns), columns)
        ]

    return view


def row_views(ref, rows, cut):
    def view(slot, half):
        start, size = (cut, rows - cut) if half else (0, cut)
        return ref.at[pl.ds(pl.multiple_of(slot * rows + start, 32), size)]

    return view


def shard_views(ref, rows, cut):
    return lambda half: ref.at[part_of(half, rows, cut)]


def run(steps):
    for _ in steps:
        pass


def advance(steps):
    return next(steps, None)


ANYWHERE = pl.BlockSpec(memory_space=pl.ANY)
ON_CHIP = pl.BlockSpec(memory_space=pltpu.VMEM)


def dot(a, b, over=((1,), (0,))):
    return lax.dot_general(a, b, (over, ((), ())), preferred_element_type=jnp.float32)


BY_ROWS = ((1,), (1,))
BY_COLUMNS = ((0,), (0,))


def forward_kernel(
    source, row_token, stitch, gain, q_hbm, kv_hbm, o_hbm, out_grad,
    token_out, hidden_out, hidden, queries, pairs, squares, grad_context,
    send, recv, local, loads,
    stitch_in, q_in, kv_in, o_in, rows_in, hidden_in, gradient_in,
    product, token_part, token_rows, total_context,
    *buffers,
):
    tp, tok, wire = Group("tp"), Group("tok"), Wire(send, recv)
    rows, columns = out_grad.shape
    source_rows = source.shape[0]
    tiles = token_part.shape[0] // rows
    pulls = [
        pltpu.make_async_copy(a, b, loads.at[i])
        for i, (a, b) in enumerate(
            ((stitch, stitch_in), (o_hbm, o_in), (q_hbm, q_in), (kv_hbm, kv_in))
        )
    ]
    for pull in pulls:
        pull.start()
    greet(tp, tok)
    pulls[0].wait()

    def placed(tile, taken):
        index = lax.broadcasted_iota(jnp.int32, (rows, taken.shape[1]), 0) + tile * rows
        return jnp.where(index == taken, 1.0, 0.0).astype(jnp.bfloat16)

    def source_ready(step, across):
        block = tp.index(step, across) // 2
        here = pl.ds(pl.multiple_of(block * 2 * source_rows, 2 * source_rows), 2 * source_rows)
        product[...] = dot(rows_in[here, :], stitch_in[...]).astype(jnp.bfloat16)

        @pl.loop(0, tiles)
        def _(tile):
            there = pl.ds(pl.multiple_of(tile * rows, rows), rows)
            moved = dot(placed(tile, row_token[:, here]), product[...]).astype(jnp.bfloat16)
            if (step, across) == (0, 0):
                token_part[there, :] = moved
            else:
                token_part[there, :] = token_part[there, :] + moved

    def nothing(step, across):
        pass

    run(
        gather_steps(
            tp, wire, shard_views(source, source_rows, 64), row_views(rows_in, source_rows, 64),
            64, local.at[pl.ds(0, 2)], "source", source_ready,
        )
    )

    cut = 64
    going, buffers = buffers[4:], buffers[:4]

    def part(step, across, half):
        start, size = (cut, rows - cut) if half else (0, cut)
        return token_part.at[
            pl.ds(pl.multiple_of(tok.index(step, across) * rows + start, 32), size)
        ]

    def finish(half, value):
        hidden[part_of(half, rows, cut), :] = value.astype(hidden.dtype)

    for step, across in ORDER:
        scatter_first(tok, wire, part, buffers[0], buffers[1], cut, "hidden", step, across)
    gathering = gather_steps(
        tp, wire, shard_views(out_grad, rows, 192), column_views(gradient_in, rows, columns, 192),
        192, local.at[pl.ds(2, 2)], "gradient", nothing,
    )
    scattering = scatter_steps(tok, wire, part, finish, going, buffers, "hidden")

    def reorder(first, last):
        @pl.loop(first, last)
        def _(tile):
            there = pl.ds(pl.multiple_of(tile * rows, rows), rows)
            token_rows[there, :] = dot(placed(tile, row_token[...]), rows_in[...]).astype(
                token_rows.dtype
            )

    advance(gathering)
    reorder(0, tiles // 4)
    advance(scattering)
    advance(gathering)
    advance(gathering)
    reorder(tiles // 4, tiles // 2)
    advance(scattering)
    run(gathering)

    def hidden_ready(step, across):
        if (step, across) == (0, 0):
            pulls[2].wait()
            pulls[3].wait()
        block = tp.index(step, across) // 2
        here = pl.ds(pl.multiple_of(block * 2 * columns, 2 * columns), 2 * columns)
        value = wide(hidden_in[:, here])
        scaled = (value * gain[:, here]).astype(jnp.bfloat16)
        to_queries = dot(scaled, q_in[here, :])
        to_pairs = dot(scaled, kv_in[here, :])
        squared = jnp.broadcast_to(
            jnp.sum(value * value, axis=1, keepdims=True), squares.shape
        )
        if (step, across) == (0, 0):
            queries[...], pairs[...], squares[...] = to_queries, to_pairs, squared
        else:
            queries[...] += to_queries
            pairs[...] += to_pairs
            squares[...] += squared

    gathering = gather_steps(
        tp, wire, shard_views(hidden, rows, 128), column_views(hidden_in, rows, columns, 128),
        128, local.at[pl.ds(4, 2)], "all", hidden_ready,
    )
    advance(gathering)
    reorder(tiles // 2, tiles)
    tokens_out = pltpu.make_async_copy(token_rows, token_out, loads.at[4])
    tokens_out.start()
    advance(gathering)
    advance(gathering)
    pulls[1].wait()
    total_context[...] = jnp.zeros_like(total_context)

    @pl.loop(0, gradient_in.shape[1] // 1024)
    def _(block):
        here = pl.ds(pl.multiple_of(block * 1024, 1024), 1024)
        total_context[...] += dot(gradient_in[:, here], o_in[:, here], BY_ROWS)

    grad_context[...] = total_context[...].astype(grad_context.dtype)
    run(gathering)
    hidden_copy = pltpu.make_async_copy(hidden_in, hidden_out, loads.at[5])
    hidden_copy.start()
    tokens_out.wait()
    hidden_copy.wait()
    wire.drain()


def forward(source, row_token, stitch, gain, q_weight, kv_weight, o_weight, out_grad):
    rows, columns = out_grad.shape
    source_rows, features = source.shape
    tokens, width, heads = 16 * source_rows, 16 * columns, q_weight.shape[1]
    half = jnp.bfloat16
    return pl.pallas_call(
        forward_kernel,
        out_shape=(
            jax.ShapeDtypeStruct((tokens, features), half),
            jax.ShapeDtypeStruct((rows, width), half),
            jax.ShapeDtypeStruct((rows, columns), half),
            jax.ShapeDtypeStruct((rows, heads), jnp.float32),
            jax.ShapeDtypeStruct((rows, HD), jnp.float32),
            jax.ShapeDtypeStruct((rows, HD), jnp.float32),
            jax.ShapeDtypeStruct((rows, heads), half),
        ),
        in_specs=[ANYWHERE, ON_CHIP, ANYWHERE, ON_CHIP, ANYWHERE, ANYWHERE, ANYWHERE, ANYWHERE],
        out_specs=(ANYWHERE, ANYWHERE) + (ON_CHIP,) * 5,
        scratch_shapes=[
            pltpu.SemaphoreType.DMA((120,)),
            pltpu.SemaphoreType.DMA((120,)),
            pltpu.SemaphoreType.DMA((6,)),
            pltpu.SemaphoreType.DMA((6,)),
            pltpu.VMEM(stitch.shape, half),
            pltpu.VMEM(q_weight.shape, half),
            pltpu.VMEM(kv_weight.shape, half),
            pltpu.VMEM(o_weight.shape, half),
            pltpu.VMEM((tokens, features), half),
            pltpu.VMEM((rows, width), half),
            pltpu.VMEM((rows, width), half),
            pltpu.VMEM((2 * source_rows, columns), half),
            pltpu.VMEM((tokens, columns), half),
            pltpu.VMEM((tokens, features), half),
            pltpu.VMEM((rows, heads), jnp.float32),
        ]
        + scatter_buffers(rows, columns, 64),
        compiler_params=pltpu.CompilerParams(
            collective_id=1, has_side_effects=True, vmem_limit_bytes=60 << 20
        ),
        cost_estimate=pl.CostEstimate(flops=30 << 30, bytes_accessed=200 << 20, transcendentals=0),
        name="forward",
    )(
        source, row_token.reshape(1, -1), stitch, gain.reshape(1, -1), q_weight, kv_weight,
        o_weight, out_grad,
    )


def backward_kernel(
    queries, pairs, squares, grad_context, cosines, sines, seg_row, seg_column, gain,
    hidden, out_grad, hidden_hbm, token_hbm, q_hbm, kv_hbm, o_hbm,
    layer_out, stitch_grad,
    send, recv, local, loads,
    q_in, kv_in, o_in, hidden_in, token_rows, every_grad, grad_hidden,
    queries_in, context, grad_queries, grad_pairs, own_pair, other_pair, leaving_pair, back_pair,
    mine, leaving, by_core, mine_out, leaving_out, by_core_out,
    *buffers,
):
    tp, tok, wire = Group("tp"), Group("tok"), Wire(send, recv)
    rows, columns = out_grad.shape
    width = hidden_in.shape[1]
    half = jnp.bfloat16
    pulls = [
        pltpu.make_async_copy(a, b, loads.at[i])
        for i, (a, b) in enumerate(
            (
                (q_hbm, q_in), (kv_hbm, kv_in), (hidden_hbm, hidden_in), (o_hbm, o_in),
                (token_hbm, token_rows),
            )
        )
    ]
    for pull in pulls:
        pull.start()
    greet(tp, tok)

    cosine, sine = cosines[...], sines[...]

    def rotate(x):
        return x * cosine + pltpu.roll(x, HD // 2, 1) * sine

    def unrotate(x):
        return x * cosine - pltpu.roll(x, HD // 2, 1) * sine

    inv_rms = lax.rsqrt(squares[...] / width + epsilon)
    is_key = tp.core == 0
    sibling = tp.device(0, 0, 1)
    projected = pairs[...] * inv_rms
    own_pair[...] = jnp.where(is_key, rotate(projected), projected).astype(half)
    wire.put(own_pair, other_pair, sibling, "pair")
    heads = queries.shape[1] // HD
    for head in range(heads):
        lanes = pl.ds(head * HD, HD)
        queries_in[:, lanes] = rotate(queries[:, lanes] * inv_rms).astype(half)
    allowed = (seg_column[...] == seg_row[...]) & (
        lax.broadcasted_iota(jnp.int32, (rows, rows), 1)
        <= lax.broadcasted_iota(jnp.int32, (rows, rows), 0)
    )
    wire.got(other_pair, sibling, "pair")
    keys = jnp.where(is_key, own_pair[...], other_pair[...])
    values = jnp.where(is_key, other_pair[...], own_pair[...])
    scale = 1.0 / math.sqrt(HD)
    grad_keys = jnp.zeros((rows, HD), jnp.float32)
    grad_values = jnp.zeros((rows, HD), jnp.float32)
    along = jnp.zeros((rows, 1), jnp.float32)
    for head in range(heads):
        lanes = pl.ds(head * HD, HD)
        query, gradient = queries_in[:, lanes], grad_context[:, lanes]
        scores = jnp.where(allowed, dot(query, keys, BY_ROWS) * scale, -1e30)
        exponents = jnp.exp(scores - jnp.max(scores, axis=1, keepdims=True))
        attention = exponents / jnp.sum(exponents, axis=1, keepdims=True)
        attention_half = attention.astype(half)
        context[:, lanes] = dot(attention_half, values).astype(half)
        grad_probs = dot(gradient, values, BY_ROWS)
        centered = grad_probs - jnp.sum(grad_probs * attention, axis=1, keepdims=True)
        score_gradient = (attention * centered * scale).astype(half)
        grad_query = unrotate(dot(score_gradient, keys)).astype(half)
        grad_queries[:, lanes] = grad_query
        along = along + jnp.sum(wide(grad_query) * queries[:, lanes], axis=1, keepdims=True)
        grad_keys = grad_keys + dot(score_gradient, query, BY_COLUMNS)
        grad_values = grad_values + dot(attention_half, gradient, BY_COLUMNS)
    leaving_pair[...] = jnp.where(is_key, grad_values, grad_keys).astype(half)
    wire.put(leaving_pair, back_pair, sibling, "back")
    wire.got(back_pair, sibling, "back")
    summed = jnp.where(is_key, grad_keys, grad_values) + wide(back_pair[...])
    pair_gradient = jnp.where(is_key, unrotate(summed), summed).astype(half)
    grad_pairs[...] = pair_gradient
    along = along + jnp.sum(wide(pair_gradient) * pairs[...], axis=1, keepdims=True)
    inv = inv_rms[:, :1]
    pulled = inv * inv * inv * along / width
    for pull in pulls[:3]:
        pull.wait()

    def gradient_term(slot):
        here = pl.ds(pl.multiple_of(slot * columns, columns), columns)
        value = dot(grad_queries[...], q_in[here, :], BY_ROWS)
        value = value + dot(grad_pairs[...], kv_in[here, :], BY_ROWS)
        return (inv * (gain[:, here] * value) - wide(hidden_in[:, here]) * pulled).astype(half)

    def output_term(slot):
        here = pl.ds(pl.multiple_of(slot * columns, columns), columns)
        return dot(context[...], o_in[:, here]).astype(half)

    first, second = buffers[:6], buffers[6:]
    cut_first, cut_second = 128, 64
    mine_first = chunk_views(mine, rows, cut_first)
    mine_second = chunk_views(mine_out, rows, cut_second)

    def gradient_total(where, value):
        here = part_of(where, rows, cut_first)
        grad_hidden[here, :] = (wide(out_grad[here, :]) + value).astype(half)

    def output_total(where, value):
        here = part_of(where, rows, cut_second)
        layer_out[here, :] = (wide(hidden[here, :]) + value).astype(half)

    meeting = core_steps(tp, wire, gradient_term, mine, leaving, by_core, "gradient")
    advance(meeting)
    for count, (step, across) in enumerate(ORDER):
        advance(meeting)
        scatter_first(
            tp, wire, mine_first, first[0], first[1], cut_first, "gradient", step, across
        )
        advance(meeting)
    pulls[3].wait()
    run(core_steps(tp, wire, output_term, mine_out, leaving_out, by_core_out, "output"))
    scattering = scatter_steps(
        tp, wire, mine_first, gradient_total, first[4:], first[:4], "gradient"
    )
    advance(scattering)
    run(scattering)

    def pack_ready(step, across):
        here = pl.ds(pl.multiple_of(tok.index(step, across) * rows, rows), rows)
        value = dot(token_rows[here, :], every_grad[here, :], BY_COLUMNS)
        if (step, across) == (0, 0):
            stitch_grad[...] = value
        else:
            stitch_grad[...] += value

    cut_grad = 192
    gathering = gather_steps(
        tok, wire, shard_views(grad_hidden, rows, cut_grad), row_views(every_grad, rows, cut_grad),
        cut_grad, local, "every", pack_ready,
    )
    pulls[4].wait()
    advance(gathering)
    for step, across in ORDER:
        scatter_first(tp, wire, mine_second, second[0], second[1], cut_second, "output", step, across)
    scattering = scatter_steps(
        tp, wire, mine_second, output_total, second[4:], second[:4], "output"
    )
    advance(gathering)
    advance(gathering)
    advance(scattering)
    run(gathering)
    run(scattering)
    wire.drain()


def backward(
    queries, pairs, squares, grad_context, cosines, sines, seg_ids, gain, hidden, out_grad,
    hidden_all, token_rows, q_weight, kv_weight, o_weight,
):
    rows, columns = out_grad.shape
    tokens, features = token_rows.shape
    half = jnp.bfloat16
    chunks = pltpu.VMEM((4, 2, rows, columns), half)
    pair = pltpu.VMEM((rows, HD), half)
    wide_shape = pltpu.VMEM((rows, q_weight.shape[1]), half)
    return pl.pallas_call(
        backward_kernel,
        out_shape=(
            jax.ShapeDtypeStruct((rows, columns), half),
            jax.ShapeDtypeStruct((features, columns), jnp.float32),
        ),
        in_specs=[ON_CHIP] * 11 + [ANYWHERE] * 5,
        out_specs=(ON_CHIP, ON_CHIP),
        scratch_shapes=[
            pltpu.SemaphoreType.DMA((80,)),
            pltpu.SemaphoreType.DMA((80,)),
            pltpu.SemaphoreType.DMA((2,)),
            pltpu.SemaphoreType.DMA((5,)),
            pltpu.VMEM(q_weight.shape, half),
            pltpu.VMEM(kv_weight.shape, half),
            pltpu.VMEM(o_weight.shape, half),
            pltpu.VMEM(hidden_all.shape, half),
            pltpu.VMEM(token_rows.shape, half),
            pltpu.VMEM((tokens, columns), half),
            pltpu.VMEM((rows, columns), half),
            wide_shape, wide_shape, wide_shape, pair, pair, pair, pair, pair,
        ]
        + [chunks] * 6
        + scatter_buffers(rows, columns, 128)
        + scatter_buffers(rows, columns, 64),
        compiler_params=pltpu.CompilerParams(
            collective_id=2, has_side_effects=True, vmem_limit_bytes=60 << 20
        ),
        cost_estimate=pl.CostEstimate(flops=10 << 30, bytes_accessed=200 << 20, transcendentals=0),
        name="backward",
    )(
        queries, pairs, squares, grad_context, cosines, sines, seg_ids, seg_ids.reshape(rows, 1),
        gain.reshape(1, -1), hidden, out_grad, hidden_all, token_rows, q_weight, kv_weight,
        o_weight,
    )


def body(
    source, row_token, seg_ids, stitch_weight, norm_gain, q_weight, kv_weight, o_weight, out_grad
):
    seg_row = seg_ids[0]
    earlier = jnp.sum((seg_row[None, :] < seg_row[:, None]).astype(jnp.int32), axis=1)
    index_row = jnp.arange(seg_row.shape[0], dtype=jnp.int32)
    angles = (index_row - earlier).astype(jnp.float32)[:, None] * frequencies()[None, :]
    cosines, sines = jnp.cos(angles), jnp.sin(angles)
    cosines = jnp.concatenate([cosines, cosines], axis=1)
    sines = jnp.concatenate([-sines, sines], axis=1)
    token_rows, hidden_all, hidden, queries, pairs, squares, grad_context = forward(
        source, row_token, stitch_weight, norm_gain, q_weight, kv_weight, o_weight, out_grad
    )
    return backward(
        queries, pairs, squares, grad_context, cosines, sines, seg_ids, norm_gain, hidden,
        out_grad, hidden_all, token_rows, q_weight, kv_weight, o_weight,
    )


def solution(mesh):
    placed = (
        P("tp", "tok"),
        P(),
        P("tok", None),
        P("tok", "tp"),
        P(),
        P(None, "tp"),
        P(None, "tp"),
        P("tp", None),
        P("tok", "tp"),
    )
    return jax.shard_map(
        body,
        mesh=mesh,
        in_specs=placed,
        out_specs=(P("tok", "tp"), P("tok", "tp")),
        check_vma=False,
    )
```

```python
import math

import jax
import jax.numpy as jnp
import numpy as np
from jax import lax
from jax.experimental import pallas as pl
from jax.experimental.pallas import tpu as pltpu
from jax.sharding import PartitionSpec as P

HD = 128


epsilon = 1e-05


def frequencies():
    exponent = np.arange(0, HD, 2, dtype=np.float32) / np.float32(HD)
    plain_rate = np.power(np.float32(500000.0), -exponent)
    wavelength = np.float32(2.0 * math.pi) / plain_rate
    smoothing = (np.float32(8192.0) / wavelength - np.float32(1.0)) / np.float32(3.0)
    blended = (np.float32(1.0) - smoothing) * plain_rate / np.float32(8.0) + smoothing * plain_rate
    rate = np.where(
        wavelength < 2048.0,
        plain_rate,
        np.where(wavelength > 8192.0, plain_rate / np.float32(8.0), blended),
    )
    return np.concatenate([rate, rate]).astype(np.float32)


class Group:
    def __init__(self, axis):
        tok, tp = lax.axis_index("tok"), lax.axis_index("tp")
        self.axis, self.tok, self.tp = axis, tok, tp
        if axis == "tp":
            self.ring, self.pair, self.core = tp // 4, (tp // 2) % 2, tp % 2
        else:
            self.ring, self.pair, self.core = tok // 2, tok % 2, 0

    def index(self, step, across, sibling=0):
        ring = lax.rem(self.ring + step, 4)
        pair = 1 - self.pair if across else self.pair
        if self.axis == "tp":
            core = 1 - self.core if sibling else self.core
            return ring * 4 + pair * 2 + core
        return ring * 2 + pair

    def device(self, step, across, sibling=0):
        index = self.index(step, across, sibling)
        return (self.tok, index) if self.axis == "tp" else (index, self.tp)

    def peers(self):
        found = [self.device(step, 0) for step in (1, 2, 3)] + [self.device(0, 1)]
        return found + ([self.device(0, 0, 1)] if self.axis == "tp" else [])


class Wire:
    def __init__(self, send, recv):
        self.send, self.recv, self.slots, self.sent = send, recv, {}, []

    def slot(self, key):
        return self.recv.at[self.slots.setdefault(key, len(self.slots))]

    def put(self, src, dst, device, key):
        copy = pltpu.make_async_remote_copy(
            src_ref=src,
            dst_ref=dst,
            send_sem=self.send.at[len(self.sent)],
            recv_sem=self.slot(key),
            device_id=device,
            device_id_type=pl.DeviceIdType.MESH,
        )
        copy.start()
        self.sent.append(copy)

    def got(self, view, device, key):
        pltpu.make_async_remote_copy(
            src_ref=view,
            dst_ref=view,
            send_sem=self.send.at[0],
            recv_sem=self.slot(key),
            device_id=device,
            device_id_type=pl.DeviceIdType.MESH,
        ).wait_recv()

    def drain(self):
        for copy in self.sent:
            copy.wait_send()


def announce(*groups):
    barrier = pltpu.get_barrier_semaphore()
    peers = [peer for group in groups for peer in group.peers()]
    for peer in peers:
        pl.semaphore_signal(
            barrier, inc=1, device_id=peer, device_id_type=pl.DeviceIdType.MESH
        )
    return lambda: pl.semaphore_wait(barrier, len(peers))


def wide(value):
    return value.astype(jnp.float32)


def gather_steps(group, wire, shard, whole, cut, local, name, ready):
    two_cores = group.axis == "tp"

    def pass_on(step, across, half):
        if two_cores:
            view = whole(group.index(step, across), half)
            wire.put(view, view, group.device(0, 0, 1), (name, "core", step, across, half))

    def arrived(step, across, half):
        view = whole(group.index(step, across), half)
        wire.got(view, group.device(0, 1), (name, step, across, half))

    def complete(step, across):
        if two_cores:
            for half in (0, 1):
                view = whole(group.index(step, across, 1), half)
                wire.got(view, group.device(0, 0, 1), (name, "core", step, across, half))
        ready(step, across)

    own = group.index(0, 0)
    wire.put(shard(0), whole(own, 0), group.device(0, 1), (name, 0, 1, 0))

    def along(half):
        for step in (1, 3, 2):
            wire.put(
                shard(half), whole(own, half), group.device(step, 0), (name, 4 - step, 0, half)
            )

    along(1)
    along(0)
    wire.put(shard(1), whole(own, 1), group.device(0, 1), (name, 0, 1, 1))
    kept = [pltpu.make_async_copy(shard(half), whole(own, half), local.at[half]) for half in (0, 1)]
    for copy in kept:
        copy.start()
    if two_cores:
        for half in (0, 1):
            wire.put(
                shard(half), whole(own, half), group.device(0, 0, 1), (name, "core", 0, 0, half)
            )
    for copy in kept:
        copy.wait()
    yield
    complete(0, 0)
    arrived(0, 1, 0)
    view = whole(group.index(0, 1), 0)
    for step in (1, 3, 2):
        wire.put(view, view, group.device(step, 0), (name, 4 - step, 1, 0))
    pass_on(0, 1, 0)
    for step in (1, 3, 2):
        arrived(step, 0, 1)
        view = whole(group.index(step, 0), 1)
        wire.put(view, view, group.device(0, 1), (name, step, 1, 1))
        pass_on(step, 0, 1)
    yield
    for step in (1, 3, 2):
        arrived(step, 0, 0)
        pass_on(step, 0, 0)
    arrived(0, 1, 1)
    pass_on(0, 1, 1)
    yield
    for step in (1, 3, 2):
        complete(step, 0)
    complete(0, 1)
    yield
    for step in (1, 3, 2):
        for half in (0, 1):
            arrived(step, 1, half)
            pass_on(step, 1, half)
    yield
    for step in (1, 3, 2):
        complete(step, 1)


ORDER = [(step, 1) for step in (0, 1, 3, 2)] + [(step, 0) for step in (1, 3, 2, 0)]


def core_steps(group, wire, term, mine, leaving, by_core, name):
    for step, across in ORDER:
        leaving[step, across] = term(group.index(step, across, 1))
        wire.put(
            leaving.at[step, across],
            by_core.at[step, across],
            group.device(0, 0, 1),
            (name, "core", step, across),
        )
        mine[step, across] = term(group.index(step, across))
        yield
        wire.got(by_core.at[step, across], group.device(0, 0, 1), (name, "core", step, across))
        mine[step, across] = (wide(mine[step, across]) + wide(by_core[step, across])).astype(
            jnp.bfloat16
        )
        yield step, across


def scatter_first(group, wire, mine, by_pair, by_ring, cut, name, step, across):
    if across:
        wire.put(
            mine(step, 1, 0), by_pair.at[step], group.device(0, 1), (name, "pair", step)
        )
    if step:
        wire.put(
            mine(step, across, 1),
            by_ring.at[4 - step, across],
            group.device(step, 0),
            (name, "ring", 4 - step, across),
        )


def scatter_steps(group, wire, mine, finish, last, buffers, name):
    by_pair, by_ring, by_ring_last, by_pair_last = buffers
    going, going_last = last
    for step in (1, 3, 2, 0):
        wire.got(by_pair.at[step], group.device(0, 1), (name, "pair", step))
        total = wide(mine(step, 0, 0)[...]) + wide(by_pair[step])
        if step:
            going[step] = total.astype(jnp.bfloat16)
            wire.put(
                going.at[step], by_ring_last.at[4 - step], group.device(step, 0),
                (name, "last", 4 - step),
            )
        else:
            first_total = total
    for across in (1, 0):
        total = wide(mine(0, across, 1)[...])
        for step in (1, 3, 2):
            wire.got(by_ring.at[step, across], group.device(step, 0), (name, "ring", step, across))
            total = total + wide(by_ring[step, across])
        if across:
            going_last[...] = total.astype(jnp.bfloat16)
            wire.put(going_last, by_pair_last, group.device(0, 1), (name, "last"))
    yield
    wire.got(by_pair_last, group.device(0, 1), (name, "last"))
    finish(1, total + wide(by_pair_last[...]))
    for step in (1, 3, 2):
        wire.got(by_ring_last.at[step], group.device(step, 0), (name, "last", step))
        first_total = first_total + wide(by_ring_last[step])
    finish(0, first_total)


def scatter_buffers(rows, columns, cut):
    first, second, kind = cut, rows - cut, jnp.bfloat16
    return [
        pltpu.VMEM((4, first, columns), kind),
        pltpu.VMEM((4, 2, second, columns), kind),
        pltpu.VMEM((4, first, columns), kind),
        pltpu.VMEM((second, columns), kind),
        pltpu.VMEM((4, first, columns), kind),
        pltpu.VMEM((second, columns), kind),
    ]


def part_of(half, rows, cut):
    return pl.ds(cut, rows - cut) if half else pl.ds(0, cut)


def chunk_views(ref, rows, cut):
    return lambda step, across, half: ref.at[step, across, part_of(half, rows, cut)]


def column_views(ref, rows, columns, cut):
    def view(slot, half):
        return ref.at[
            part_of(half, rows, cut), pl.ds(pl.multiple_of(slot * columns, columns), columns)
        ]

    return view


def row_views(ref, rows, cut):
    def view(slot, half):
        start, size = (cut, rows - cut) if half else (0, cut)
        return ref.at[pl.ds(pl.multiple_of(slot * rows + start, 32), size)]

    return view


def shard_views(ref, rows, cut):
    return lambda half: ref.at[part_of(half, rows, cut)]


def run(steps):
    for _ in steps:
        pass


def advance(steps):
    return next(steps, None)


ANYWHERE = pl.BlockSpec(memory_space=pl.ANY)
ON_CHIP = pl.BlockSpec(memory_space=pltpu.VMEM)


def dot(a, b, over=((1,), (0,))):
    return lax.dot_general(a, b, (over, ((), ())), preferred_element_type=jnp.float32)


BY_ROWS = ((1,), (1,))
BY_COLUMNS = ((0,), (0,))


def forward_kernel(
    source, row_token, stitch, gain, q_hbm, kv_hbm, o_hbm, out_grad,
    token_out, hidden_out, hidden, queries, pairs, squares, grad_context,
    send, recv, local, loads,
    stitch_in, q_in, kv_in, o_in, rows_in, hidden_in, gradient_in,
    product, token_part, token_rows, total_context,
    *buffers,
):
    tp, tok, wire = Group("tp"), Group("tok"), Wire(send, recv)
    rows, columns = out_grad.shape
    source_rows = source.shape[0]
    tiles = token_part.shape[0] // rows
    pulls = [
        pltpu.make_async_copy(a, b, loads.at[i])
        for i, (a, b) in enumerate(
            ((stitch, stitch_in), (o_hbm, o_in), (q_hbm, q_in), (kv_hbm, kv_in))
        )
    ]
    met = announce(tp, tok)
    for pull in pulls:
        pull.start()
    met()
    pulls[0].wait()

    def placed(tile, taken, size=rows):
        index = lax.broadcasted_iota(jnp.int32, (size, taken.shape[1]), 0) + tile * size
        return jnp.where(index == taken, 1.0, 0.0).astype(jnp.bfloat16)

    def block_of(step, across):
        block = tp.index(step, across) // 2
        return pl.ds(pl.multiple_of(block * 2 * source_rows, 2 * source_rows), 2 * source_rows)

    def tile_of(tile, size=rows):
        return pl.ds(pl.multiple_of(tile * size, size), size)

    late = [(1, 1), (3, 1), (2, 1)]

    def source_ready(step, across):
        here = block_of(step, across)
        slot = late.index((step, across)) if (step, across) in late else 0
        product[slot] = dot(rows_in[here, :], stitch_in[...]).astype(jnp.bfloat16)
        if (step, across) in late:
            return

        @pl.loop(0, tiles // 4)
        def _(tile):
            there = tile_of(tile, 4 * rows)
            moved = dot(placed(tile, row_token[:, here], 4 * rows), product[0]).astype(
                jnp.bfloat16
            )
            if (step, across) == (0, 0):
                token_part[there, :] = moved
            else:
                token_part[there, :] = token_part[there, :] + moved

    def place_late(tile):
        total = wide(token_part[tile_of(tile), :])
        for slot, (step, across) in enumerate(late):
            total = total + dot(placed(tile, row_token[:, block_of(step, across)]), product[slot])
        token_part[tile_of(tile), :] = total.astype(jnp.bfloat16)

    def nothing(step, across):
        pass

    fetching = gather_steps(
        tp, wire, shard_views(source, source_rows, 64), row_views(rows_in, source_rows, 64),
        64, local.at[pl.ds(0, 2)], "source", source_ready,
    )
    gathering = gather_steps(
        tp, wire, shard_views(out_grad, rows, 192), column_views(gradient_in, rows, columns, 192),
        192, local.at[pl.ds(2, 2)], "gradient", nothing,
    )
    for _ in range(3):
        advance(fetching)
    advance(gathering)
    run(fetching)
    cut = 128
    going, buffers = buffers[4:], buffers[:4]

    def part(step, across, half):
        start, size = (cut, rows - cut) if half else (0, cut)
        return token_part.at[
            pl.ds(pl.multiple_of(tok.index(step, across) * rows + start, 32), size)
        ]

    def finish(half, value):
        hidden[part_of(half, rows, cut), :] = value.astype(hidden.dtype)

    for step, across in ORDER:
        place_late(tok.index(step, across))
        scatter_first(tok, wire, part, buffers[0], buffers[1], cut, "hidden", step, across)
    scattering = scatter_steps(tok, wire, part, finish, going, buffers, "hidden")

    def reorder(first, last):
        @pl.loop(first // 2, last // 2)
        def _(tile):
            token_rows[tile_of(tile, 2 * rows), :] = dot(
                placed(tile, row_token[...], 2 * rows), rows_in[...]
            ).astype(
                token_rows.dtype
            )

    reorder(0, tiles // 2)
    advance(scattering)
    advance(gathering)
    advance(scattering)
    def hidden_ready(step, across):
        if (step, across) == (0, 0):
            pulls[2].wait()
            pulls[3].wait()
        here = pl.ds(
            pl.multiple_of(tp.index(step, across) // 2 * 2 * columns, 2 * columns), 2 * columns
        )
        value = wide(hidden_in[:, here])
        scaled = (value * gain[:, here]).astype(jnp.bfloat16)
        to_queries = dot(scaled, q_in[here, :])
        to_pairs = dot(scaled, kv_in[here, :])
        squared = jnp.broadcast_to(
            jnp.sum(value * value, axis=1, keepdims=True), squares.shape
        )
        if (step, across) == (0, 0):
            queries[...], pairs[...], squares[...] = to_queries, to_pairs, squared
        else:
            queries[...] += to_queries
            pairs[...] += to_pairs
            squares[...] += squared

    collecting = gather_steps(
        tp, wire, shard_views(hidden, rows, 128), column_views(hidden_in, rows, columns, 128),
        128, local.at[pl.ds(4, 2)], "all", hidden_ready,
    )
    advance(collecting)
    run(gathering)
    reorder(tiles // 2, tiles * 3 // 4)
    advance(collecting)
    reorder(tiles * 3 // 4, tiles)
    tokens_out = pltpu.make_async_copy(token_rows, token_out, loads.at[4])
    tokens_out.start()
    advance(collecting)
    pulls[1].wait()
    advance(collecting)
    total_context[...] = jnp.zeros_like(total_context)

    @pl.loop(0, gradient_in.shape[1] // 1024)
    def _(block):
        here = pl.ds(pl.multiple_of(block * 1024, 1024), 1024)
        total_context[...] += dot(gradient_in[:, here], o_in[:, here], BY_ROWS)

    grad_context[...] = total_context[...].astype(grad_context.dtype)
    run(collecting)
    hidden_copy = pltpu.make_async_copy(hidden_in, hidden_out, loads.at[5])
    hidden_copy.start()
    tokens_out.wait()
    hidden_copy.wait()
    wire.drain()


def forward(source, row_token, stitch, gain, q_weight, kv_weight, o_weight, out_grad):
    rows, columns = out_grad.shape
    source_rows, features = source.shape
    tokens, width, heads = 16 * source_rows, 16 * columns, q_weight.shape[1]
    half = jnp.bfloat16
    return pl.pallas_call(
        forward_kernel,
        out_shape=(
            jax.ShapeDtypeStruct((tokens, features), half),
            jax.ShapeDtypeStruct((rows, width), half),
            jax.ShapeDtypeStruct((rows, columns), half),
            jax.ShapeDtypeStruct((rows, heads), jnp.float32),
            jax.ShapeDtypeStruct((rows, HD), jnp.float32),
            jax.ShapeDtypeStruct((rows, HD), jnp.float32),
            jax.ShapeDtypeStruct((rows, heads), half),
        ),
        in_specs=[ANYWHERE, ON_CHIP, ANYWHERE, ON_CHIP, ANYWHERE, ANYWHERE, ANYWHERE, ANYWHERE],
        out_specs=(ANYWHERE, ANYWHERE) + (ON_CHIP,) * 5,
        scratch_shapes=[
            pltpu.SemaphoreType.DMA((120,)),
            pltpu.SemaphoreType.DMA((120,)),
            pltpu.SemaphoreType.DMA((6,)),
            pltpu.SemaphoreType.DMA((6,)),
            pltpu.VMEM(stitch.shape, half),
            pltpu.VMEM(q_weight.shape, half),
            pltpu.VMEM(kv_weight.shape, half),
            pltpu.VMEM(o_weight.shape, half),
            pltpu.VMEM((tokens, features), half),
            pltpu.VMEM((rows, width), half),
            pltpu.VMEM((rows, width), half),
            pltpu.VMEM((3, 2 * source_rows, columns), half),
            pltpu.VMEM((tokens, columns), half),
            pltpu.VMEM((tokens, features), half),
            pltpu.VMEM((rows, heads), jnp.float32),
        ]
        + scatter_buffers(rows, columns, 128),
        compiler_params=pltpu.CompilerParams(
            collective_id=1, has_side_effects=True, vmem_limit_bytes=60 << 20
        ),
        cost_estimate=pl.CostEstimate(flops=30 << 30, bytes_accessed=200 << 20, transcendentals=0),
        name="forward",
    )(
        source, row_token.reshape(1, -1), stitch, gain.reshape(1, -1), q_weight, kv_weight,
        o_weight, out_grad,
    )


def backward_kernel(
    queries, pairs, squares, grad_context, rates, seg_row, gain,
    hidden, out_grad, hidden_hbm, token_hbm, q_hbm, kv_hbm, o_hbm,
    layer_out, stitch_grad,
    send, recv, local, loads,
    q_in, kv_in, o_in, hidden_in, token_rows, every_grad, grad_hidden,
    queries_in, context, grad_queries, grad_pairs, own_pair, other_pair, leaving_pair, back_pair,
    mine, leaving, by_core, mine_out, leaving_out, by_core_out,
    *buffers,
):
    tp, tok, wire = Group("tp"), Group("tok"), Wire(send, recv)
    rows, columns = out_grad.shape
    width = hidden_in.shape[1]
    half = jnp.bfloat16
    pulls = [
        pltpu.make_async_copy(a, b, loads.at[i])
        for i, (a, b) in enumerate(
            (
                (q_hbm, q_in), (kv_hbm, kv_in), (hidden_hbm, hidden_in), (o_hbm, o_in),
                (token_hbm, token_rows),
            )
        )
    ]
    met = announce(tp, tok)
    for pull in pulls:
        pull.start()
    segments = jnp.broadcast_to(seg_row[...].astype(jnp.float32), (rows, rows))
    own_segment = segments.T
    index = lax.broadcasted_iota(jnp.int32, (rows, rows), 0)
    allowed = (own_segment == segments) & (
        lax.broadcasted_iota(jnp.int32, (rows, rows), 1) <= index
    )
    earlier = jnp.sum(jnp.where(segments < own_segment, 1.0, 0.0), axis=1, keepdims=True)
    angles = (index[:, :HD].astype(jnp.float32) - earlier) * rates[...]
    cosine, sine = jnp.cos(angles), jnp.sin(angles)
    sine = jnp.where(
        lax.broadcasted_iota(jnp.int32, (rows, HD), 1) < HD // 2, -sine, sine
    )

    def rotate(x):
        return x * cosine + pltpu.roll(x, HD // 2, 1) * sine

    def unrotate(x):
        return x * cosine - pltpu.roll(x, HD // 2, 1) * sine

    inv_rms = lax.rsqrt(squares[...] / width + epsilon)
    is_key = tp.core == 0
    sibling = tp.device(0, 0, 1)
    projected = pairs[...] * inv_rms
    own_pair[...] = jnp.where(is_key, rotate(projected), projected).astype(half)
    heads = queries.shape[1] // HD
    met()
    wire.put(own_pair, other_pair, sibling, "pair")
    for head in range(heads):
        lanes = pl.ds(head * HD, HD)
        queries_in[:, lanes] = rotate(queries[:, lanes] * inv_rms).astype(half)
    wire.got(other_pair, sibling, "pair")
    keys = jnp.where(is_key, own_pair[...], other_pair[...])
    values = jnp.where(is_key, other_pair[...], own_pair[...])
    scale = 1.0 / math.sqrt(HD)
    grad_keys = jnp.zeros((rows, HD), jnp.float32)
    grad_values = jnp.zeros((rows, HD), jnp.float32)
    along = jnp.zeros((rows, 1), jnp.float32)
    for head in range(heads):
        lanes = pl.ds(head * HD, HD)
        query, gradient = queries_in[:, lanes], grad_context[:, lanes]
        scores = jnp.where(allowed, dot(query, keys, BY_ROWS) * scale, -1e30)
        exponents = jnp.exp(scores - jnp.max(scores, axis=1, keepdims=True))
        attention = exponents / jnp.sum(exponents, axis=1, keepdims=True)
        attention_half = attention.astype(half)
        context[:, lanes] = dot(attention_half, values).astype(half)
        grad_probs = dot(gradient, values, BY_ROWS)
        centered = grad_probs - jnp.sum(grad_probs * attention, axis=1, keepdims=True)
        score_gradient = (attention * centered * scale).astype(half)
        grad_query = unrotate(dot(score_gradient, keys)).astype(half)
        grad_queries[:, lanes] = grad_query
        along = along + jnp.sum(wide(grad_query) * queries[:, lanes], axis=1, keepdims=True)
        grad_keys = grad_keys + dot(score_gradient, query, BY_COLUMNS)
        grad_values = grad_values + dot(attention_half, gradient, BY_COLUMNS)
    leaving_pair[...] = jnp.where(is_key, grad_values, grad_keys).astype(half)
    wire.put(leaving_pair, back_pair, sibling, "back")
    wire.got(back_pair, sibling, "back")
    summed = jnp.where(is_key, grad_keys, grad_values) + wide(back_pair[...])
    pair_gradient = jnp.where(is_key, unrotate(summed), summed).astype(half)
    grad_pairs[...] = pair_gradient
    along = along + jnp.sum(wide(pair_gradient) * pairs[...], axis=1, keepdims=True)
    inv = inv_rms[:, :1]
    pulled = inv * inv * inv * along / width
    for pull in pulls[:3]:
        pull.wait()

    def gradient_term(slot):
        here = pl.ds(pl.multiple_of(slot * columns, columns), columns)
        value = dot(grad_queries[...], q_in[here, :], BY_ROWS)
        value = value + dot(grad_pairs[...], kv_in[here, :], BY_ROWS)
        return (inv * (gain[:, here] * value) - wide(hidden_in[:, here]) * pulled).astype(half)

    def output_term(slot):
        here = pl.ds(pl.multiple_of(slot * columns, columns), columns)
        return dot(context[...], o_in[:, here]).astype(half)

    first, second = buffers[:6], buffers[6:]
    cut_first, cut_second = 128, 64
    mine_first = chunk_views(mine, rows, cut_first)
    mine_second = chunk_views(mine_out, rows, cut_second)

    def gradient_total(where, value):
        here = part_of(where, rows, cut_first)
        grad_hidden[here, :] = (wide(out_grad[here, :]) + value).astype(half)

    def output_total(where, value):
        here = part_of(where, rows, cut_second)
        layer_out[here, :] = (wide(hidden[here, :]) + value).astype(half)

    meeting = core_steps(tp, wire, gradient_term, mine, leaving, by_core, "gradient")
    advance(meeting)
    for count, (step, across) in enumerate(ORDER):
        advance(meeting)
        scatter_first(
            tp, wire, mine_first, first[0], first[1], cut_first, "gradient", step, across
        )
        advance(meeting)
    pulls[3].wait()
    run(core_steps(tp, wire, output_term, mine_out, leaving_out, by_core_out, "output"))
    scattering = scatter_steps(
        tp, wire, mine_first, gradient_total, first[4:], first[:4], "gradient"
    )
    advance(scattering)
    run(scattering)

    def pack_ready(step, across):
        here = pl.ds(pl.multiple_of(tok.index(step, across) * rows, rows), rows)
        value = dot(token_rows[here, :], every_grad[here, :], BY_COLUMNS)
        if (step, across) == (0, 0):
            stitch_grad[...] = value
        else:
            stitch_grad[...] += value

    cut_grad = 192
    gathering = gather_steps(
        tok, wire, shard_views(grad_hidden, rows, cut_grad), row_views(every_grad, rows, cut_grad),
        cut_grad, local, "every", pack_ready,
    )
    pulls[4].wait()
    advance(gathering)
    for step, across in ORDER:
        scatter_first(tp, wire, mine_second, second[0], second[1], cut_second, "output", step, across)
    scattering = scatter_steps(
        tp, wire, mine_second, output_total, second[4:], second[:4], "output"
    )
    advance(gathering)
    advance(gathering)
    advance(scattering)
    run(gathering)
    run(scattering)
    wire.drain()


def backward(
    queries, pairs, squares, grad_context, seg_ids, gain, hidden, out_grad,
    hidden_all, token_rows, q_weight, kv_weight, o_weight,
):
    rows, columns = out_grad.shape
    tokens, features = token_rows.shape
    half = jnp.bfloat16
    chunks = pltpu.VMEM((4, 2, rows, columns), half)
    pair = pltpu.VMEM((rows, HD), half)
    wide_shape = pltpu.VMEM((rows, q_weight.shape[1]), half)
    return pl.pallas_call(
        backward_kernel,
        out_shape=(
            jax.ShapeDtypeStruct((rows, columns), half),
            jax.ShapeDtypeStruct((features, columns), jnp.float32),
        ),
        in_specs=[ON_CHIP] * 9 + [ANYWHERE] * 5,
        out_specs=(ON_CHIP, ON_CHIP),
        scratch_shapes=[
            pltpu.SemaphoreType.DMA((80,)),
            pltpu.SemaphoreType.DMA((80,)),
            pltpu.SemaphoreType.DMA((2,)),
            pltpu.SemaphoreType.DMA((5,)),
            pltpu.VMEM(q_weight.shape, half),
            pltpu.VMEM(kv_weight.shape, half),
            pltpu.VMEM(o_weight.shape, half),
            pltpu.VMEM(hidden_all.shape, half),
            pltpu.VMEM(token_rows.shape, half),
            pltpu.VMEM((tokens, columns), half),
            pltpu.VMEM((rows, columns), half),
            wide_shape, wide_shape, wide_shape, pair, pair, pair, pair, pair,
        ]
        + [chunks] * 6
        + scatter_buffers(rows, columns, 128)
        + scatter_buffers(rows, columns, 64),
        compiler_params=pltpu.CompilerParams(
            collective_id=2, has_side_effects=True, vmem_limit_bytes=60 << 20
        ),
        cost_estimate=pl.CostEstimate(flops=10 << 30, bytes_accessed=200 << 20, transcendentals=0),
        name="backward",
    )(
        queries, pairs, squares, grad_context, jnp.asarray(frequencies())[None], seg_ids,
        gain.reshape(1, -1), hidden, out_grad, hidden_all, token_rows, q_weight, kv_weight,
        o_weight,
    )


def body(
    source, row_token, seg_ids, stitch_weight, norm_gain, q_weight, kv_weight, o_weight, out_grad
):
    token_rows, hidden_all, hidden, queries, pairs, squares, grad_context = forward(
        source, row_token, stitch_weight, norm_gain, q_weight, kv_weight, o_weight, out_grad
    )
    return backward(
        queries, pairs, squares, grad_context, seg_ids, norm_gain, hidden,
        out_grad, hidden_all, token_rows, q_weight, kv_weight, o_weight,
    )


def solution(mesh):
    placed = (
        P("tp", "tok"),
        P(),
        P("tok", None),
        P("tok", "tp"),
        P(),
        P(None, "tp"),
        P(None, "tp"),
        P("tp", None),
        P("tok", "tp"),
    )
    return jax.shard_map(
        body,
        mesh=mesh,
        in_specs=placed,
        out_specs=(P("tok", "tp"), P("tok", "tp")),
        check_vma=False,
    )
```

```python
import math

import jax
import jax.numpy as jnp
import numpy as np
from jax import lax
from jax.experimental import pallas as pl
from jax.experimental.pallas import tpu as pltpu
from jax.sharding import PartitionSpec as P

HD = 128


epsilon = 1e-05


def frequencies():
    exponent = np.arange(0, HD, 2, dtype=np.float32) / np.float32(HD)
    plain_rate = np.power(np.float32(500000.0), -exponent)
    wavelength = np.float32(2.0 * math.pi) / plain_rate
    smoothing = (np.float32(8192.0) / wavelength - np.float32(1.0)) / np.float32(3.0)
    blended = (np.float32(1.0) - smoothing) * plain_rate / np.float32(8.0) + smoothing * plain_rate
    rate = np.where(
        wavelength < 2048.0,
        plain_rate,
        np.where(wavelength > 8192.0, plain_rate / np.float32(8.0), blended),
    )
    return np.concatenate([rate, rate]).astype(np.float32)


class Group:
    def __init__(self, axis):
        tok, tp = lax.axis_index("tok"), lax.axis_index("tp")
        self.axis, self.tok, self.tp = axis, tok, tp
        if axis == "tp":
            self.ring, self.pair, self.core = tp // 4, (tp // 2) % 2, tp % 2
        else:
            self.ring, self.pair, self.core = tok // 2, tok % 2, 0

    def index(self, step, across, sibling=0):
        ring = lax.rem(self.ring + step, 4)
        pair = 1 - self.pair if across else self.pair
        if self.axis == "tp":
            core = 1 - self.core if sibling else self.core
            return ring * 4 + pair * 2 + core
        return ring * 2 + pair

    def device(self, step, across, sibling=0):
        index = self.index(step, across, sibling)
        return (self.tok, index) if self.axis == "tp" else (index, self.tp)

    def peers(self):
        found = [self.device(step, 0) for step in (1, 2, 3)] + [self.device(0, 1)]
        return found + ([self.device(0, 0, 1)] if self.axis == "tp" else [])


class Wire:
    def __init__(self, send, recv):
        self.send, self.recv, self.slots, self.sent, self.waited = send, recv, {}, [], 0

    def slot(self, key):
        return self.recv.at[self.slots.setdefault(key, len(self.slots))]

    def put(self, src, dst, device, key):
        copy = pltpu.make_async_remote_copy(
            src_ref=src,
            dst_ref=dst,
            send_sem=self.send.at[len(self.sent)],
            recv_sem=self.slot(key),
            device_id=device,
            device_id_type=pl.DeviceIdType.MESH,
        )
        copy.start()
        self.sent.append(copy)

    def got(self, view, device, key):
        pltpu.make_async_remote_copy(
            src_ref=view,
            dst_ref=view,
            send_sem=self.send.at[0],
            recv_sem=self.slot(key),
            device_id=device,
            device_id_type=pl.DeviceIdType.MESH,
        ).wait_recv()

    def drain(self):
        for copy in self.sent[self.waited :]:
            copy.wait_send()
        self.waited = len(self.sent)


def announce(*groups):
    barrier = pltpu.get_barrier_semaphore()
    peers = [peer for group in groups for peer in group.peers()]
    for peer in peers:
        pl.semaphore_signal(
            barrier, inc=1, device_id=peer, device_id_type=pl.DeviceIdType.MESH
        )
    return lambda: pl.semaphore_wait(barrier, len(peers))


def wide(value):
    return value.astype(jnp.float32)


def gather_steps(group, wire, shard, whole, cut, local, name, ready):
    two_cores = group.axis == "tp"

    def pass_on(step, across, half):
        if two_cores:
            view = whole(group.index(step, across), half)
            wire.put(view, view, group.device(0, 0, 1), (name, "core", step, across, half))

    def arrived(step, across, half):
        view = whole(group.index(step, across), half)
        wire.got(view, group.device(0, 1), (name, step, across, half))

    def complete(step, across):
        if two_cores:
            for half in (0, 1):
                view = whole(group.index(step, across, 1), half)
                wire.got(view, group.device(0, 0, 1), (name, "core", step, across, half))
        ready(step, across)

    own = group.index(0, 0)
    wire.put(shard(0), whole(own, 0), group.device(0, 1), (name, 0, 1, 0))

    def along(half):
        for step in (1, 3, 2):
            wire.put(
                shard(half), whole(own, half), group.device(step, 0), (name, 4 - step, 0, half)
            )

    along(1)
    along(0)
    wire.put(shard(1), whole(own, 1), group.device(0, 1), (name, 0, 1, 1))
    kept = [pltpu.make_async_copy(shard(half), whole(own, half), local.at[half]) for half in (0, 1)]
    for copy in kept:
        copy.start()
    if two_cores:
        for half in (0, 1):
            wire.put(
                shard(half), whole(own, half), group.device(0, 0, 1), (name, "core", 0, 0, half)
            )
    for copy in kept:
        copy.wait()
    yield
    complete(0, 0)
    arrived(0, 1, 0)
    view = whole(group.index(0, 1), 0)
    for step in (1, 3, 2):
        wire.put(view, view, group.device(step, 0), (name, 4 - step, 1, 0))
    pass_on(0, 1, 0)
    for step in (1, 3, 2):
        arrived(step, 0, 1)
        view = whole(group.index(step, 0), 1)
        wire.put(view, view, group.device(0, 1), (name, step, 1, 1))
        pass_on(step, 0, 1)
    yield
    for step in (1, 3, 2):
        arrived(step, 0, 0)
        pass_on(step, 0, 0)
    arrived(0, 1, 1)
    pass_on(0, 1, 1)
    yield
    for step in (1, 3, 2):
        complete(step, 0)
    complete(0, 1)
    yield
    for step in (1, 3, 2):
        for half in (0, 1):
            arrived(step, 1, half)
            pass_on(step, 1, half)
    yield
    for step in (1, 3, 2):
        complete(step, 1)


ORDER = [(step, 1) for step in (0, 1, 3, 2)] + [(step, 0) for step in (1, 3, 2, 0)]


def core_steps(group, wire, term, mine, leaving, by_core, name):
    for step, across in ORDER:
        going, kept = leaving(step, across), mine(step, across)
        going[...] = term(group.index(step, across, 1))
        wire.put(
            going, by_core.at[step, across], group.device(0, 0, 1), (name, "core", step, across)
        )
        kept[...] = term(group.index(step, across))
        yield
        wire.got(by_core.at[step, across], group.device(0, 0, 1), (name, "core", step, across))
        kept[...] = (wide(kept[...]) + wide(by_core[step, across])).astype(jnp.bfloat16)
        yield step, across


def scatter_first(group, wire, mine, by_pair, by_ring, cut, name, step, across):
    if across:
        wire.put(
            mine(step, 1, 0), by_pair.at[step], group.device(0, 1), (name, "pair", step)
        )
    if step:
        wire.put(
            mine(step, across, 1),
            by_ring.at[4 - step, across],
            group.device(step, 0),
            (name, "ring", 4 - step, across),
        )


def scatter_steps(group, wire, mine, finish, last, buffers, name):
    by_pair, by_ring, by_ring_last, by_pair_last = buffers
    going, going_last = last
    for step in (1, 3, 2, 0):
        wire.got(by_pair.at[step], group.device(0, 1), (name, "pair", step))
        total = wide(mine(step, 0, 0)[...]) + wide(by_pair[step])
        if step:
            going[step] = total.astype(jnp.bfloat16)
            wire.put(
                going.at[step], by_ring_last.at[4 - step], group.device(step, 0),
                (name, "last", 4 - step),
            )
        else:
            first_total = total
    for across in (1, 0):
        total = wide(mine(0, across, 1)[...])
        for step in (1, 3, 2):
            wire.got(by_ring.at[step, across], group.device(step, 0), (name, "ring", step, across))
            total = total + wide(by_ring[step, across])
        if across:
            going_last[...] = total.astype(jnp.bfloat16)
            wire.put(going_last, by_pair_last, group.device(0, 1), (name, "last"))
    yield
    wire.got(by_pair_last, group.device(0, 1), (name, "last"))
    finish(1, total + wide(by_pair_last[...]))
    for step in (1, 3, 2):
        wire.got(by_ring_last.at[step], group.device(step, 0), (name, "last", step))
        first_total = first_total + wide(by_ring_last[step])
    finish(0, first_total)


def scatter_buffers(rows, columns, cut):
    first, second, kind = cut, rows - cut, jnp.bfloat16
    return [
        pltpu.VMEM((4, first, columns), kind),
        pltpu.VMEM((4, 2, second, columns), kind),
        pltpu.VMEM((4, first, columns), kind),
        pltpu.VMEM((second, columns), kind),
        pltpu.VMEM((4, first, columns), kind),
        pltpu.VMEM((second, columns), kind),
    ]


def part_of(half, rows, cut):
    return pl.ds(cut, rows - cut) if half else pl.ds(0, cut)


def chunks_in_rows(ref, rows, columns, side):
    def view(step, across, half=None, cut=0):
        start, size = (0, rows) if half is None else (cut, rows - cut) if half else (0, cut)
        return ref.at[pl.ds((step * 2 + across) * rows + start, size), pl.ds(side * columns, columns)]

    return view


def chunks_in_columns(ref, rows, columns, side):
    def view(step, across, half=None, cut=0):
        part = pl.ds(0, rows) if half is None else part_of(half, rows, cut)
        return ref.at[part, pl.ds((side * 8 + step * 2 + across) * columns, columns)]

    return view


def column_views(ref, rows, columns, cut):
    def view(slot, half):
        return ref.at[
            part_of(half, rows, cut), pl.ds(pl.multiple_of(slot * columns, columns), columns)
        ]

    return view


def row_views(ref, rows, cut):
    def view(slot, half):
        start, size = (cut, rows - cut) if half else (0, cut)
        return ref.at[pl.ds(pl.multiple_of(slot * rows + start, 32), size)]

    return view


def shard_views(ref, rows, cut):
    return lambda half: ref.at[part_of(half, rows, cut)]


def run(steps):
    for _ in steps:
        pass


def advance(steps):
    return next(steps, None)


ANYWHERE = pl.BlockSpec(memory_space=pl.ANY)
ON_CHIP = pl.BlockSpec(memory_space=pltpu.VMEM)


def dot(a, b, over=((1,), (0,))):
    return lax.dot_general(a, b, (over, ((), ())), preferred_element_type=jnp.float32)


BY_ROWS = ((1,), (1,))
BY_COLUMNS = ((0,), (0,))


def step_kernel(
    source, row_token, seg_row, rates, stitch, gain, q_hbm, kv_hbm, o_hbm, out_grad,
    layer_out, stitch_grad,
    send, recv, local, loads,
    stitch_in, q_in, kv_in, o_in, rows_in, hidden_in, gradient_in,
    token_part, token_rows, hidden, queries, pairs, squares, grad_context,
    cosines, sines, every_grad, grad_hidden,
    queries_in, context, grad_queries, grad_pairs, own_pair, other_pair, leaving_pair, back_pair,
    by_core, by_core_out,
    *buffers,
):
    tp, tok, wire = Group("tp"), Group("tok"), Wire(send, recv)
    rows, columns = out_grad.shape
    source_rows = source.shape[0]
    tiles = token_part.shape[0] // rows
    pulls = [
        pltpu.make_async_copy(a, b, loads.at[i])
        for i, (a, b) in enumerate(
            ((stitch, stitch_in), (o_hbm, o_in), (q_hbm, q_in), (kv_hbm, kv_in), (out_grad, grad_hidden))
        )
    ]
    met = announce(tp, tok)
    for pull in pulls:
        pull.start()
    width, half = hidden_in.shape[1], jnp.bfloat16
    segments = jnp.broadcast_to(seg_row[...].astype(jnp.float32), (rows, rows))
    own_segment = segments.T
    index = lax.broadcasted_iota(jnp.int32, (rows, rows), 0)
    earlier = jnp.sum(jnp.where(segments < own_segment, 1.0, 0.0), axis=1, keepdims=True)
    angles = (index[:, :HD].astype(jnp.float32) - earlier) * rates[...]
    cosines[...] = jnp.cos(angles)
    sine = jnp.sin(angles)
    sines[...] = jnp.where(
        lax.broadcasted_iota(jnp.int32, (rows, HD), 1) < HD // 2, -sine, sine
    )
    met()
    pulls[0].wait()

    def placed(tile, taken, size=rows):
        index = lax.broadcasted_iota(jnp.int32, (size, taken.shape[1]), 0) + tile * size
        return jnp.where(index == taken, 1.0, 0.0).astype(jnp.bfloat16)

    def block_of(step, across):
        block = tp.index(step, across) // 2
        return pl.ds(pl.multiple_of(block * 2 * source_rows, 2 * source_rows), 2 * source_rows)

    def tile_of(tile, size=rows):
        return pl.ds(pl.multiple_of(tile * size, size), size)

    late = [(1, 1), (3, 1), (2, 1)]
    product = [queries_in, context, grad_queries]
    total_context = stitch_grad.at[pl.ds(0, rows)]

    def source_ready(step, across):
        here = block_of(step, across)
        slot = late.index((step, across)) if (step, across) in late else 0
        product[slot][...] = dot(rows_in[here, :], stitch_in[...]).astype(jnp.bfloat16)
        if (step, across) in late:
            return

        @pl.loop(0, tiles // 4)
        def _(tile):
            there = tile_of(tile, 4 * rows)
            moved = dot(placed(tile, row_token[:, here], 4 * rows), product[0][...]).astype(
                jnp.bfloat16
            )
            if (step, across) == (0, 0):
                token_part[there, :] = moved
            else:
                token_part[there, :] = token_part[there, :] + moved

    def place_late(tile):
        total = wide(token_part[tile_of(tile), :])
        for slot, (step, across) in enumerate(late):
            total = total + dot(placed(tile, row_token[:, block_of(step, across)]), product[slot][...])
        token_part[tile_of(tile), :] = total.astype(jnp.bfloat16)

    def nothing(step, across):
        pass

    fetching = gather_steps(
        tp, wire, shard_views(source, source_rows, 64), row_views(rows_in, source_rows, 64),
        64, local.at[pl.ds(0, 2)], "source", source_ready,
    )
    gathering = gather_steps(
        tp, wire, shard_views(out_grad, rows, 192), column_views(gradient_in, rows, columns, 192),
        192, local.at[pl.ds(2, 2)], "gradient", nothing,
    )
    for _ in range(3):
        advance(fetching)
    advance(gathering)
    run(fetching)
    cut = 128
    later, going, buffers = buffers[6:], buffers[4:6], buffers[:4]

    def part(step, across, half):
        start, size = (cut, rows - cut) if half else (0, cut)
        return token_part.at[
            pl.ds(pl.multiple_of(tok.index(step, across) * rows + start, 32), size)
        ]

    def finish(half, value):
        hidden[part_of(half, rows, cut), :] = value.astype(hidden.dtype)

    for step, across in ORDER:
        place_late(tok.index(step, across))
        scatter_first(tok, wire, part, buffers[0], buffers[1], cut, "hidden", step, across)
    scattering = scatter_steps(tok, wire, part, finish, going, buffers, "hidden")

    def reorder(first, last):
        @pl.loop(first // 2, last // 2)
        def _(tile):
            token_rows[tile_of(tile, 2 * rows), :] = dot(
                placed(tile, row_token[...], 2 * rows), rows_in[...]
            ).astype(
                token_rows.dtype
            )

    reorder(0, tiles // 2)
    advance(scattering)
    advance(gathering)
    advance(scattering)
    def hidden_ready(step, across):
        if (step, across) == (0, 0):
            pulls[2].wait()
            pulls[3].wait()
            pulls[4].wait()
        here = pl.ds(
            pl.multiple_of(tp.index(step, across) // 2 * 2 * columns, 2 * columns), 2 * columns
        )
        value = wide(hidden_in[:, here])
        scaled = (value * gain[:, here]).astype(jnp.bfloat16)
        to_queries = dot(scaled, q_in[here, :])
        to_pairs = dot(scaled, kv_in[here, :])
        squared = jnp.broadcast_to(
            jnp.sum(value * value, axis=1, keepdims=True), squares.shape
        )
        if (step, across) == (0, 0):
            queries[...], pairs[...], squares[...] = to_queries, to_pairs, squared
        else:
            queries[...] += to_queries
            pairs[...] += to_pairs
            squares[...] += squared

    collecting = gather_steps(
        tp, wire, shard_views(hidden, rows, 128), column_views(hidden_in, rows, columns, 128),
        128, local.at[pl.ds(4, 2)], "all", hidden_ready,
    )
    advance(collecting)
    run(gathering)
    reorder(tiles // 2, tiles * 3 // 4)
    advance(collecting)
    reorder(tiles * 3 // 4, tiles)
    advance(collecting)
    pulls[1].wait()
    advance(collecting)
    total_context[...] = jnp.zeros_like(total_context)

    @pl.loop(0, gradient_in.shape[1] // 1024)
    def _(block):
        here = pl.ds(pl.multiple_of(block * 1024, 1024), 1024)
        total_context[...] += dot(gradient_in[:, here], o_in[:, here], BY_ROWS)

    grad_context[...] = total_context[...].astype(grad_context.dtype)
    run(collecting)
    wire.drain()

    cosine, sine = cosines[...], sines[...]
    segments = jnp.broadcast_to(seg_row[...].astype(jnp.float32), (rows, rows))
    allowed = (segments.T == segments) & (
        lax.broadcasted_iota(jnp.int32, (rows, rows), 1)
        <= lax.broadcasted_iota(jnp.int32, (rows, rows), 0)
    )

    def rotate(x):
        return x * cosine + pltpu.roll(x, HD // 2, 1) * sine

    def unrotate(x):
        return x * cosine - pltpu.roll(x, HD // 2, 1) * sine

    inv_rms = lax.rsqrt(squares[...] / width + epsilon)
    is_key = tp.core == 0
    sibling = tp.device(0, 0, 1)
    projected = pairs[...] * inv_rms
    own_pair[...] = jnp.where(is_key, rotate(projected), projected).astype(half)
    heads = queries.shape[1] // HD
    wire.put(own_pair, other_pair, sibling, "pair")
    for head in range(heads):
        lanes = pl.ds(head * HD, HD)
        queries_in[:, lanes] = rotate(queries[:, lanes] * inv_rms).astype(half)
    wire.got(other_pair, sibling, "pair")
    keys = jnp.where(is_key, own_pair[...], other_pair[...])
    values = jnp.where(is_key, other_pair[...], own_pair[...])
    scale = 1.0 / math.sqrt(HD)
    grad_keys = jnp.zeros((rows, HD), jnp.float32)
    grad_values = jnp.zeros((rows, HD), jnp.float32)
    along = jnp.zeros((rows, 1), jnp.float32)
    for head in range(heads):
        lanes = pl.ds(head * HD, HD)
        query, gradient = queries_in[:, lanes], grad_context[:, lanes]
        scores = jnp.where(allowed, dot(query, keys, BY_ROWS) * scale, -1e30)
        exponents = jnp.exp(scores - jnp.max(scores, axis=1, keepdims=True))
        attention = exponents / jnp.sum(exponents, axis=1, keepdims=True)
        attention_half = attention.astype(half)
        context[:, lanes] = dot(attention_half, values).astype(half)
        grad_probs = dot(gradient, values, BY_ROWS)
        centered = grad_probs - jnp.sum(grad_probs * attention, axis=1, keepdims=True)
        score_gradient = (attention * centered * scale).astype(half)
        grad_query = unrotate(dot(score_gradient, keys)).astype(half)
        grad_queries[:, lanes] = grad_query
        along = along + jnp.sum(wide(grad_query) * queries[:, lanes], axis=1, keepdims=True)
        grad_keys = grad_keys + dot(score_gradient, query, BY_COLUMNS)
        grad_values = grad_values + dot(attention_half, gradient, BY_COLUMNS)
    leaving_pair[...] = jnp.where(is_key, grad_values, grad_keys).astype(half)
    wire.put(leaving_pair, back_pair, sibling, "back")
    wire.got(back_pair, sibling, "back")
    summed = jnp.where(is_key, grad_keys, grad_values) + wide(back_pair[...])
    pair_gradient = jnp.where(is_key, unrotate(summed), summed).astype(half)
    grad_pairs[...] = pair_gradient
    along = along + jnp.sum(wide(pair_gradient) * pairs[...], axis=1, keepdims=True)
    inv = inv_rms[:, :1]
    pulled = inv * inv * inv * along / width

    def gradient_term(slot):
        here = pl.ds(pl.multiple_of(slot * columns, columns), columns)
        value = dot(grad_queries[...], q_in[here, :], BY_ROWS)
        value = value + dot(grad_pairs[...], kv_in[here, :], BY_ROWS)
        return (inv * (gain[:, here] * value) - wide(hidden_in[:, here]) * pulled).astype(half)

    def output_term(slot):
        here = pl.ds(pl.multiple_of(slot * columns, columns), columns)
        return dot(context[...], o_in[:, here]).astype(half)

    first, second = later[:6], later[6:]
    cut_first, cut_second = 128, 64
    mine, leaving = (chunks_in_rows(rows_in, rows, columns, side) for side in (0, 1))
    mine_out, leaving_out = (
        chunks_in_columns(gradient_in, rows, columns, side) for side in (0, 1)
    )

    def mine_first(step, across, half):
        return mine(step, across, half, cut_first)

    def mine_second(step, across, half):
        return mine_out(step, across, half, cut_second)


    def gradient_total(where, value):
        here = part_of(where, rows, cut_first)
        grad_hidden[here, :] = (wide(grad_hidden[here, :]) + value).astype(half)

    def output_total(where, value):
        here = part_of(where, rows, cut_second)
        layer_out[here, :] = (wide(hidden[here, :]) + value).astype(half)

    meeting = core_steps(tp, wire, gradient_term, mine, leaving, by_core, "gradient")
    advance(meeting)
    for count, (step, across) in enumerate(ORDER):
        advance(meeting)
        scatter_first(
            tp, wire, mine_first, first[0], first[1], cut_first, "gradient", step, across
        )
        advance(meeting)
    run(core_steps(tp, wire, output_term, mine_out, leaving_out, by_core_out, "output"))
    scattering = scatter_steps(
        tp, wire, mine_first, gradient_total, first[4:], first[:4], "gradient"
    )
    advance(scattering)
    run(scattering)

    def pack_ready(step, across):
        here = pl.ds(pl.multiple_of(tok.index(step, across) * rows, rows), rows)
        value = dot(token_rows[here, :], every_grad[here, :], BY_COLUMNS)
        if (step, across) == (0, 0):
            stitch_grad[...] = value
        else:
            stitch_grad[...] += value

    cut_grad = 192
    gathering = gather_steps(
        tok, wire, shard_views(grad_hidden, rows, cut_grad), row_views(every_grad, rows, cut_grad),
        cut_grad, local.at[pl.ds(6, 2)], "every", pack_ready,
    )
    advance(gathering)
    for step, across in ORDER:
        scatter_first(tp, wire, mine_second, second[0], second[1], cut_second, "output", step, across)
    scattering = scatter_steps(
        tp, wire, mine_second, output_total, second[4:], second[:4], "output"
    )
    advance(gathering)
    advance(gathering)
    advance(scattering)
    run(gathering)
    run(scattering)
    wire.drain()


def body(
    source, row_token, seg_ids, stitch_weight, norm_gain, q_weight, kv_weight, o_weight, out_grad
):
    rows, columns = out_grad.shape
    source_rows, features = source.shape
    tokens, width, heads = 16 * source_rows, 16 * columns, q_weight.shape[1]
    kind = jnp.bfloat16

    def on_chip(*shape, dtype=kind):
        return pltpu.VMEM(shape, dtype)

    return pl.pallas_call(
        step_kernel,
        out_shape=(
            jax.ShapeDtypeStruct((rows, columns), kind),
            jax.ShapeDtypeStruct((features, columns), jnp.float32),
        ),
        in_specs=[ANYWHERE] + [ON_CHIP] * 3 + [ANYWHERE, ON_CHIP] + [ANYWHERE] * 4,
        out_specs=(ON_CHIP, ON_CHIP),
        scratch_shapes=[
            pltpu.SemaphoreType.DMA((200,)),
            pltpu.SemaphoreType.DMA((200,)),
            pltpu.SemaphoreType.DMA((8,)),
            pltpu.SemaphoreType.DMA((5,)),
            on_chip(*stitch_weight.shape),
            on_chip(*q_weight.shape),
            on_chip(*kv_weight.shape),
            on_chip(*o_weight.shape),
            on_chip(tokens, features),
            on_chip(rows, width),
            on_chip(rows, width),
            on_chip(tokens, columns),
            on_chip(tokens, features),
            on_chip(rows, columns),
            on_chip(rows, heads, dtype=jnp.float32),
            on_chip(rows, HD, dtype=jnp.float32),
            on_chip(rows, HD, dtype=jnp.float32),
            on_chip(rows, heads),
            on_chip(rows, HD, dtype=jnp.float32),
            on_chip(rows, HD, dtype=jnp.float32),
            on_chip(tokens, columns),
            on_chip(rows, columns),
        ]
        + [on_chip(rows, heads)] * 3
        + [on_chip(rows, HD)] * 5
        + [on_chip(4, 2, rows, columns)] * 2
        + scatter_buffers(rows, columns, 128)
        + scatter_buffers(rows, columns, 128)
        + scatter_buffers(rows, columns, 64),
        compiler_params=pltpu.CompilerParams(
            collective_id=1, has_side_effects=True, vmem_limit_bytes=60 << 20
        ),
        cost_estimate=pl.CostEstimate(flops=30 << 30, bytes_accessed=200 << 20, transcendentals=0),
        name="step",
    )(
        source, row_token.reshape(1, -1), seg_ids, jnp.asarray(frequencies())[None], stitch_weight,
        norm_gain.reshape(1, -1), q_weight, kv_weight, o_weight, out_grad,
    )


def solution(mesh):
    placed = (
        P("tp", "tok"),
        P(),
        P("tok", None),
        P("tok", "tp"),
        P(),
        P(None, "tp"),
        P(None, "tp"),
        P("tp", None),
        P("tok", "tp"),
    )
    return jax.shard_map(
        body,
        mesh=mesh,
        in_specs=placed,
        out_specs=(P("tok", "tp"), P("tok", "tp")),
        check_vma=False,
    )
```

```python
import math

import jax
import jax.numpy as jnp
import numpy as np
from jax import lax
from jax.experimental import pallas as pl
from jax.experimental.pallas import tpu as pltpu
from jax.sharding import PartitionSpec as P

HD = 128


epsilon = 1e-05


def frequencies():
    exponent = np.arange(0, HD, 2, dtype=np.float32) / np.float32(HD)
    plain_rate = np.power(np.float32(500000.0), -exponent)
    wavelength = np.float32(2.0 * math.pi) / plain_rate
    smoothing = (np.float32(8192.0) / wavelength - np.float32(1.0)) / np.float32(3.0)
    blended = (np.float32(1.0) - smoothing) * plain_rate / np.float32(8.0) + smoothing * plain_rate
    rate = np.where(
        wavelength < 2048.0,
        plain_rate,
        np.where(wavelength > 8192.0, plain_rate / np.float32(8.0), blended),
    )
    return np.concatenate([rate, rate]).astype(np.float32)


class Group:
    def __init__(self, axis):
        tok, tp = lax.axis_index("tok"), lax.axis_index("tp")
        self.axis, self.tok, self.tp = axis, tok, tp
        if axis == "tp":
            self.ring, self.pair, self.core = tp // 4, (tp // 2) % 2, tp % 2
        else:
            self.ring, self.pair, self.core = tok // 2, tok % 2, 0

    def index(self, step, across, sibling=0):
        ring = lax.rem(self.ring + step, 4)
        pair = 1 - self.pair if across else self.pair
        if self.axis == "tp":
            core = 1 - self.core if sibling else self.core
            return ring * 4 + pair * 2 + core
        return ring * 2 + pair

    def device(self, step, across, sibling=0):
        index = self.index(step, across, sibling)
        return (self.tok, index) if self.axis == "tp" else (index, self.tp)

    def peers(self):
        found = [self.device(step, 0) for step in (1, 2, 3)] + [self.device(0, 1)]
        return found + ([self.device(0, 0, 1)] if self.axis == "tp" else [])


class Wire:
    def __init__(self, send, recv):
        self.send, self.recv, self.slots, self.sent, self.waited = send, recv, {}, [], 0

    def slot(self, key):
        return self.recv.at[self.slots.setdefault(key, len(self.slots))]

    def put(self, src, dst, device, key):
        copy = pltpu.make_async_remote_copy(
            src_ref=src,
            dst_ref=dst,
            send_sem=self.send.at[len(self.sent)],
            recv_sem=self.slot(key),
            device_id=device,
            device_id_type=pl.DeviceIdType.MESH,
        )
        copy.start()
        self.sent.append(copy)

    def got(self, view, device, key):
        pltpu.make_async_remote_copy(
            src_ref=view,
            dst_ref=view,
            send_sem=self.send.at[0],
            recv_sem=self.slot(key),
            device_id=device,
            device_id_type=pl.DeviceIdType.MESH,
        ).wait_recv()

    def drain(self):
        for copy in self.sent[self.waited :]:
            copy.wait_send()
        self.waited = len(self.sent)


def announce(*groups):
    barrier = pltpu.get_barrier_semaphore()
    peers = [peer for group in groups for peer in group.peers()]
    for peer in peers:
        pl.semaphore_signal(
            barrier, inc=1, device_id=peer, device_id_type=pl.DeviceIdType.MESH
        )
    return lambda: pl.semaphore_wait(barrier, len(peers))


def wide(value):
    return value.astype(jnp.float32)


def gather_steps(group, wire, shard, whole, cut, local, name, ready):
    two_cores = group.axis == "tp"

    def pass_on(step, across, half):
        if two_cores:
            view = whole(group.index(step, across), half)
            wire.put(view, view, group.device(0, 0, 1), (name, "core", step, across, half))

    def arrived(step, across, half):
        view = whole(group.index(step, across), half)
        wire.got(view, group.device(0, 1), (name, step, across, half))

    def complete(step, across):
        if two_cores:
            for half in (0, 1):
                view = whole(group.index(step, across, 1), half)
                wire.got(view, group.device(0, 0, 1), (name, "core", step, across, half))
        ready(step, across)

    own = group.index(0, 0)
    wire.put(shard(0), whole(own, 0), group.device(0, 1), (name, 0, 1, 0))

    def along(half):
        for step in (1, 3, 2):
            wire.put(
                shard(half), whole(own, half), group.device(step, 0), (name, 4 - step, 0, half)
            )

    along(1)
    along(0)
    wire.put(shard(1), whole(own, 1), group.device(0, 1), (name, 0, 1, 1))
    kept = [pltpu.make_async_copy(shard(half), whole(own, half), local.at[half]) for half in (0, 1)]
    for copy in kept:
        copy.start()
    if two_cores:
        for half in (0, 1):
            wire.put(
                shard(half), whole(own, half), group.device(0, 0, 1), (name, "core", 0, 0, half)
            )
    for copy in kept:
        copy.wait()
    yield
    complete(0, 0)
    arrived(0, 1, 0)
    view = whole(group.index(0, 1), 0)
    for step in (1, 3, 2):
        wire.put(view, view, group.device(step, 0), (name, 4 - step, 1, 0))
    pass_on(0, 1, 0)
    for step in (1, 3, 2):
        arrived(step, 0, 1)
        view = whole(group.index(step, 0), 1)
        wire.put(view, view, group.device(0, 1), (name, step, 1, 1))
        pass_on(step, 0, 1)
    yield
    for step in (1, 3, 2):
        arrived(step, 0, 0)
        pass_on(step, 0, 0)
    arrived(0, 1, 1)
    pass_on(0, 1, 1)
    yield
    for step in (1, 3, 2):
        complete(step, 0)
    complete(0, 1)
    yield
    for step in (1, 3, 2):
        for half in (0, 1):
            arrived(step, 1, half)
            pass_on(step, 1, half)
    yield
    for step in (1, 3, 2):
        complete(step, 1)


ORDER = [(step, 1) for step in (0, 1, 3, 2)] + [(step, 0) for step in (1, 3, 2, 0)]


def core_steps(group, wire, term, mine, leaving, by_core, name):
    for step, across in ORDER:
        going, kept = leaving(step, across), mine(step, across)
        going[...] = term(group.index(step, across, 1))
        wire.put(
            going, by_core.at[step, across], group.device(0, 0, 1), (name, "core", step, across)
        )
        kept[...] = term(group.index(step, across))
        yield
        wire.got(by_core.at[step, across], group.device(0, 0, 1), (name, "core", step, across))
        kept[...] = (wide(kept[...]) + wide(by_core[step, across])).astype(jnp.bfloat16)
        yield step, across


def scatter_first(group, wire, mine, by_pair, by_ring, cut, name, step, across):
    if across:
        wire.put(
            mine(step, 1, 0), by_pair.at[step], group.device(0, 1), (name, "pair", step)
        )
    if step:
        wire.put(
            mine(step, across, 1),
            by_ring.at[4 - step, across],
            group.device(step, 0),
            (name, "ring", 4 - step, across),
        )


def scatter_steps(group, wire, mine, finish, last, buffers, name):
    by_pair, by_ring, by_ring_last, by_pair_last = buffers
    going, going_last = last
    for step in (1, 3, 2, 0):
        wire.got(by_pair.at[step], group.device(0, 1), (name, "pair", step))
        total = wide(mine(step, 0, 0)[...]) + wide(by_pair[step])
        if step:
            going[step] = total.astype(jnp.bfloat16)
            wire.put(
                going.at[step], by_ring_last.at[4 - step], group.device(step, 0),
                (name, "last", 4 - step),
            )
        else:
            first_total = total
    for across in (1, 0):
        total = wide(mine(0, across, 1)[...])
        for step in (1, 3, 2):
            wire.got(by_ring.at[step, across], group.device(step, 0), (name, "ring", step, across))
            total = total + wide(by_ring[step, across])
        if across:
            going_last[...] = total.astype(jnp.bfloat16)
            wire.put(going_last, by_pair_last, group.device(0, 1), (name, "last"))
    yield
    wire.got(by_pair_last, group.device(0, 1), (name, "last"))
    finish(1, total + wide(by_pair_last[...]))
    for step in (1, 3, 2):
        wire.got(by_ring_last.at[step], group.device(step, 0), (name, "last", step))
        first_total = first_total + wide(by_ring_last[step])
    finish(0, first_total)


def scatter_buffers(rows, columns, cut):
    first, second, kind = cut, rows - cut, jnp.bfloat16
    return [
        pltpu.VMEM((4, first, columns), kind),
        pltpu.VMEM((4, 2, second, columns), kind),
        pltpu.VMEM((4, first, columns), kind),
        pltpu.VMEM((second, columns), kind),
        pltpu.VMEM((4, first, columns), kind),
        pltpu.VMEM((second, columns), kind),
    ]


def part_of(half, rows, cut):
    return pl.ds(cut, rows - cut) if half else pl.ds(0, cut)


def chunks_in_rows(ref, rows, columns, side):
    def view(step, across, half=None, cut=0):
        start, size = (0, rows) if half is None else (cut, rows - cut) if half else (0, cut)
        return ref.at[pl.ds((step * 2 + across) * rows + start, size), pl.ds(side * columns, columns)]

    return view


def chunks_in_columns(ref, rows, columns, side):
    def view(step, across, half=None, cut=0):
        part = pl.ds(0, rows) if half is None else part_of(half, rows, cut)
        return ref.at[part, pl.ds((side * 8 + step * 2 + across) * columns, columns)]

    return view


def column_views(ref, rows, columns, cut):
    def view(slot, half):
        return ref.at[
            part_of(half, rows, cut), pl.ds(pl.multiple_of(slot * columns, columns), columns)
        ]

    return view


def row_views(ref, rows, cut):
    def view(slot, half):
        start, size = (cut, rows - cut) if half else (0, cut)
        return ref.at[pl.ds(pl.multiple_of(slot * rows + start, 32), size)]

    return view


def shard_views(ref, rows, cut):
    return lambda half: ref.at[part_of(half, rows, cut)]


def run(steps):
    for _ in steps:
        pass


def advance(steps):
    return next(steps, None)


ANYWHERE = pl.BlockSpec(memory_space=pl.ANY)
ON_CHIP = pl.BlockSpec(memory_space=pltpu.VMEM)


def dot(a, b, over=((1,), (0,))):
    return lax.dot_general(a, b, (over, ((), ())), preferred_element_type=jnp.float32)


BY_ROWS = ((1,), (1,))
BY_COLUMNS = ((0,), (0,))


def step_kernel(
    source, row_token, seg_row, rates, stitch, gain, q_hbm, kv_hbm, o_hbm, out_grad,
    layer_out, stitch_grad,
    send, recv, local, loads,
    stitch_in, q_in, kv_in, o_in, rows_in, hidden_in, gradient_in,
    token_part, token_rows, hidden, queries, pairs, squares, grad_context,
    cosines, sines, every_grad, grad_hidden,
    queries_in, context, grad_queries, grad_pairs, own_pair, other_pair, leaving_pair, back_pair,
    by_core, by_core_out,
    *buffers,
):
    tp, tok, wire = Group("tp"), Group("tok"), Wire(send, recv)
    rows, columns = out_grad.shape
    source_rows = source.shape[0]
    tiles = token_part.shape[0] // rows
    pulls = [
        pltpu.make_async_copy(a, b, loads.at[i])
        for i, (a, b) in enumerate(
            ((stitch, stitch_in), (o_hbm, o_in), (q_hbm, q_in), (kv_hbm, kv_in), (out_grad, grad_hidden))
        )
    ]
    met = announce(tp, tok)
    for pull in pulls:
        pull.start()
    width, half = hidden_in.shape[1], jnp.bfloat16
    segments = jnp.broadcast_to(seg_row[...].astype(jnp.float32), (rows, rows))
    own_segment = segments.T
    index = lax.broadcasted_iota(jnp.int32, (rows, rows), 0)
    earlier = jnp.sum(jnp.where(segments < own_segment, 1.0, 0.0), axis=1, keepdims=True)
    angles = (index[:, :HD].astype(jnp.float32) - earlier) * rates[...]
    cosines[...] = jnp.cos(angles)
    sine = jnp.sin(angles)
    sines[...] = jnp.where(
        lax.broadcasted_iota(jnp.int32, (rows, HD), 1) < HD // 2, -sine, sine
    )
    met()
    pulls[0].wait()

    def placed(tile, taken, size=rows):
        index = lax.broadcasted_iota(jnp.int32, (size, taken.shape[1]), 0) + tile * size
        return jnp.where(index == taken, 1.0, 0.0).astype(jnp.bfloat16)

    def block_of(step, across):
        block = tp.index(step, across) // 2
        return pl.ds(pl.multiple_of(block * 2 * source_rows, 2 * source_rows), 2 * source_rows)

    def tile_of(tile, size=rows):
        return pl.ds(pl.multiple_of(tile * size, size), size)

    late = [(1, 1), (3, 1), (2, 1)]
    product = [queries_in, context, grad_queries]
    total_context = stitch_grad.at[pl.ds(0, rows)]

    def source_ready(step, across):
        here = block_of(step, across)
        slot = late.index((step, across)) if (step, across) in late else 0
        product[slot][...] = dot(rows_in[here, :], stitch_in[...]).astype(jnp.bfloat16)
        if (step, across) in late:
            return

        @pl.loop(0, tiles // 4)
        def _(tile):
            there = tile_of(tile, 4 * rows)
            moved = dot(placed(tile, row_token[:, here], 4 * rows), product[0][...]).astype(
                jnp.bfloat16
            )
            if (step, across) == (0, 0):
                token_part[there, :] = moved
            else:
                token_part[there, :] = token_part[there, :] + moved

    def place_late(step):
        tile = lax.rem(tok.ring + step, 4)
        there = tile_of(tile, 2 * rows)
        total = wide(token_part[there, :])
        for slot, place in enumerate(late):
            taken = row_token[:, block_of(*place)]
            total = total + dot(placed(tile, taken, 2 * rows), product[slot][...])
        token_part[there, :] = total.astype(jnp.bfloat16)

    def nothing(step, across):
        pass

    fetching = gather_steps(
        tp, wire, shard_views(source, source_rows, 64), row_views(rows_in, source_rows, 64),
        64, local.at[pl.ds(0, 2)], "source", source_ready,
    )
    gathering = gather_steps(
        tp, wire, shard_views(out_grad, rows, 128), column_views(gradient_in, rows, columns, 128),
        128, local.at[pl.ds(2, 2)], "gradient", nothing,
    )
    for _ in range(3):
        advance(fetching)
    advance(gathering)
    run(fetching)
    cut = 128
    later, going, buffers = buffers[6:], buffers[4:6], buffers[:4]

    def part(step, across, half):
        start, size = (cut, rows - cut) if half else (0, cut)
        return token_part.at[
            pl.ds(pl.multiple_of(tok.index(step, across) * rows + start, 32), size)
        ]

    def finish(half, value):
        hidden[part_of(half, rows, cut), :] = value.astype(hidden.dtype)

    for step in (1, 3, 2, 0):
        place_late(step)
        for across in (1, 0):
            scatter_first(tok, wire, part, buffers[0], buffers[1], cut, "hidden", step, across)
    scattering = scatter_steps(tok, wire, part, finish, going, buffers, "hidden")

    def reorder(first, last):
        @pl.loop(first // 2, last // 2)
        def _(tile):
            token_rows[tile_of(tile, 2 * rows), :] = dot(
                placed(tile, row_token[...], 2 * rows), rows_in[...]
            ).astype(
                token_rows.dtype
            )

    reorder(0, tiles // 2)
    advance(scattering)
    advance(gathering)
    advance(scattering)
    def hidden_ready(step, across):
        if (step, across) == (0, 0):
            pulls[2].wait()
            pulls[3].wait()
            pulls[4].wait()
        here = pl.ds(
            pl.multiple_of(tp.index(step, across) // 2 * 2 * columns, 2 * columns), 2 * columns
        )
        value = wide(hidden_in[:, here])
        scaled = (value * gain[:, here]).astype(jnp.bfloat16)
        to_queries = dot(scaled, q_in[here, :])
        to_pairs = dot(scaled, kv_in[here, :])
        squared = jnp.broadcast_to(
            jnp.sum(value * value, axis=1, keepdims=True), squares.shape
        )
        if (step, across) == (0, 0):
            queries[...], pairs[...], squares[...] = to_queries, to_pairs, squared
        else:
            queries[...] += to_queries
            pairs[...] += to_pairs
            squares[...] += squared

    collecting = gather_steps(
        tp, wire, shard_views(hidden, rows, 128), column_views(hidden_in, rows, columns, 128),
        128, local.at[pl.ds(4, 2)], "all", hidden_ready,
    )
    advance(collecting)
    reorder(tiles // 2, tiles * 3 // 4)
    advance(collecting)
    run(gathering)
    reorder(tiles * 3 // 4, tiles)
    advance(collecting)
    pulls[1].wait()
    advance(collecting)
    total_context[...] = jnp.zeros_like(total_context)

    @pl.loop(0, gradient_in.shape[1] // 1024)
    def _(block):
        here = pl.ds(pl.multiple_of(block * 1024, 1024), 1024)
        total_context[...] += dot(gradient_in[:, here], o_in[:, here], BY_ROWS)

    grad_context[...] = total_context[...].astype(grad_context.dtype)
    run(collecting)
    wire.drain()

    cosine, sine = cosines[...], sines[...]
    segments = jnp.broadcast_to(seg_row[...].astype(jnp.float32), (rows, rows))
    allowed = (segments.T == segments) & (
        lax.broadcasted_iota(jnp.int32, (rows, rows), 1)
        <= lax.broadcasted_iota(jnp.int32, (rows, rows), 0)
    )

    def rotate(x):
        return x * cosine + pltpu.roll(x, HD // 2, 1) * sine

    def unrotate(x):
        return x * cosine - pltpu.roll(x, HD // 2, 1) * sine

    inv_rms = lax.rsqrt(squares[...] / width + epsilon)
    is_key = tp.core == 0
    sibling = tp.device(0, 0, 1)
    projected = pairs[...] * inv_rms
    own_pair[...] = jnp.where(is_key, rotate(projected), projected).astype(half)
    heads = queries.shape[1] // HD
    wire.put(own_pair, other_pair, sibling, "pair")
    for head in range(heads):
        lanes = pl.ds(head * HD, HD)
        queries_in[:, lanes] = rotate(queries[:, lanes] * inv_rms).astype(half)
    wire.got(other_pair, sibling, "pair")
    keys = jnp.where(is_key, own_pair[...], other_pair[...])
    values = jnp.where(is_key, other_pair[...], own_pair[...])
    scale = 1.0 / math.sqrt(HD)
    grad_keys = jnp.zeros((HD, rows), jnp.float32)
    grad_values = jnp.zeros((HD, rows), jnp.float32)
    along = jnp.zeros((rows, 1), jnp.float32)
    for head in range(heads):
        lanes = pl.ds(head * HD, HD)
        query, gradient = queries_in[:, lanes], grad_context[:, lanes]
        scores = jnp.where(allowed, dot(query, keys, BY_ROWS) * scale, -1e30)
        exponents = jnp.exp(scores - jnp.max(scores, axis=1, keepdims=True))
        attention = exponents * (1.0 / jnp.sum(exponents, axis=1, keepdims=True))
        attention_half = attention.astype(half)
        context[:, lanes] = dot(attention_half, values).astype(half)
        grad_probs = dot(gradient, values, BY_ROWS)
        centered = grad_probs - jnp.sum(grad_probs * attention, axis=1, keepdims=True)
        score_gradient = (attention * centered * scale).astype(half)
        grad_query = unrotate(dot(score_gradient, keys)).astype(half)
        grad_queries[:, lanes] = grad_query
        along = along + jnp.sum(wide(grad_query) * queries[:, lanes], axis=1, keepdims=True)
        grad_keys = grad_keys + dot(query, score_gradient, BY_COLUMNS)
        grad_values = grad_values + dot(gradient, attention_half, BY_COLUMNS)
    grad_keys, grad_values = grad_keys.T, grad_values.T
    leaving_pair[...] = jnp.where(is_key, grad_values, grad_keys).astype(half)
    wire.put(leaving_pair, back_pair, sibling, "back")
    first, second = later[:6], later[6:]
    cut_first, cut_second = 128, 64
    mine, leaving = (chunks_in_rows(rows_in, rows, columns, side) for side in (0, 1))
    mine_out, leaving_out = (
        chunks_in_columns(gradient_in, rows, columns, side) for side in (0, 1)
    )

    def mine_first(step, across, half):
        return mine(step, across, half, cut_first)

    def mine_second(step, across, half):
        return mine_out(step, across, half, cut_second)


    def output_term(slot):
        here = pl.ds(pl.multiple_of(slot * columns, columns), columns)
        return dot(context[...], o_in[:, here]).astype(half)

    output_meeting = core_steps(
        tp, wire, output_term, mine_out, leaving_out, by_core_out, "output"
    )
    for _ in range(5):
        advance(output_meeting)
    wire.got(back_pair, sibling, "back")
    summed = jnp.where(is_key, grad_keys, grad_values) + wide(back_pair[...])
    pair_gradient = jnp.where(is_key, unrotate(summed), summed).astype(half)
    grad_pairs[...] = pair_gradient
    along = along + jnp.sum(wide(pair_gradient) * pairs[...], axis=1, keepdims=True)
    inv = inv_rms[:, :1]
    pulled = inv * inv * inv * along / width

    def gradient_term(slot):
        here = pl.ds(pl.multiple_of(slot * columns, columns), columns)
        value = dot(grad_queries[...], q_in[here, :], BY_ROWS)
        value = value + dot(grad_pairs[...], kv_in[here, :], BY_ROWS)
        return (inv * (gain[:, here] * value) - wide(hidden_in[:, here]) * pulled).astype(half)

    def gradient_total(where, value):
        here = part_of(where, rows, cut_first)
        grad_hidden[here, :] = (wide(grad_hidden[here, :]) + value).astype(half)

    def output_total(where, value):
        here = part_of(where, rows, cut_second)
        layer_out[here, :] = (wide(hidden[here, :]) + value).astype(half)

    meeting = core_steps(tp, wire, gradient_term, mine, leaving, by_core, "gradient")
    advance(meeting)
    for count, (step, across) in enumerate(ORDER):
        advance(meeting)
        scatter_first(
            tp, wire, mine_first, first[0], first[1], cut_first, "gradient", step, across
        )
        advance(meeting)
    run(output_meeting)
    scattering = scatter_steps(
        tp, wire, mine_first, gradient_total, first[4:], first[:4], "gradient"
    )
    advance(scattering)
    run(scattering)

    def pack_ready(step, across):
        here = pl.ds(pl.multiple_of(tok.index(step, across) * rows, rows), rows)
        value = dot(token_rows[here, :], every_grad[here, :], BY_COLUMNS)
        if (step, across) == (0, 0):
            stitch_grad[...] = value
        else:
            stitch_grad[...] += value

    cut_grad = 192
    gathering = gather_steps(
        tok, wire, shard_views(grad_hidden, rows, cut_grad), row_views(every_grad, rows, cut_grad),
        cut_grad, local.at[pl.ds(6, 2)], "every", pack_ready,
    )
    advance(gathering)
    for step, across in ORDER:
        scatter_first(tp, wire, mine_second, second[0], second[1], cut_second, "output", step, across)
    scattering = scatter_steps(
        tp, wire, mine_second, output_total, second[4:], second[:4], "output"
    )
    advance(gathering)
    advance(gathering)
    advance(scattering)
    run(gathering)
    run(scattering)
    wire.drain()


def body(
    source, row_token, seg_ids, stitch_weight, norm_gain, q_weight, kv_weight, o_weight, out_grad
):
    rows, columns = out_grad.shape
    source_rows, features = source.shape
    tokens, width, heads = 16 * source_rows, 16 * columns, q_weight.shape[1]
    kind = jnp.bfloat16

    def on_chip(*shape, dtype=kind):
        return pltpu.VMEM(shape, dtype)

    return pl.pallas_call(
        step_kernel,
        out_shape=(
            jax.ShapeDtypeStruct((rows, columns), kind),
            jax.ShapeDtypeStruct((features, columns), jnp.float32),
        ),
        in_specs=[ANYWHERE] + [ON_CHIP] * 3 + [ANYWHERE, ON_CHIP] + [ANYWHERE] * 4,
        out_specs=(ON_CHIP, ON_CHIP),
        scratch_shapes=[
            pltpu.SemaphoreType.DMA((200,)),
            pltpu.SemaphoreType.DMA((200,)),
            pltpu.SemaphoreType.DMA((8,)),
            pltpu.SemaphoreType.DMA((5,)),
            on_chip(*stitch_weight.shape),
            on_chip(*q_weight.shape),
            on_chip(*kv_weight.shape),
            on_chip(*o_weight.shape),
            on_chip(tokens, features),
            on_chip(rows, width),
            on_chip(rows, width),
            on_chip(tokens, columns),
            on_chip(tokens, features),
            on_chip(rows, columns),
            on_chip(rows, heads, dtype=jnp.float32),
            on_chip(rows, HD, dtype=jnp.float32),
            on_chip(rows, HD, dtype=jnp.float32),
            on_chip(rows, heads),
            on_chip(rows, HD, dtype=jnp.float32),
            on_chip(rows, HD, dtype=jnp.float32),
            on_chip(tokens, columns),
            on_chip(rows, columns),
        ]
        + [on_chip(rows, heads)] * 3
        + [on_chip(rows, HD)] * 5
        + [on_chip(4, 2, rows, columns)] * 2
        + scatter_buffers(rows, columns, 128)
        + scatter_buffers(rows, columns, 128)
        + scatter_buffers(rows, columns, 64),
        compiler_params=pltpu.CompilerParams(
            collective_id=1, has_side_effects=True, vmem_limit_bytes=60 << 20
        ),
        cost_estimate=pl.CostEstimate(flops=30 << 30, bytes_accessed=200 << 20, transcendentals=0),
        name="step",
    )(
        source, row_token.reshape(1, -1), seg_ids, jnp.asarray(frequencies())[None], stitch_weight,
        norm_gain.reshape(1, -1), q_weight, kv_weight, o_weight, out_grad,
    )


def solution(mesh):
    placed = (
        P("tp", "tok"),
        P(),
        P("tok", None),
        P("tok", "tp"),
        P(),
        P(None, "tp"),
        P(None, "tp"),
        P("tp", None),
        P("tok", "tp"),
    )
    return jax.shard_map(
        body,
        mesh=mesh,
        in_specs=placed,
        out_specs=(P("tok", "tp"), P("tok", "tp")),
        check_vma=False,
    )
```

```python
import math

import jax
import jax.numpy as jnp
import numpy as np
from jax import lax
from jax.experimental import pallas as pl
from jax.experimental.pallas import tpu as pltpu
from jax.sharding import PartitionSpec as P

HD = 128


epsilon = 1e-05


def frequencies():
    exponent = np.arange(0, HD, 2, dtype=np.float32) / np.float32(HD)
    plain_rate = np.power(np.float32(500000.0), -exponent)
    wavelength = np.float32(2.0 * math.pi) / plain_rate
    smoothing = (np.float32(8192.0) / wavelength - np.float32(1.0)) / np.float32(3.0)
    blended = (np.float32(1.0) - smoothing) * plain_rate / np.float32(8.0) + smoothing * plain_rate
    rate = np.where(
        wavelength < 2048.0,
        plain_rate,
        np.where(wavelength > 8192.0, plain_rate / np.float32(8.0), blended),
    )
    return np.concatenate([rate, rate]).astype(np.float32)


class Group:
    def __init__(self, axis):
        tok, tp = lax.axis_index("tok"), lax.axis_index("tp")
        self.axis, self.tok, self.tp = axis, tok, tp
        if axis == "tp":
            self.ring, self.pair, self.core = tp // 4, (tp // 2) % 2, tp % 2
        else:
            self.ring, self.pair, self.core = tok // 2, tok % 2, 0

    def index(self, step, across, sibling=0):
        ring = lax.rem(self.ring + step, 4)
        pair = 1 - self.pair if across else self.pair
        if self.axis == "tp":
            core = 1 - self.core if sibling else self.core
            return ring * 4 + pair * 2 + core
        return ring * 2 + pair

    def device(self, step, across, sibling=0):
        index = self.index(step, across, sibling)
        return (self.tok, index) if self.axis == "tp" else (index, self.tp)

    def peers(self):
        found = [self.device(step, 0) for step in (1, 2, 3)] + [self.device(0, 1)]
        return found + ([self.device(0, 0, 1)] if self.axis == "tp" else [])


class Wire:
    def __init__(self, send, recv):
        self.send, self.recv, self.slots, self.sent, self.waited = send, recv, {}, [], 0

    def slot(self, key):
        return self.recv.at[self.slots.setdefault(key, len(self.slots))]

    def put(self, src, dst, device, key):
        copy = pltpu.make_async_remote_copy(
            src_ref=src,
            dst_ref=dst,
            send_sem=self.send.at[len(self.sent)],
            recv_sem=self.slot(key),
            device_id=device,
            device_id_type=pl.DeviceIdType.MESH,
        )
        copy.start()
        self.sent.append(copy)

    def got(self, view, device, key):
        pltpu.make_async_remote_copy(
            src_ref=view,
            dst_ref=view,
            send_sem=self.send.at[0],
            recv_sem=self.slot(key),
            device_id=device,
            device_id_type=pl.DeviceIdType.MESH,
        ).wait_recv()

    def drain(self):
        for copy in self.sent[self.waited :]:
            copy.wait_send()
        self.waited = len(self.sent)


def announce(*groups):
    barrier = pltpu.get_barrier_semaphore()
    peers = [peer for group in groups for peer in group.peers()]
    for peer in peers:
        pl.semaphore_signal(
            barrier, inc=1, device_id=peer, device_id_type=pl.DeviceIdType.MESH
        )
    return lambda: pl.semaphore_wait(barrier, len(peers))


def wide(value):
    return value.astype(jnp.float32)


def gather_steps(group, wire, shard, whole, cut, local, name, ready):
    two_cores = group.axis == "tp"

    def pass_on(step, across, half):
        if two_cores:
            view = whole(group.index(step, across), half)
            wire.put(view, view, group.device(0, 0, 1), (name, "core", step, across, half))

    def arrived(step, across, half):
        view = whole(group.index(step, across), half)
        wire.got(view, group.device(0, 1), (name, step, across, half))

    def complete(step, across):
        if two_cores:
            for half in (0, 1):
                view = whole(group.index(step, across, 1), half)
                wire.got(view, group.device(0, 0, 1), (name, "core", step, across, half))
        ready(step, across)

    own = group.index(0, 0)
    wire.put(shard(0), whole(own, 0), group.device(0, 1), (name, 0, 1, 0))

    def along(half):
        for step in (1, 3, 2):
            wire.put(
                shard(half), whole(own, half), group.device(step, 0), (name, 4 - step, 0, half)
            )

    along(1)
    along(0)
    wire.put(shard(1), whole(own, 1), group.device(0, 1), (name, 0, 1, 1))
    kept = [pltpu.make_async_copy(shard(half), whole(own, half), local.at[half]) for half in (0, 1)]
    for copy in kept:
        copy.start()
    if two_cores:
        for half in (0, 1):
            wire.put(
                shard(half), whole(own, half), group.device(0, 0, 1), (name, "core", 0, 0, half)
            )
    for copy in kept:
        copy.wait()
    yield
    complete(0, 0)
    arrived(0, 1, 0)
    view = whole(group.index(0, 1), 0)
    for step in (1, 3, 2):
        wire.put(view, view, group.device(step, 0), (name, 4 - step, 1, 0))
    pass_on(0, 1, 0)
    for step in (1, 3, 2):
        arrived(step, 0, 1)
        view = whole(group.index(step, 0), 1)
        wire.put(view, view, group.device(0, 1), (name, step, 1, 1))
        pass_on(step, 0, 1)
    yield
    for step in (1, 3, 2):
        arrived(step, 0, 0)
        pass_on(step, 0, 0)
    arrived(0, 1, 1)
    pass_on(0, 1, 1)
    yield
    for step in (1, 3, 2):
        complete(step, 0)
    complete(0, 1)
    yield
    for step in (1, 3, 2):
        for half in (0, 1):
            arrived(step, 1, half)
            pass_on(step, 1, half)
    yield
    for step in (1, 3, 2):
        complete(step, 1)


ORDER = [(step, 1) for step in (0, 1, 3, 2)] + [(step, 0) for step in (1, 3, 2, 0)]


def core_steps(group, wire, term, mine, leaving, by_core, name):
    for step, across in ORDER:
        going, kept = leaving(step, across), mine(step, across)
        going[...] = term(group.index(step, across, 1))
        wire.put(
            going, by_core.at[step, across], group.device(0, 0, 1), (name, "core", step, across)
        )
        kept[...] = term(group.index(step, across))
        yield
        wire.got(by_core.at[step, across], group.device(0, 0, 1), (name, "core", step, across))
        kept[...] = (wide(kept[...]) + wide(by_core[step, across])).astype(jnp.bfloat16)
        yield step, across


def scatter_first(group, wire, mine, by_pair, by_ring, cut, name, step, across):
    if across:
        wire.put(
            mine(step, 1, 0), by_pair.at[step], group.device(0, 1), (name, "pair", step)
        )
    if step:
        wire.put(
            mine(step, across, 1),
            by_ring.at[3 - step, across],
            group.device(step, 0),
            (name, "ring", 4 - step, across),
        )


def scatter_steps(group, wire, mine, finish, last, buffers, name):
    by_pair, by_ring, by_ring_last, by_pair_last = buffers
    going, going_last = last
    for step in (1, 3, 2, 0):
        wire.got(by_pair.at[step], group.device(0, 1), (name, "pair", step))
        total = wide(mine(step, 0, 0)[...]) + wide(by_pair[step])
        if step:
            going[step - 1] = total.astype(jnp.bfloat16)
            wire.put(
                going.at[step - 1], by_ring_last.at[3 - step], group.device(step, 0),
                (name, "last", 4 - step),
            )
        else:
            first_total = total
    for across in (1, 0):
        total = wide(mine(0, across, 1)[...])
        for step in (1, 3, 2):
            wire.got(by_ring.at[step - 1, across], group.device(step, 0), (name, "ring", step, across))
            total = total + wide(by_ring[step - 1, across])
        if across:
            going_last[...] = total.astype(jnp.bfloat16)
            wire.put(going_last, by_pair_last, group.device(0, 1), (name, "last"))
    yield
    wire.got(by_pair_last, group.device(0, 1), (name, "last"))
    finish(1, total + wide(by_pair_last[...]))
    for step in (1, 3, 2):
        wire.got(by_ring_last.at[step - 1], group.device(step, 0), (name, "last", step))
        first_total = first_total + wide(by_ring_last[step - 1])
    finish(0, first_total)


def scatter_buffers(rows, columns, cut):
    first, second, kind = cut, rows - cut, jnp.bfloat16
    return [
        pltpu.VMEM((4, first, columns), kind),
        pltpu.VMEM((3, 2, second, columns), kind),
        pltpu.VMEM((3, first, columns), kind),
        pltpu.VMEM((second, columns), kind),
        pltpu.VMEM((3, first, columns), kind),
        pltpu.VMEM((second, columns), kind),
    ]


def part_of(half, rows, cut):
    return pl.ds(cut, rows - cut) if half else pl.ds(0, cut)


def chunks_in_rows(ref, rows, columns, side):
    def view(step, across, half=None, cut=0):
        start, size = (0, rows) if half is None else (cut, rows - cut) if half else (0, cut)
        return ref.at[pl.ds((step * 2 + across) * rows + start, size), pl.ds(side * columns, columns)]

    return view


def chunks_in_columns(ref, rows, columns, side):
    def view(step, across, half=None, cut=0):
        part = pl.ds(0, rows) if half is None else part_of(half, rows, cut)
        return ref.at[part, pl.ds((side * 8 + step * 2 + across) * columns, columns)]

    return view


def column_views(ref, rows, columns, cut):
    def view(slot, half):
        return ref.at[
            part_of(half, rows, cut), pl.ds(pl.multiple_of(slot * columns, columns), columns)
        ]

    return view


def row_views(ref, rows, cut):
    def view(slot, half):
        start, size = (cut, rows - cut) if half else (0, cut)
        return ref.at[pl.ds(pl.multiple_of(slot * rows + start, 32), size)]

    return view


def shard_views(ref, rows, cut):
    return lambda half: ref.at[part_of(half, rows, cut)]


def run(steps):
    for _ in steps:
        pass


def advance(steps):
    return next(steps, None)


ANYWHERE = pl.BlockSpec(memory_space=pl.ANY)
ON_CHIP = pl.BlockSpec(memory_space=pltpu.VMEM)


def dot(a, b, over=((1,), (0,))):
    return lax.dot_general(a, b, (over, ((), ())), preferred_element_type=jnp.float32)


BY_ROWS = ((1,), (1,))
BY_COLUMNS = ((0,), (0,))


def step_kernel(
    source, row_token, seg_row, rates, stitch, gain, q_hbm, kv_hbm, o_hbm, out_grad,
    layer_out, stitch_out,
    send, recv, local, loads,
    stitch_in, q_in, kv_in, o_in, rows_in, hidden_in, gradient_in,
    token_part, token_rows, hidden, queries, pairs, squares, grad_context,
    cosines, sines, every_grad, grad_hidden, stitch_grad,
    queries_in, context, grad_queries, grad_pairs, own_pair, other_pair, leaving_pair, back_pair,
    by_core, by_core_out,
    *buffers,
):
    tp, tok, wire = Group("tp"), Group("tok"), Wire(send, recv)
    rows, columns = out_grad.shape
    source_rows = source.shape[0]
    tiles = token_part.shape[0] // rows
    pulls = [
        pltpu.make_async_copy(a, b, loads.at[i])
        for i, (a, b) in enumerate(
            ((stitch, stitch_in), (o_hbm, o_in), (q_hbm, q_in), (kv_hbm, kv_in), (out_grad, grad_hidden))
        )
    ]
    met = announce(tp, tok)
    for pull in pulls:
        pull.start()
    width, half = hidden_in.shape[1], jnp.bfloat16
    segments = jnp.broadcast_to(seg_row[...].astype(jnp.float32), (rows, rows))
    own_segment = segments.T
    index = lax.broadcasted_iota(jnp.int32, (rows, rows), 0)
    earlier = jnp.sum(jnp.where(segments < own_segment, 1.0, 0.0), axis=1, keepdims=True)
    angles = (index[:, :HD].astype(jnp.float32) - earlier) * rates[...]
    cosines[...] = jnp.cos(angles)
    sine = jnp.sin(angles)
    sines[...] = jnp.where(
        lax.broadcasted_iota(jnp.int32, (rows, HD), 1) < HD // 2, -sine, sine
    )
    met()
    pulls[0].wait()

    def placed(tile, taken, size=rows):
        index = lax.broadcasted_iota(jnp.int32, (size, taken.shape[1]), 0) + tile * size
        return jnp.where(index == taken, 1.0, 0.0).astype(jnp.bfloat16)

    def block_of(step, across):
        block = tp.index(step, across) // 2
        return pl.ds(pl.multiple_of(block * 2 * source_rows, 2 * source_rows), 2 * source_rows)

    def tile_of(tile, size=rows):
        return pl.ds(pl.multiple_of(tile * size, size), size)

    late = [(1, 1), (3, 1), (2, 1)]
    product = [queries_in, context, grad_queries]
    total_context = stitch_grad.at[pl.ds(0, rows)]

    def source_ready(step, across):
        here = block_of(step, across)
        slot = late.index((step, across)) if (step, across) in late else 0
        product[slot][...] = dot(rows_in[here, :], stitch_in[...]).astype(jnp.bfloat16)
        if (step, across) in late:
            return

        @pl.loop(0, tiles // 4)
        def _(tile):
            there = tile_of(tile, 4 * rows)
            moved = dot(placed(tile, row_token[:, here], 4 * rows), product[0][...]).astype(
                jnp.bfloat16
            )
            if (step, across) == (0, 0):
                token_part[there, :] = moved
            else:
                token_part[there, :] = token_part[there, :] + moved

    def place_late(step):
        tile = lax.rem(tok.ring + step, 4)
        there = tile_of(tile, 2 * rows)
        total = wide(token_part[there, :])
        for slot, place in enumerate(late):
            taken = row_token[:, block_of(*place)]
            total = total + dot(placed(tile, taken, 2 * rows), product[slot][...])
        token_part[there, :] = total.astype(jnp.bfloat16)

    def nothing(step, across):
        pass

    fetching = gather_steps(
        tp, wire, shard_views(source, source_rows, 64), row_views(rows_in, source_rows, 64),
        64, local.at[pl.ds(0, 2)], "source", source_ready,
    )
    gathering = gather_steps(
        tp, wire, shard_views(out_grad, rows, 128), column_views(gradient_in, rows, columns, 128),
        128, local.at[pl.ds(2, 2)], "gradient", nothing,
    )
    for _ in range(3):
        advance(fetching)
    advance(gathering)
    run(fetching)
    cut = 128
    later, going, buffers = buffers[6:], buffers[4:6], buffers[:4]

    def part(step, across, half):
        start, size = (cut, rows - cut) if half else (0, cut)
        return token_part.at[
            pl.ds(pl.multiple_of(tok.index(step, across) * rows + start, 32), size)
        ]

    def finish(half, value):
        hidden[part_of(half, rows, cut), :] = value.astype(hidden.dtype)

    for step in (1, 3, 2, 0):
        place_late(step)
        for across in (1, 0):
            scatter_first(tok, wire, part, buffers[0], buffers[1], cut, "hidden", step, across)
    scattering = scatter_steps(tok, wire, part, finish, going, buffers, "hidden")

    def reorder(first, last):
        @pl.loop(first // 2, last // 2)
        def _(tile):
            token_rows[tile_of(tile, 2 * rows), :] = dot(
                placed(tile, row_token[...], 2 * rows), rows_in[...]
            ).astype(
                token_rows.dtype
            )

    reorder(0, tiles // 2)
    advance(scattering)
    advance(gathering)
    advance(scattering)
    def hidden_ready(step, across):
        if (step, across) == (0, 0):
            pulls[2].wait()
            pulls[3].wait()
            pulls[4].wait()
        here = pl.ds(
            pl.multiple_of(tp.index(step, across) // 2 * 2 * columns, 2 * columns), 2 * columns
        )
        value = wide(hidden_in[:, here])
        scaled = (value * gain[:, here]).astype(jnp.bfloat16)
        to_queries = dot(scaled, q_in[here, :])
        to_pairs = dot(scaled, kv_in[here, :])
        squared = jnp.broadcast_to(
            jnp.sum(value * value, axis=1, keepdims=True), squares.shape
        )
        if (step, across) == (0, 0):
            queries[...], pairs[...], squares[...] = to_queries, to_pairs, squared
        else:
            queries[...] += to_queries
            pairs[...] += to_pairs
            squares[...] += squared

    collecting = gather_steps(
        tp, wire, shard_views(hidden, rows, 128), column_views(hidden_in, rows, columns, 128),
        128, local.at[pl.ds(4, 2)], "all", hidden_ready,
    )
    advance(collecting)
    reorder(tiles // 2, tiles * 3 // 4)
    advance(collecting)
    run(gathering)
    reorder(tiles * 3 // 4, tiles)
    advance(collecting)
    pulls[1].wait()
    advance(collecting)
    total_context[...] = jnp.zeros_like(total_context)

    @pl.loop(0, gradient_in.shape[1] // 1024)
    def _(block):
        here = pl.ds(pl.multiple_of(block * 1024, 1024), 1024)
        total_context[...] += dot(gradient_in[:, here], o_in[:, here], BY_ROWS)

    grad_context[...] = total_context[...].astype(grad_context.dtype)
    run(collecting)
    wire.drain()

    cosine, sine = cosines[...], sines[...]
    segments = jnp.broadcast_to(seg_row[...].astype(jnp.float32), (rows, rows))
    allowed = (segments.T == segments) & (
        lax.broadcasted_iota(jnp.int32, (rows, rows), 1)
        <= lax.broadcasted_iota(jnp.int32, (rows, rows), 0)
    )

    def rotate(x):
        return x * cosine + pltpu.roll(x, HD // 2, 1) * sine

    def unrotate(x):
        return x * cosine - pltpu.roll(x, HD // 2, 1) * sine

    inv_rms = lax.rsqrt(squares[...] / width + epsilon)
    is_key = tp.core == 0
    sibling = tp.device(0, 0, 1)
    projected = pairs[...] * inv_rms
    own_pair[...] = jnp.where(is_key, rotate(projected), projected).astype(half)
    heads = queries.shape[1] // HD
    wire.put(own_pair, other_pair, sibling, "pair")
    for head in range(heads):
        lanes = pl.ds(head * HD, HD)
        queries_in[:, lanes] = rotate(queries[:, lanes] * inv_rms).astype(half)
    wire.got(other_pair, sibling, "pair")
    keys = jnp.where(is_key, own_pair[...], other_pair[...])
    values = jnp.where(is_key, other_pair[...], own_pair[...])
    scale = 1.0 / math.sqrt(HD)
    grad_keys = jnp.zeros((HD, rows), jnp.float32)
    grad_values = jnp.zeros((HD, rows), jnp.float32)
    along = jnp.zeros((rows, 1), jnp.float32)
    for head in range(heads):
        lanes = pl.ds(head * HD, HD)
        query, gradient = queries_in[:, lanes], grad_context[:, lanes]
        scores = jnp.where(allowed, dot(query, keys, BY_ROWS) * scale, -1e30)
        exponents = jnp.exp(scores - jnp.max(scores, axis=1, keepdims=True))
        attention = exponents * (1.0 / jnp.sum(exponents, axis=1, keepdims=True))
        attention_half = attention.astype(half)
        context[:, lanes] = dot(attention_half, values).astype(half)
        grad_probs = dot(gradient, values, BY_ROWS)
        centered = grad_probs - jnp.sum(grad_probs * attention, axis=1, keepdims=True)
        score_gradient = (attention * centered * scale).astype(half)
        grad_query = unrotate(dot(score_gradient, keys)).astype(half)
        grad_queries[:, lanes] = grad_query
        along = along + jnp.sum(wide(grad_query) * queries[:, lanes], axis=1, keepdims=True)
        grad_keys = grad_keys + dot(query, score_gradient, BY_COLUMNS)
        grad_values = grad_values + dot(gradient, attention_half, BY_COLUMNS)
    grad_keys, grad_values = grad_keys.T, grad_values.T
    leaving_pair[...] = jnp.where(is_key, grad_values, grad_keys).astype(half)
    wire.put(leaving_pair, back_pair, sibling, "back")
    first, second = later[:6], later[6:]
    cut_first, cut_second = 128, 64
    mine, leaving = (chunks_in_rows(rows_in, rows, columns, side) for side in (0, 1))
    mine_out, leaving_out = (
        chunks_in_columns(gradient_in, rows, columns, side) for side in (0, 1)
    )

    def mine_first(step, across, half):
        return mine(step, across, half, cut_first)

    def mine_second(step, across, half):
        return mine_out(step, across, half, cut_second)


    def output_term(slot):
        here = pl.ds(pl.multiple_of(slot * columns, columns), columns)
        return dot(context[...], o_in[:, here]).astype(half)

    output_meeting = core_steps(
        tp, wire, output_term, mine_out, leaving_out, by_core_out, "output"
    )
    for _ in range(5):
        advance(output_meeting)
    wire.got(back_pair, sibling, "back")
    summed = jnp.where(is_key, grad_keys, grad_values) + wide(back_pair[...])
    pair_gradient = jnp.where(is_key, unrotate(summed), summed).astype(half)
    grad_pairs[...] = pair_gradient
    along = along + jnp.sum(wide(pair_gradient) * pairs[...], axis=1, keepdims=True)
    inv = inv_rms[:, :1]
    pulled = inv * inv * inv * along / width

    def gradient_term(slot):
        here = pl.ds(pl.multiple_of(slot * columns, columns), columns)
        value = dot(grad_queries[...], q_in[here, :], BY_ROWS)
        value = value + dot(grad_pairs[...], kv_in[here, :], BY_ROWS)
        return (inv * (gain[:, here] * value) - wide(hidden_in[:, here]) * pulled).astype(half)

    def gradient_total(where, value):
        here = part_of(where, rows, cut_first)
        grad_hidden[here, :] = (wide(grad_hidden[here, :]) + value).astype(half)

    def output_total(where, value):
        here = part_of(where, rows, cut_second)
        layer_out[here, :] = (wide(hidden[here, :]) + value).astype(half)

    meeting = core_steps(tp, wire, gradient_term, mine, leaving, by_core, "gradient")
    advance(meeting)
    for count, (step, across) in enumerate(ORDER):
        advance(meeting)
        scatter_first(
            tp, wire, mine_first, first[0], first[1], cut_first, "gradient", step, across
        )
        advance(meeting)
    run(output_meeting)
    scattering = scatter_steps(
        tp, wire, mine_first, gradient_total, first[4:], first[:4], "gradient"
    )
    advance(scattering)
    run(scattering)

    def pack_ready(step, across):
        here = pl.ds(pl.multiple_of(tok.index(step, across) * rows, rows), rows)
        value = dot(token_rows[here, :], every_grad[here, :], BY_COLUMNS)
        if (step, across) == (0, 0):
            stitch_grad[...] = value
        elif (step, across) == (2, 1):
            stitch_out[...] = (stitch_grad[...] + value).astype(half)
        else:
            stitch_grad[...] += value

    cut_grad = 192
    gathering = gather_steps(
        tok, wire, shard_views(grad_hidden, rows, cut_grad), row_views(every_grad, rows, cut_grad),
        cut_grad, local.at[pl.ds(6, 2)], "every", pack_ready,
    )
    advance(gathering)
    for step, across in ORDER:
        scatter_first(tp, wire, mine_second, second[0], second[1], cut_second, "output", step, across)
    scattering = scatter_steps(
        tp, wire, mine_second, output_total, second[4:], second[:4], "output"
    )
    advance(gathering)
    advance(gathering)
    advance(scattering)
    run(gathering)
    run(scattering)
    wire.drain()


def body(
    source, row_token, seg_ids, stitch_weight, norm_gain, q_weight, kv_weight, o_weight, out_grad
):
    rows, columns = out_grad.shape
    source_rows, features = source.shape
    tokens, width, heads = 16 * source_rows, 16 * columns, q_weight.shape[1]
    kind = jnp.bfloat16

    def on_chip(*shape, dtype=kind):
        return pltpu.VMEM(shape, dtype)

    layer_out, stitch_grad = pl.pallas_call(
        step_kernel,
        out_shape=(
            jax.ShapeDtypeStruct((rows, columns), kind),
            jax.ShapeDtypeStruct((features, columns), kind),
        ),
        in_specs=[ANYWHERE] + [ON_CHIP] * 3 + [ANYWHERE, ON_CHIP] + [ANYWHERE] * 4,
        out_specs=(ON_CHIP, ON_CHIP),
        scratch_shapes=[
            pltpu.SemaphoreType.DMA((200,)),
            pltpu.SemaphoreType.DMA((200,)),
            pltpu.SemaphoreType.DMA((8,)),
            pltpu.SemaphoreType.DMA((5,)),
            on_chip(*stitch_weight.shape),
            on_chip(*q_weight.shape),
            on_chip(*kv_weight.shape),
            on_chip(*o_weight.shape),
            on_chip(tokens, features),
            on_chip(rows, width),
            on_chip(rows, width),
            on_chip(tokens, columns),
            on_chip(tokens, features),
            on_chip(rows, columns),
            on_chip(rows, heads, dtype=jnp.float32),
            on_chip(rows, HD, dtype=jnp.float32),
            on_chip(rows, HD, dtype=jnp.float32),
            on_chip(rows, heads),
            on_chip(rows, HD, dtype=jnp.float32),
            on_chip(rows, HD, dtype=jnp.float32),
            on_chip(tokens, columns),
            on_chip(rows, columns),
            on_chip(features, columns, dtype=jnp.float32),
        ]
        + [on_chip(rows, heads)] * 3
        + [on_chip(rows, HD)] * 5
        + [on_chip(4, 2, rows, columns)] * 2
        + scatter_buffers(rows, columns, 128)
        + scatter_buffers(rows, columns, 128)
        + scatter_buffers(rows, columns, 64),
        compiler_params=pltpu.CompilerParams(
            collective_id=1, has_side_effects=True, vmem_limit_bytes=60 << 20
        ),
        cost_estimate=pl.CostEstimate(flops=30 << 30, bytes_accessed=200 << 20, transcendentals=0),
        name="step",
    )(
        source, row_token.reshape(1, -1), seg_ids, jnp.asarray(frequencies())[None], stitch_weight,
        norm_gain.reshape(1, -1), q_weight, kv_weight, o_weight, out_grad,
    )
    return layer_out, stitch_grad.astype(jnp.float32)


def solution(mesh):
    placed = (
        P("tp", "tok"),
        P(),
        P("tok", None),
        P("tok", "tp"),
        P(),
        P(None, "tp"),
        P(None, "tp"),
        P("tp", None),
        P("tok", "tp"),
    )
    return jax.shard_map(
        body,
        mesh=mesh,
        in_specs=placed,
        out_specs=(P("tok", "tp"), P("tok", "tp")),
        check_vma=False,
    )
```

```python
import math

import jax
import jax.numpy as jnp
import numpy as np
from jax import lax
from jax.experimental import pallas as pl
from jax.experimental.pallas import tpu as pltpu
from jax.sharding import PartitionSpec as P

HD = 128


epsilon = 1e-05


def frequencies():
    exponent = np.arange(0, HD, 2, dtype=np.float32) / np.float32(HD)
    plain_rate = np.power(np.float32(500000.0), -exponent)
    wavelength = np.float32(2.0 * math.pi) / plain_rate
    smoothing = (np.float32(8192.0) / wavelength - np.float32(1.0)) / np.float32(3.0)
    blended = (np.float32(1.0) - smoothing) * plain_rate / np.float32(8.0) + smoothing * plain_rate
    rate = np.where(
        wavelength < 2048.0,
        plain_rate,
        np.where(wavelength > 8192.0, plain_rate / np.float32(8.0), blended),
    )
    return np.concatenate([rate, rate]).astype(np.float32)


class Group:
    def __init__(self, axis):
        tok, tp = lax.axis_index("tok"), lax.axis_index("tp")
        self.axis, self.tok, self.tp = axis, tok, tp
        if axis == "tp":
            self.ring, self.pair, self.core = tp // 4, (tp // 2) % 2, tp % 2
        else:
            self.ring, self.pair, self.core = tok // 2, tok % 2, 0

    def index(self, step, across, sibling=0):
        ring = lax.rem(self.ring + step, 4)
        pair = 1 - self.pair if across else self.pair
        if self.axis == "tp":
            core = 1 - self.core if sibling else self.core
            return ring * 4 + pair * 2 + core
        return ring * 2 + pair

    def device(self, step, across, sibling=0):
        index = self.index(step, across, sibling)
        return (self.tok, index) if self.axis == "tp" else (index, self.tp)

    def peers(self):
        found = [self.device(step, 0) for step in (1, 2, 3)] + [self.device(0, 1)]
        return found + ([self.device(0, 0, 1)] if self.axis == "tp" else [])


class Wire:
    def __init__(self, send, recv):
        self.send, self.recv, self.slots, self.sent, self.waited = send, recv, {}, [], 0

    def slot(self, key):
        return self.recv.at[self.slots.setdefault(key, len(self.slots))]

    def put(self, src, dst, device, key):
        copy = pltpu.make_async_remote_copy(
            src_ref=src,
            dst_ref=dst,
            send_sem=self.send.at[len(self.sent)],
            recv_sem=self.slot(key),
            device_id=device,
            device_id_type=pl.DeviceIdType.MESH,
        )
        copy.start()
        self.sent.append(copy)

    def got(self, view, device, key):
        pltpu.make_async_remote_copy(
            src_ref=view,
            dst_ref=view,
            send_sem=self.send.at[0],
            recv_sem=self.slot(key),
            device_id=device,
            device_id_type=pl.DeviceIdType.MESH,
        ).wait_recv()

    def drain(self):
        for copy in self.sent[self.waited :]:
            copy.wait_send()
        self.waited = len(self.sent)


def announce(*groups):
    barrier = pltpu.get_barrier_semaphore()
    peers = [peer for group in groups for peer in group.peers()]
    for peer in peers:
        pl.semaphore_signal(
            barrier, inc=1, device_id=peer, device_id_type=pl.DeviceIdType.MESH
        )
    return lambda: pl.semaphore_wait(barrier, len(peers))


def wide(value):
    return value.astype(jnp.float32)


def gather_steps(group, wire, shard, whole, cut, local, name, ready):
    two_cores = group.axis == "tp"

    def pass_on(step, across, half):
        if two_cores:
            view = whole(group.index(step, across), half)
            wire.put(view, view, group.device(0, 0, 1), (name, "core", step, across, half))

    def arrived(step, across, half):
        view = whole(group.index(step, across), half)
        wire.got(view, group.device(0, 1), (name, step, across, half))

    def complete(step, across):
        if two_cores:
            for half in (0, 1):
                view = whole(group.index(step, across, 1), half)
                wire.got(view, group.device(0, 0, 1), (name, "core", step, across, half))
        ready(step, across)

    own = group.index(0, 0)
    wire.put(shard(0), whole(own, 0), group.device(0, 1), (name, 0, 1, 0))

    def along(half):
        for step in (1, 3, 2):
            wire.put(
                shard(half), whole(own, half), group.device(step, 0), (name, 4 - step, 0, half)
            )

    along(1)
    along(0)
    wire.put(shard(1), whole(own, 1), group.device(0, 1), (name, 0, 1, 1))
    kept = [pltpu.make_async_copy(shard(half), whole(own, half), local.at[half]) for half in (0, 1)]
    for copy in kept:
        copy.start()
    if two_cores:
        for half in (0, 1):
            wire.put(
                shard(half), whole(own, half), group.device(0, 0, 1), (name, "core", 0, 0, half)
            )
    for copy in kept:
        copy.wait()
    yield
    complete(0, 0)
    arrived(0, 1, 0)
    view = whole(group.index(0, 1), 0)
    for step in (1, 3, 2):
        wire.put(view, view, group.device(step, 0), (name, 4 - step, 1, 0))
    pass_on(0, 1, 0)
    for step in (1, 3, 2):
        arrived(step, 0, 1)
        view = whole(group.index(step, 0), 1)
        wire.put(view, view, group.device(0, 1), (name, step, 1, 1))
        pass_on(step, 0, 1)
    yield
    for step in (1, 3, 2):
        arrived(step, 0, 0)
        pass_on(step, 0, 0)
    arrived(0, 1, 1)
    pass_on(0, 1, 1)
    yield
    for step in (1, 3, 2):
        complete(step, 0)
    complete(0, 1)
    yield
    for step in (1, 3, 2):
        for half in (0, 1):
            arrived(step, 1, half)
            pass_on(step, 1, half)
    yield
    for step in (1, 3, 2):
        complete(step, 1)


ORDER = [(step, 1) for step in (0, 1, 3, 2)] + [(step, 0) for step in (1, 3, 2, 0)]


def core_steps(group, wire, term, mine, leaving, by_core, name):
    for step, across in ORDER:
        going, kept = leaving(step, across), mine(step, across)
        going[...] = term(group.index(step, across, 1))
        wire.put(
            going, by_core.at[step, across], group.device(0, 0, 1), (name, "core", step, across)
        )
        kept[...] = term(group.index(step, across))
        yield
        wire.got(by_core.at[step, across], group.device(0, 0, 1), (name, "core", step, across))
        kept[...] = (wide(kept[...]) + wide(by_core[step, across])).astype(jnp.bfloat16)
        yield step, across


def scatter_first(group, wire, mine, by_pair, by_ring, cut, name, step, across):
    if across:
        wire.put(
            mine(step, 1, 0), by_pair.at[step], group.device(0, 1), (name, "pair", step)
        )
    if step:
        wire.put(
            mine(step, across, 1),
            by_ring.at[3 - step, across],
            group.device(step, 0),
            (name, "ring", 4 - step, across),
        )


def scatter_steps(group, wire, mine, finish, last, buffers, name):
    by_pair, by_ring, by_ring_last, by_pair_last = buffers
    going, going_last = last
    for step in (1, 3, 2, 0):
        wire.got(by_pair.at[step], group.device(0, 1), (name, "pair", step))
        total = wide(mine(step, 0, 0)[...]) + wide(by_pair[step])
        if step:
            going[step - 1] = total.astype(jnp.bfloat16)
            wire.put(
                going.at[step - 1], by_ring_last.at[3 - step], group.device(step, 0),
                (name, "last", 4 - step),
            )
        else:
            first_total = total
    for across in (1, 0):
        total = wide(mine(0, across, 1)[...])
        for step in (1, 3, 2):
            wire.got(by_ring.at[step - 1, across], group.device(step, 0), (name, "ring", step, across))
            total = total + wide(by_ring[step - 1, across])
        if across:
            going_last[...] = total.astype(jnp.bfloat16)
            wire.put(going_last, by_pair_last, group.device(0, 1), (name, "last"))
    yield
    wire.got(by_pair_last, group.device(0, 1), (name, "last"))
    finish(1, total + wide(by_pair_last[...]))
    for step in (1, 3, 2):
        wire.got(by_ring_last.at[step - 1], group.device(step, 0), (name, "last", step))
        first_total = first_total + wide(by_ring_last[step - 1])
    finish(0, first_total)


def scatter_buffers(rows, columns, cut):
    first, second, kind = cut, rows - cut, jnp.bfloat16
    return [
        pltpu.VMEM((4, first, columns), kind),
        pltpu.VMEM((3, 2, second, columns), kind),
        pltpu.VMEM((3, first, columns), kind),
        pltpu.VMEM((second, columns), kind),
        pltpu.VMEM((3, first, columns), kind),
        pltpu.VMEM((second, columns), kind),
    ]


def part_of(half, rows, cut):
    return pl.ds(cut, rows - cut) if half else pl.ds(0, cut)


def chunks_in_rows(ref, rows, columns, side):
    def view(step, across, half=None, cut=0):
        start, size = (0, rows) if half is None else (cut, rows - cut) if half else (0, cut)
        return ref.at[pl.ds((step * 2 + across) * rows + start, size), pl.ds(side * columns, columns)]

    return view


def chunks_in_columns(ref, rows, columns, side):
    def view(step, across, half=None, cut=0):
        part = pl.ds(0, rows) if half is None else part_of(half, rows, cut)
        return ref.at[part, pl.ds((side * 8 + step * 2 + across) * columns, columns)]

    return view


def column_views(ref, rows, columns, cut):
    def view(slot, half):
        return ref.at[
            part_of(half, rows, cut), pl.ds(pl.multiple_of(slot * columns, columns), columns)
        ]

    return view


def row_views(ref, rows, cut):
    def view(slot, half):
        start, size = (cut, rows - cut) if half else (0, cut)
        return ref.at[pl.ds(pl.multiple_of(slot * rows + start, 32), size)]

    return view


def shard_views(ref, rows, cut):
    return lambda half: ref.at[part_of(half, rows, cut)]


def run(steps):
    for _ in steps:
        pass


def advance(steps):
    return next(steps, None)


ANYWHERE = pl.BlockSpec(memory_space=pl.ANY)
ON_CHIP = pl.BlockSpec(memory_space=pltpu.VMEM)


def dot(a, b, over=((1,), (0,))):
    return lax.dot_general(a, b, (over, ((), ())), preferred_element_type=jnp.float32)


BY_ROWS = ((1,), (1,))
BY_COLUMNS = ((0,), (0,))


def step_kernel(
    source, row_token, seg_row, rates, stitch, gain, q_hbm, kv_hbm, o_hbm, out_grad,
    layer_out, stitch_out,
    send, recv, local, loads,
    stitch_in, q_in, kv_in, o_in, rows_in, hidden_in, gradient_in,
    token_part, token_rows, hidden, queries, pairs, squares, grad_context,
    cosines, sines, every_grad, grad_hidden, stitch_grad,
    queries_in, context, grad_queries, grad_pairs, own_pair, other_pair, leaving_pair, back_pair,
    by_core, by_core_out,
    *buffers,
):
    tp, tok, wire = Group("tp"), Group("tok"), Wire(send, recv)
    rows, columns = out_grad.shape
    source_rows = source.shape[0]
    tiles = token_part.shape[0] // rows
    pulls = [
        pltpu.make_async_copy(a, b, loads.at[i])
        for i, (a, b) in enumerate(
            ((stitch, stitch_in), (o_hbm, o_in), (q_hbm, q_in), (kv_hbm, kv_in), (out_grad, grad_hidden))
        )
    ]
    met = announce(tp, tok)
    for pull in pulls:
        pull.start()
    width, half = hidden_in.shape[1], jnp.bfloat16
    segments = jnp.broadcast_to(seg_row[...].astype(jnp.float32), (rows, rows))
    own_segment = segments.T
    index = lax.broadcasted_iota(jnp.int32, (rows, rows), 0)
    earlier = jnp.sum(jnp.where(segments < own_segment, 1.0, 0.0), axis=1, keepdims=True)
    angles = (index[:, :HD].astype(jnp.float32) - earlier) * rates[...]
    cosines[...] = jnp.cos(angles)
    sine = jnp.sin(angles)
    sines[...] = jnp.where(
        lax.broadcasted_iota(jnp.int32, (rows, HD), 1) < HD // 2, -sine, sine
    )
    met()
    pulls[0].wait()

    def placed(tile, taken, size=rows):
        index = lax.broadcasted_iota(jnp.int32, (size, taken.shape[1]), 0) + tile * size
        return jnp.where(index == taken, 1.0, 0.0).astype(jnp.bfloat16)

    def block_of(step, across):
        block = tp.index(step, across) // 2
        return pl.ds(pl.multiple_of(block * 2 * source_rows, 2 * source_rows), 2 * source_rows)

    def tile_of(tile, size=rows):
        return pl.ds(pl.multiple_of(tile * size, size), size)

    late = [(1, 1), (3, 1), (2, 1)]
    product = [queries_in, context, grad_queries]
    total_context = stitch_grad.at[pl.ds(0, rows)]

    def source_ready(step, across):
        here = block_of(step, across)
        slot = late.index((step, across)) if (step, across) in late else 0
        product[slot][...] = dot(rows_in[here, :], stitch_in[...]).astype(jnp.bfloat16)
        if (step, across) in late:
            return

        @pl.loop(0, tiles // 4)
        def _(tile):
            there = tile_of(tile, 4 * rows)
            moved = dot(placed(tile, row_token[:, here], 4 * rows), product[0][...]).astype(
                jnp.bfloat16
            )
            if (step, across) == (0, 0):
                token_part[there, :] = moved
            else:
                token_part[there, :] = token_part[there, :] + moved

    def place_late(step):
        tile = lax.rem(tok.ring + step, 4)
        there = tile_of(tile, 2 * rows)
        total = wide(token_part[there, :])
        for slot, place in enumerate(late):
            taken = row_token[:, block_of(*place)]
            total = total + dot(placed(tile, taken, 2 * rows), product[slot][...])
        token_part[there, :] = total.astype(jnp.bfloat16)

    def nothing(step, across):
        pass

    fetching = gather_steps(
        tp, wire, shard_views(source, source_rows, 64), row_views(rows_in, source_rows, 64),
        64, local.at[pl.ds(0, 2)], "source", source_ready,
    )
    gathering = gather_steps(
        tp, wire, shard_views(out_grad, rows, 128), column_views(gradient_in, rows, columns, 128),
        128, local.at[pl.ds(2, 2)], "gradient", nothing,
    )
    for _ in range(3):
        advance(fetching)
    advance(gathering)
    run(fetching)
    cut = 128
    later, going, buffers = buffers[6:], buffers[4:6], buffers[:4]

    def part(step, across, half):
        start, size = (cut, rows - cut) if half else (0, cut)
        return token_part.at[
            pl.ds(pl.multiple_of(tok.index(step, across) * rows + start, 32), size)
        ]

    def finish(half, value):
        hidden[part_of(half, rows, cut), :] = value.astype(hidden.dtype)

    for step in (1, 3, 2, 0):
        place_late(step)
        for across in (1, 0):
            scatter_first(tok, wire, part, buffers[0], buffers[1], cut, "hidden", step, across)
    scattering = scatter_steps(tok, wire, part, finish, going, buffers, "hidden")

    def reorder(first, last):
        @pl.loop(first // 2, last // 2)
        def _(tile):
            token_rows[tile_of(tile, 2 * rows), :] = dot(
                placed(tile, row_token[...], 2 * rows), rows_in[...]
            ).astype(
                token_rows.dtype
            )

    reorder(0, tiles // 2)
    advance(scattering)
    advance(gathering)
    advance(scattering)
    def hidden_ready(step, across):
        if (step, across) == (0, 0):
            pulls[2].wait()
            pulls[3].wait()
            pulls[4].wait()
        here = pl.ds(
            pl.multiple_of(tp.index(step, across) // 2 * 2 * columns, 2 * columns), 2 * columns
        )
        value = wide(hidden_in[:, here])
        scaled = (value * gain[:, here]).astype(jnp.bfloat16)
        to_queries = dot(scaled, q_in[here, :])
        to_pairs = dot(scaled, kv_in[here, :])
        squared = jnp.broadcast_to(
            jnp.sum(value * value, axis=1, keepdims=True), squares.shape
        )
        if (step, across) == (0, 0):
            queries[...], pairs[...], squares[...] = to_queries, to_pairs, squared
        else:
            queries[...] += to_queries
            pairs[...] += to_pairs
            squares[...] += squared

    collecting = gather_steps(
        tp, wire, shard_views(hidden, rows, 128), column_views(hidden_in, rows, columns, 128),
        128, local.at[pl.ds(4, 2)], "all", hidden_ready,
    )
    advance(collecting)
    reorder(tiles // 2, tiles * 3 // 4)
    advance(collecting)
    run(gathering)
    reorder(tiles * 3 // 4, tiles)
    advance(collecting)
    pulls[1].wait()
    advance(collecting)
    total_context[...] = jnp.zeros_like(total_context)

    @pl.loop(0, gradient_in.shape[1] // 1024)
    def _(block):
        here = pl.ds(pl.multiple_of(block * 1024, 1024), 1024)
        total_context[...] += dot(gradient_in[:, here], o_in[:, here], BY_ROWS)

    grad_context[...] = total_context[...].astype(grad_context.dtype)
    run(collecting)
    wire.drain()

    cosine, sine = cosines[...], sines[...]
    segments = jnp.broadcast_to(seg_row[...].astype(jnp.float32), (rows, rows))
    allowed = (segments.T == segments) & (
        lax.broadcasted_iota(jnp.int32, (rows, rows), 1)
        <= lax.broadcasted_iota(jnp.int32, (rows, rows), 0)
    )

    def rotate(x):
        return x * cosine + pltpu.roll(x, HD // 2, 1) * sine

    def unrotate(x):
        return x * cosine - pltpu.roll(x, HD // 2, 1) * sine

    inv_rms = lax.rsqrt(squares[...] / width + epsilon)
    is_key = tp.core == 0
    sibling = tp.device(0, 0, 1)
    projected = pairs[...] * inv_rms
    own_pair[...] = jnp.where(is_key, rotate(projected), projected).astype(half)
    heads = queries.shape[1] // HD
    wire.put(own_pair, other_pair, sibling, "pair")
    for head in range(heads):
        lanes = pl.ds(head * HD, HD)
        queries_in[:, lanes] = rotate(queries[:, lanes] * inv_rms).astype(half)
    wire.got(other_pair, sibling, "pair")
    keys = jnp.where(is_key, own_pair[...], other_pair[...])
    values = jnp.where(is_key, other_pair[...], own_pair[...])
    scale = 1.0 / math.sqrt(HD)
    grad_keys = jnp.zeros((HD, rows), jnp.float32)
    grad_values = jnp.zeros((HD, rows), jnp.float32)
    along = jnp.zeros((rows, 1), jnp.float32)
    for head in range(heads):
        lanes = pl.ds(head * HD, HD)
        query, gradient = queries_in[:, lanes], grad_context[:, lanes]
        scores = jnp.where(allowed, dot(query, keys, BY_ROWS) * scale, -1e30)
        exponents = jnp.exp(scores - jnp.max(scores, axis=1, keepdims=True))
        attention = exponents * (1.0 / jnp.sum(exponents, axis=1, keepdims=True))
        attention_half = attention.astype(half)
        context[:, lanes] = dot(attention_half, values).astype(half)
        grad_probs = dot(gradient, values, BY_ROWS)
        centered = grad_probs - jnp.sum(grad_probs * attention, axis=1, keepdims=True)
        score_gradient = (attention * centered * scale).astype(half)
        grad_query = unrotate(dot(score_gradient, keys)).astype(half)
        grad_queries[:, lanes] = grad_query
        along = along + jnp.sum(wide(grad_query) * queries[:, lanes], axis=1, keepdims=True)
        grad_keys = grad_keys + dot(query, score_gradient, BY_COLUMNS)
        grad_values = grad_values + dot(gradient, attention_half, BY_COLUMNS)
    grad_keys, grad_values = grad_keys.T, grad_values.T
    leaving_pair[...] = jnp.where(is_key, grad_values, grad_keys).astype(half)
    wire.put(leaving_pair, back_pair, sibling, "back")
    first, second = later[:6], later[6:]
    cut_first, cut_second = 128, 64
    mine, leaving = (chunks_in_rows(rows_in, rows, columns, side) for side in (0, 1))
    mine_out, leaving_out = (
        chunks_in_columns(gradient_in, rows, columns, side) for side in (0, 1)
    )

    def mine_first(step, across, half):
        return mine(step, across, half, cut_first)

    def mine_second(step, across, half):
        return mine_out(step, across, half, cut_second)


    def output_term(slot):
        here = pl.ds(pl.multiple_of(slot * columns, columns), columns)
        return dot(context[...], o_in[:, here]).astype(half)

    output_meeting = core_steps(
        tp, wire, output_term, mine_out, leaving_out, by_core_out, "output"
    )
    for _ in range(5):
        advance(output_meeting)
    wire.got(back_pair, sibling, "back")
    summed = jnp.where(is_key, grad_keys, grad_values) + wide(back_pair[...])
    pair_gradient = jnp.where(is_key, unrotate(summed), summed).astype(half)
    grad_pairs[...] = pair_gradient
    along = along + jnp.sum(wide(pair_gradient) * pairs[...], axis=1, keepdims=True)
    inv = inv_rms[:, :1]
    pulled = inv * inv * inv * along / width

    def gradient_term(slot):
        here = pl.ds(pl.multiple_of(slot * columns, columns), columns)
        value = dot(grad_queries[...], q_in[here, :], BY_ROWS)
        value = value + dot(grad_pairs[...], kv_in[here, :], BY_ROWS)
        return (inv * (gain[:, here] * value) - wide(hidden_in[:, here]) * pulled).astype(half)

    def gradient_total(where, value):
        here = part_of(where, rows, cut_first)
        grad_hidden[here, :] = (wide(grad_hidden[here, :]) + value).astype(half)

    def output_total(where, value):
        here = part_of(where, rows, cut_second)
        layer_out[here, :] = (wide(hidden[here, :]) + value).astype(half)

    meeting = core_steps(tp, wire, gradient_term, mine, leaving, by_core, "gradient")
    advance(meeting)
    for count, (step, across) in enumerate(ORDER):
        advance(meeting)
        scatter_first(
            tp, wire, mine_first, first[0], first[1], cut_first, "gradient", step, across
        )
        advance(meeting)
    run(output_meeting)
    scattering = scatter_steps(
        tp, wire, mine_first, gradient_total, first[4:], first[:4], "gradient"
    )
    advance(scattering)
    for step, across in ORDER:
        scatter_first(tp, wire, mine_second, second[0], second[1], cut_second, "output", step, across)
    run(scattering)

    def pack_ready(step, across):
        here = pl.ds(pl.multiple_of(tok.index(step, across) * rows, rows), rows)
        value = dot(token_rows[here, :], every_grad[here, :], BY_COLUMNS)
        if (step, across) == (0, 0):
            stitch_grad[...] = value
        elif (step, across) == (2, 1):
            stitch_out[...] = (stitch_grad[...] + value).astype(half)
        else:
            stitch_grad[...] += value

    cut_grad = 192
    gathering = gather_steps(
        tok, wire, shard_views(grad_hidden, rows, cut_grad), row_views(every_grad, rows, cut_grad),
        cut_grad, local.at[pl.ds(6, 2)], "every", pack_ready,
    )
    advance(gathering)
    scattering = scatter_steps(
        tp, wire, mine_second, output_total, second[4:], second[:4], "output"
    )
    advance(gathering)
    advance(gathering)
    advance(scattering)
    run(gathering)
    run(scattering)
    wire.drain()


def body(
    source, row_token, seg_ids, stitch_weight, norm_gain, q_weight, kv_weight, o_weight, out_grad
):
    rows, columns = out_grad.shape
    source_rows, features = source.shape
    tokens, width, heads = 16 * source_rows, 16 * columns, q_weight.shape[1]
    kind = jnp.bfloat16

    def on_chip(*shape, dtype=kind):
        return pltpu.VMEM(shape, dtype)

    layer_out, stitch_grad = pl.pallas_call(
        step_kernel,
        out_shape=(
            jax.ShapeDtypeStruct((rows, columns), kind),
            jax.ShapeDtypeStruct((features, columns), kind),
        ),
        in_specs=[ANYWHERE] + [ON_CHIP] * 3 + [ANYWHERE, ON_CHIP] + [ANYWHERE] * 4,
        out_specs=(ON_CHIP, ON_CHIP),
        scratch_shapes=[
            pltpu.SemaphoreType.DMA((200,)),
            pltpu.SemaphoreType.DMA((200,)),
            pltpu.SemaphoreType.DMA((8,)),
            pltpu.SemaphoreType.DMA((5,)),
            on_chip(*stitch_weight.shape),
            on_chip(*q_weight.shape),
            on_chip(*kv_weight.shape),
            on_chip(*o_weight.shape),
            on_chip(tokens, features),
            on_chip(rows, width),
            on_chip(rows, width),
            on_chip(tokens, columns),
            on_chip(tokens, features),
            on_chip(rows, columns),
            on_chip(rows, heads, dtype=jnp.float32),
            on_chip(rows, HD, dtype=jnp.float32),
            on_chip(rows, HD, dtype=jnp.float32),
            on_chip(rows, heads),
            on_chip(rows, HD, dtype=jnp.float32),
            on_chip(rows, HD, dtype=jnp.float32),
            on_chip(tokens, columns),
            on_chip(rows, columns),
            on_chip(features, columns, dtype=jnp.float32),
        ]
        + [on_chip(rows, heads)] * 3
        + [on_chip(rows, HD)] * 5
        + [on_chip(4, 2, rows, columns)] * 2
        + scatter_buffers(rows, columns, 128)
        + scatter_buffers(rows, columns, 128)
        + scatter_buffers(rows, columns, 64),
        compiler_params=pltpu.CompilerParams(
            collective_id=1, has_side_effects=True, vmem_limit_bytes=60 << 20
        ),
        cost_estimate=pl.CostEstimate(flops=30 << 30, bytes_accessed=200 << 20, transcendentals=0),
        name="step",
    )(
        source, row_token.reshape(1, -1), seg_ids, jnp.asarray(frequencies())[None], stitch_weight,
        norm_gain.reshape(1, -1), q_weight, kv_weight, o_weight, out_grad,
    )
    return layer_out, stitch_grad.astype(jnp.float32)


def solution(mesh):
    placed = (
        P("tp", "tok"),
        P(),
        P("tok", None),
        P("tok", "tp"),
        P(),
        P(None, "tp"),
        P(None, "tp"),
        P("tp", None),
        P("tok", "tp"),
    )
    return jax.shard_map(
        body,
        mesh=mesh,
        in_specs=placed,
        out_specs=(P("tok", "tp"), P("tok", "tp")),
        check_vma=False,
    )
```
